256 devices in a mesh: seq: 32 (over y, x, core), section: 8 (over z).
Axes of the slice: x: 4, y: 4, z: 8, core: 2. Of those that a mesh axis runs over, the one named last changes fastest.
Arguments:
- cotangent: bfloat16 [1, 4096, 768], P(None, 'seq'), may hold values from -6 to 6
- projected: bfloat16 [8, 1, 4096, 2304], P('section', None, 'seq'), may hold values from -6 to 6
- w_in: bfloat16 [8, 768, 2304], P('section'), may hold values from -0.21875 to 0.21875
- w_out: bfloat16 [8, 768, 768], P('section'), may hold values from -0.0546875 to 0.0546875
- short_filter: float32 [8, 3, 2304], P('section'), may hold values from -3.5 to 3.5
- long_filter: float32 [8, 4096, 768], P('section', 'seq'), may hold values from -1.1 to 1.1, as said below
- filter_bias: float32 [8, 768], P('section'), may hold values from 0.3 to 0.9
Outputs:
- grads: bfloat16 [8, 1, 4096, 768], P('section', None, 'seq')
The draws below stay inside these ranges and needn't reach their ends.
Inputs may be any that keep to these rules, and one draw needn't show every extreme that they name: `long_filter`: row t of a section's long filter is its response at lag t.
All inputs are finite; a program needn't handle non-finite values.
Results may differ from the reference program's by a relative error of at most 0.03.
Values may be sent and summed in bfloat16 or wider, within the bound.
A program may use at most 64 MiB of HBM per device.

```python
import math
import jax
import jax.numpy as jnp

D = 768
TAPS = 3
MICRO = 1
SECTIONS = 8
SEQ = 4096


def draw_long_filter(key, part):
    keys = jax.random.split(key, 7)
    lags = jnp.arange(SEQ, dtype=jnp.float32)[None, :, None]
    noise = jnp.clip(jax.random.normal(keys[0], (SECTIONS, SEQ, D), jnp.float32), -3.8, 3.8)
    slow_share = 0.5
    slow = jax.random.uniform(keys[1], (SECTIONS, 1, D), jnp.float32) < slow_share
    slow_rate = jnp.exp(jax.random.uniform(keys[2], (SECTIONS, 1, D), jnp.float32, math.log(0.2), 0.0)) / SEQ
    fast_rate = jnp.exp(jax.random.uniform(keys[3], (SECTIONS, 1, D), jnp.float32, math.log(1.0 / 50.0), math.log(1.0 / 30.0)))
    head_rate = jnp.where(slow, slow_rate, fast_rate)
    tail_rate = jnp.exp(jax.random.uniform(keys[5], (SECTIONS, 1, D), jnp.float32, math.log(0.1), math.log(0.5))) / SEQ
    tail_share = jnp.exp(jax.random.uniform(keys[6], (SECTIONS, 1, D), jnp.float32, 0.0, math.log(2.0)))
    head_power = 2.0 * head_rate * jnp.exp(-2.0 * head_rate * lags)
    tail_norm = 2.0 * tail_rate * tail_share / (1.0 - jnp.exp(-2.0 * tail_rate * SEQ))
    tail_power = tail_norm * jnp.exp(-2.0 * tail_rate * lags)
    marks = jax.random.randint(keys[4], (SECTIONS, 1, 1, 3), 1, SEQ).astype(jnp.float32)
    count = jnp.sum((lags[..., None] >= marks).astype(jnp.float32), axis=-1)
    envelope = jnp.sqrt(head_power + tail_power) * jnp.power(0.7, count)
    return noise * envelope


def steps_of(own_key, extent, cuts, low, top_value):
    factor_of = 1.0
    for axis_at, blocks in cuts:
        heights = jax.random.uniform(jax.random.fold_in(jax.random.fold_in(own_key, 6), axis_at), (blocks,), jnp.float32, low / len(cuts), top_value / len(cuts))
        factor_of = factor_of * jnp.repeat(jnp.exp(heights), extent[axis_at] // blocks).reshape((-1,) + (1,) * (len(extent) - 1 - axis_at))
    return factor_of


def bell_draw(own_key, extent, scale, limit, cuts=(), kind=jnp.bfloat16):
    loudness = steps_of(own_key, extent, cuts, -0.22, 0.18) if cuts else 1.0
    result = jax.random.normal(own_key, extent, jnp.float32) * scale * loudness
    return jnp.minimum(jnp.maximum(result, -limit), limit).astype(kind)


def setup_inputs(seed: int = 0) -> dict:
    splits = jax.random.split(jax.random.key(seed), 8)
    return {
        "cotangent": bell_draw(splits[0], (MICRO, SEQ, D), 1.0, 6.0, ((1, 32),)),
        "projected": bell_draw(splits[1], (SECTIONS, MICRO, SEQ, 3 * D), 1.0, 6.0, ((0, 8), (2, 32))),
        "w_in": bell_draw(splits[2], (SECTIONS, D, 3 * D), D ** -0.5, 0.21875, ((0, 8),)),
        "w_out": bell_draw(splits[3], (SECTIONS, D, D), (2 * SECTIONS * D) ** -0.5, 0.0546875, ((0, 8),)),
        "short_filter": bell_draw(splits[4], (SECTIONS, TAPS, 3 * D), TAPS ** -0.5, 3.5, ((0, 8),), jnp.float32),
        "long_filter": draw_long_filter(jax.random.fold_in(splits[7], 71), 0),
        "filter_bias": jnp.clip(0.3 + 0.59999996 * jax.random.uniform(splits[6], (SECTIONS, D), jnp.float32) ** steps_of(splits[6], (SECTIONS, D), ((0, 8),), -0.2, 0.2), 0.3, 0.9),
    }


def causal_conv(response, series):
    size = 2 * series.shape[0]
    spectrum = jnp.fft.rfft(response, n=size, axis=0) * jnp.fft.rfft(series, n=size, axis=0)
    return jnp.fft.irfft(spectrum, n=size, axis=0)[:series.shape[0]]

def causal_corr(response, series):
    size = 2 * series.shape[0]
    spectrum = jnp.conj(jnp.fft.rfft(response, n=size, axis=0)) * jnp.fft.rfft(series, n=size, axis=0)
    return jnp.fft.irfft(spectrum, n=size, axis=0)[:series.shape[0]]

def section_grad(incoming, stored, weight_in, weight_out, taps, response, bias):
    width = weight_out.shape[0]
    zero_rows = jnp.zeros((2, stored.shape[1]), jnp.float32)
    padded = jnp.concatenate([zero_rows, stored.astype(jnp.float32)], axis=0)
    mixed = taps[0] * padded[2:] + taps[1] * padded[1:-1] + taps[2] * padded[:-2]
    query = mixed[:, :width]
    keys = mixed[:, width:2 * width]
    values = mixed[:, 2 * width:]
    product = (keys * values).astype(jnp.bfloat16)
    product_wide = product.astype(jnp.float32)
    conv = (causal_conv(response, product_wide) + bias * product_wide).astype(jnp.bfloat16)
    d_out = jnp.dot(incoming, weight_out.T, preferred_element_type=jnp.float32)
    d_conv = (d_out * query).astype(jnp.bfloat16)
    d_conv_wide = d_conv.astype(jnp.float32)
    d_prod = (causal_corr(response, d_conv_wide) + bias * d_conv_wide).astype(jnp.bfloat16)
    d_prod_wide = d_prod.astype(jnp.float32)
    d_mixed = jnp.concatenate([d_out * conv.astype(jnp.float32), d_prod_wide * values, d_prod_wide * keys], axis=1).astype(jnp.bfloat16)
    padded_grad = jnp.concatenate([d_mixed.astype(jnp.float32), zero_rows], axis=0)
    d_proj = (taps[0] * padded_grad[:-2] + taps[1] * padded_grad[1:-1] + taps[2] * padded_grad[2:]).astype(jnp.bfloat16)
    total = incoming.astype(jnp.float32) + jnp.dot(d_proj, weight_in.T, preferred_element_type=jnp.float32)
    return total.astype(jnp.bfloat16)

def reference(cotangent, projected, w_in, w_out, short_filter, long_filter, filter_bias):
    results = [None] * SECTIONS
    incoming = [cotangent[batch] for batch in range(MICRO)]
    for section in range(SECTIONS - 1, -1, -1):
        outputs = [section_grad(incoming[batch], projected[section, batch], w_in[section], w_out[section], short_filter[section], long_filter[section], filter_bias[section]) for batch in range(MICRO)]
        results[section] = jnp.stack(outputs)
        incoming = outputs
    return jnp.stack(results)
```

```python
import functools
import math

import jax
import jax.numpy as jnp
from jax import lax
from jax.sharding import PartitionSpec as P

accuracy = lax.Precision.HIGH


def shifted(value, axis, by):
    count = lax.axis_size(axis)
    pairs = [(i, i + by) for i in range(count) if 0 <= i + by < count]
    return lax.ppermute(value, axis, pairs)


def phase_table(height, breadth, period):
    row_ids = lax.broadcasted_iota(jnp.int32, (height, breadth), 0)
    col_ids = lax.broadcasted_iota(jnp.int32, (height, breadth), 1)
    angle = (row_ids * col_ids % period).astype(jnp.float32) * (2.0 * math.pi / period)
    return (jnp.cos(angle), jnp.sin(angle))


def forward_spectrum(series, inner):
    length, chans = series.shape
    outer = 2 * length // inner
    blocks = series.reshape(length // inner, inner, chans)
    cos_outer, sin_outer = phase_table(outer, length // inner, outer)
    real_one = jnp.einsum("kn,nbc->cbk", cos_outer, blocks, precision=accuracy)
    imag_one = -jnp.einsum("kn,nbc->cbk", sin_outer, blocks, precision=accuracy)
    cos_twist, sin_twist = phase_table(inner, outer, 2 * length)
    real_two = real_one * cos_twist + imag_one * sin_twist
    imag_two = imag_one * cos_twist - real_one * sin_twist
    cos_inner, sin_inner = phase_table(inner, inner, inner)
    real = jnp.einsum("jb,cbk->cjk", cos_inner, real_two, precision=accuracy) + jnp.einsum(
        "jb,cbk->cjk", sin_inner, imag_two, precision=accuracy
    )
    imag = jnp.einsum("jb,cbk->cjk", cos_inner, imag_two, precision=accuracy) - jnp.einsum(
        "jb,cbk->cjk", sin_inner, real_two, precision=accuracy
    )
    return (real, imag)


def inverse_spectrum(real, imag, inner):
    chans, _, outer = real.shape
    length = outer * inner // 2
    cos_inner, sin_inner = phase_table(inner, inner, inner)
    real_one = jnp.einsum("jb,cjk->cbk", cos_inner, real, precision=accuracy) - jnp.einsum(
        "jb,cjk->cbk", sin_inner, imag, precision=accuracy
    )
    imag_one = jnp.einsum("jb,cjk->cbk", cos_inner, imag, precision=accuracy) + jnp.einsum(
        "jb,cjk->cbk", sin_inner, real, precision=accuracy
    )
    cos_twist, sin_twist = phase_table(inner, outer, 2 * length)
    real_two = real_one * cos_twist - imag_one * sin_twist
    imag_two = imag_one * cos_twist + real_one * sin_twist
    cos_outer, sin_outer = phase_table(outer, length // inner, outer)
    series = jnp.einsum("kn,cbk->nbc", cos_outer, real_two, precision=accuracy) - jnp.einsum(
        "kn,cbk->nbc", sin_outer, imag_two, precision=accuracy
    )
    return series.reshape(length, chans) / (2.0 * length)


def channel_conv(series, spectrum, bias_part, adjoint, inner):
    values = series.astype(jnp.float32)
    real, imag = forward_spectrum(values, inner)
    filter_real, filter_imag = spectrum
    if adjoint:
        prod_real = real * filter_real + imag * filter_imag
        prod_imag = imag * filter_real - real * filter_imag
    else:
        prod_real = real * filter_real - imag * filter_imag
        prod_imag = real * filter_imag + imag * filter_real
    return (inverse_spectrum(prod_real, prod_imag, inner) + bias_part * values).astype(jnp.bfloat16)


def when(active, action, *operands):

    def skipped(*inputs):
        return jax.tree.map(jnp.zeros_like, action(*inputs))

    return lax.cond(active, action, skipped, *operands)


def shards(cotangent, projected, w_in, w_out, short_filter, long_filter, filter_bias):
    seq_count = lax.axis_size("seq")
    seq_place = lax.axis_index("seq")
    section_count = lax.axis_size("section")
    section_place = lax.axis_index("section")
    micro = projected.shape[1]
    height = projected.shape[2]
    width = w_out.shape[2]
    length = height * seq_count
    inner = math.gcd(length, 32)
    chans = width // seq_count
    filter_local = lax.all_to_all(
        long_filter[0].astype(jnp.bfloat16), "seq", split_axis=1, concat_axis=0, tiled=True
    ).astype(jnp.float32)
    spectrum = forward_spectrum(filter_local, inner)
    bias_part = lax.dynamic_slice_in_dim(filter_bias[0], seq_place * chans, chans, 0)
    weight_in = w_in[0]
    weight_out = w_out[0]
    taps = short_filter[0]
    contract = (((1,), (1,)), ((), ()))

    def causal(series):
        return channel_conv(series, spectrum, bias_part, False, inner)

    def adjoint(series):
        return channel_conv(series, spectrum, bias_part, True, inner)

    forward = []
    for slot in range(micro):
        proj = projected[0, slot]
        rim = shifted(proj[height - 2 :], "seq", 1)
        padded = jnp.concatenate([rim, proj], axis=0).astype(jnp.float32)
        mixed = taps[0] * padded[2:] + taps[1] * padded[1:-1] + taps[2] * padded[:-2]
        query = mixed[:, :width]
        keys = mixed[:, width : 2 * width]
        values = mixed[:, 2 * width :]
        product = (keys * values).astype(jnp.bfloat16)
        product_local = lax.all_to_all(product, "seq", split_axis=1, concat_axis=0, tiled=True)
        conv = lax.all_to_all(causal(product_local), "seq", split_axis=0, concat_axis=1, tiled=True)
        forward.append((query, keys, values, conv.astype(jnp.float32)))

    def stage(grad_out, slot):
        query, keys, values, conv_wide = forward[slot]
        d_out = lax.dot_general(grad_out, weight_out, contract, preferred_element_type=jnp.float32)
        d_conv = (d_out * query).astype(jnp.bfloat16)
        d_conv_local = lax.all_to_all(d_conv, "seq", split_axis=1, concat_axis=0, tiled=True)
        d_prod = lax.all_to_all(adjoint(d_conv_local), "seq", split_axis=0, concat_axis=1, tiled=True)
        d_prod_wide = d_prod.astype(jnp.float32)
        d_mixed = jnp.concatenate(
            [d_out * conv_wide, d_prod_wide * values, d_prod_wide * keys], axis=1
        ).astype(jnp.bfloat16)
        rim_below = shifted(d_mixed[:2], "seq", -1)
        padded = jnp.concatenate([d_mixed, rim_below], axis=0).astype(jnp.float32)
        d_proj = (taps[0] * padded[:-2] + taps[1] * padded[1:-1] + taps[2] * padded[2:]).astype(
            jnp.bfloat16
        )
        total = grad_out.astype(jnp.float32) + lax.dot_general(
            d_proj, weight_in, contract, preferred_element_type=jnp.float32
        )
        return total.astype(jnp.bfloat16)

    def tick(step, carry):
        incoming, grads = carry
        index = step - (section_count - 1 - section_place)
        active = (index >= 0) & (index < micro)
        slot = jnp.clip(index, 0, micro - 1)
        if micro == 1:
            d_input = stage(incoming, 0)
        else:
            d_input = lax.switch(slot, [functools.partial(stage, slot=m) for m in range(micro)], incoming)
        grads = jnp.where(active, lax.dynamic_update_index_in_dim(grads, d_input, slot, 0), grads)
        later = jnp.clip(index + 1, 0, micro - 1)
        top = lax.dynamic_index_in_dim(cotangent, later, 0, keepdims=False)
        incoming = jnp.where(section_place == section_count - 1, top, shifted(d_input, "section", -1))
        return (incoming, grads)

    start = (
        cotangent[0],
        jnp.zeros((micro, height, width), jnp.bfloat16),
    )
    incoming, grads = lax.fori_loop(0, micro + section_count - 1, tick, start)
    return grads[None]


def solution(mesh):
    return jax.shard_map(
        shards,
        mesh=mesh,
        in_specs=(
            P(None, "seq", None),
            P("section", None, "seq", None),
            P("section", None, None),
            P("section", None, None),
            P("section", None, None),
            P("section", "seq", None),
            P("section", None),
        ),
        out_specs=P("section", None, "seq", None),
        check_vma=False,
    )
```

```python
import functools
import math

import jax
import jax.numpy as jnp
from jax import lax
from jax.experimental import pallas as pl
from jax.experimental.pallas import tpu as pltpu
from jax.sharding import PartitionSpec as P

accuracy = lax.Precision.HIGH


def shifted(value, axis, by):
    count = lax.axis_size(axis)
    pairs = [(i, i + by) for i in range(count) if 0 <= i + by < count]
    return lax.ppermute(value, axis, pairs)


def phase_table(height, breadth, period):
    row_ids = lax.broadcasted_iota(jnp.int32, (height, breadth), 0)
    col_ids = lax.broadcasted_iota(jnp.int32, (height, breadth), 1)
    angle = (row_ids * col_ids % period).astype(jnp.float32) * (2.0 * math.pi / period)
    return (jnp.cos(angle), jnp.sin(angle))


def forward_spectrum(series, inner):
    length, chans = series.shape
    outer = 2 * length // inner
    blocks = series.reshape(length // inner, inner, chans)
    cos_outer, sin_outer = phase_table(outer, length // inner, outer)
    real_one = jnp.einsum("kn,nbc->cbk", cos_outer, blocks, precision=accuracy)
    imag_one = -jnp.einsum("kn,nbc->cbk", sin_outer, blocks, precision=accuracy)
    cos_twist, sin_twist = phase_table(inner, outer, 2 * length)
    real_two = real_one * cos_twist + imag_one * sin_twist
    imag_two = imag_one * cos_twist - real_one * sin_twist
    cos_inner, sin_inner = phase_table(inner, inner, inner)
    real = jnp.einsum("jb,cbk->cjk", cos_inner, real_two, precision=accuracy) + jnp.einsum(
        "jb,cbk->cjk", sin_inner, imag_two, precision=accuracy
    )
    imag = jnp.einsum("jb,cbk->cjk", cos_inner, imag_two, precision=accuracy) - jnp.einsum(
        "jb,cbk->cjk", sin_inner, real_two, precision=accuracy
    )
    return (real, imag)


def inverse_spectrum(real, imag, inner):
    chans, _, outer = real.shape
    length = outer * inner // 2
    cos_inner, sin_inner = phase_table(inner, inner, inner)
    real_one = jnp.einsum("jb,cjk->cbk", cos_inner, real, precision=accuracy) - jnp.einsum(
        "jb,cjk->cbk", sin_inner, imag, precision=accuracy
    )
    imag_one = jnp.einsum("jb,cjk->cbk", cos_inner, imag, precision=accuracy) + jnp.einsum(
        "jb,cjk->cbk", sin_inner, real, precision=accuracy
    )
    cos_twist, sin_twist = phase_table(inner, outer, 2 * length)
    real_two = real_one * cos_twist - imag_one * sin_twist
    imag_two = imag_one * cos_twist + real_one * sin_twist
    cos_outer, sin_outer = phase_table(outer, length // inner, outer)
    series = jnp.einsum("kn,cbk->nbc", cos_outer, real_two, precision=accuracy) - jnp.einsum(
        "kn,cbk->nbc", sin_outer, imag_two, precision=accuracy
    )
    return series.reshape(length, chans) / (2.0 * length)


def channel_conv(series, spectrum, bias_part, adjoint, inner):
    values = series.astype(jnp.float32)
    real, imag = forward_spectrum(values, inner)
    filter_real, filter_imag = spectrum
    if adjoint:
        prod_real = real * filter_real + imag * filter_imag
        prod_imag = imag * filter_real - real * filter_imag
    else:
        prod_real = real * filter_real - imag * filter_imag
        prod_imag = real * filter_imag + imag * filter_real
    return (inverse_spectrum(prod_real, prod_imag, inner) + bias_part * values).astype(jnp.bfloat16)


def exchange_kernel(x_ref, o_ref, landed, send_sems, recv_sems):
    count = x_ref.shape[0]
    me = lax.axis_index("seq")
    section = lax.axis_index("section")
    mesh_ids = pl.DeviceIdType.MESH
    barrier = pltpu.get_barrier_semaphore()

    def greet(k, _):
        peer = lax.rem(me + k, count)
        pl.semaphore_signal(barrier, inc=1, device_id=(peer, section), device_id_type=mesh_ids)
        return 0

    lax.fori_loop(1, count, greet, 0)
    pl.semaphore_wait(barrier, count - 1)

    def describe(k):
        peer = lax.rem(me + k, count)
        return pltpu.make_async_remote_copy(
            src_ref=x_ref.at[peer],
            dst_ref=landed.at[me],
            send_sem=send_sems.at[k],
            recv_sem=recv_sems.at[k],
            device_id=(peer, section),
            device_id_type=mesh_ids,
        )

    def send(k, _):
        describe(k).start()
        return 0

    def finish(k, _):
        describe(k).wait()
        return 0

    lax.fori_loop(1, count, send, 0)
    lax.fori_loop(1, count, finish, 0)
    o_ref[...] = landed[...]
    o_ref[pl.ds(me, 1)] = x_ref[pl.ds(me, 1)]


def seq_exchange(blocks):
    count = blocks.shape[0]
    return pl.pallas_call(
        exchange_kernel,
        out_shape=jax.ShapeDtypeStruct(blocks.shape, blocks.dtype),
        in_specs=[pl.BlockSpec(memory_space=pltpu.VMEM)],
        out_specs=pl.BlockSpec(memory_space=pltpu.VMEM),
        scratch_shapes=[
            pltpu.VMEM(blocks.shape, blocks.dtype),
            pltpu.SemaphoreType.DMA((count,)),
            pltpu.SemaphoreType.DMA((count,)),
        ],
        compiler_params=pltpu.CompilerParams(collective_id=0, has_side_effects=True),
    )(blocks)


def when(active, action, *operands):

    def skipped(*inputs):
        return jax.tree.map(jnp.zeros_like, action(*inputs))

    return lax.cond(active, action, skipped, *operands)


def shards(cotangent, projected, w_in, w_out, short_filter, long_filter, filter_bias):
    seq_count = lax.axis_size("seq")
    seq_place = lax.axis_index("seq")
    section_count = lax.axis_size("section")
    section_place = lax.axis_index("section")
    micro = projected.shape[1]
    height = projected.shape[2]
    width = w_out.shape[2]
    length = height * seq_count
    inner = math.gcd(length, 32)
    chans = width // seq_count
    bias_part = lax.dynamic_slice_in_dim(filter_bias[0], seq_place * chans, chans, 0)
    weight_in = w_in[0]
    weight_out = w_out[0]
    taps = short_filter[0]
    contract = (((1,), (1,)), ((), ()))

    held = {}

    def causal(series):
        return channel_conv(series, held["spectrum"], bias_part, False, inner)

    def adjoint(series):
        return channel_conv(series, held["spectrum"], bias_part, True, inner)

    forward = []
    for slot in range(micro):
        proj = projected[0, slot]
        rim = shifted(proj[height - 2 :], "seq", 1)
        padded = jnp.concatenate([rim, proj], axis=0).astype(jnp.float32)
        mixed = taps[0] * padded[2:] + taps[1] * padded[1:-1] + taps[2] * padded[:-2]
        query = mixed[:, :width]
        keys = mixed[:, width : 2 * width]
        values = mixed[:, 2 * width :]
        product = (keys * values).astype(jnp.bfloat16)
        if slot == 0:
            both = jnp.stack([long_filter[0].astype(jnp.bfloat16), product])
            both = lax.all_to_all(both, "seq", split_axis=2, concat_axis=1, tiled=True)
            held["spectrum"] = forward_spectrum(both[0].astype(jnp.float32), inner)
            product_local = both[1]
        else:
            product_local = lax.all_to_all(product, "seq", split_axis=1, concat_axis=0, tiled=True)
        conv = lax.all_to_all(causal(product_local), "seq", split_axis=0, concat_axis=1, tiled=True)
        forward.append((query, keys, values, conv.astype(jnp.float32)))

    def stage(grad_out, slot):
        query, keys, values, conv_wide = forward[slot]
        d_out = lax.dot_general(grad_out, weight_out, contract, preferred_element_type=jnp.float32)
        d_conv = (d_out * query).astype(jnp.bfloat16)
        sent = seq_exchange(d_conv.reshape(height, seq_count, chans).transpose(1, 2, 0))
        d_conv_local = sent.transpose(0, 2, 1).reshape(length, chans)
        d_prod_local = adjoint(d_conv_local)
        back = seq_exchange(d_prod_local.reshape(seq_count, height, chans).transpose(0, 2, 1))
        d_prod = back.transpose(2, 0, 1).reshape(height, width)
        d_prod_wide = d_prod.astype(jnp.float32)
        d_mixed = jnp.concatenate(
            [d_out * conv_wide, d_prod_wide * values, d_prod_wide * keys], axis=1
        ).astype(jnp.bfloat16)
        rim_below = shifted(d_mixed[:2], "seq", -1)
        padded = jnp.concatenate([d_mixed, rim_below], axis=0).astype(jnp.float32)
        d_proj = (taps[0] * padded[:-2] + taps[1] * padded[1:-1] + taps[2] * padded[2:]).astype(
            jnp.bfloat16
        )
        total = grad_out.astype(jnp.float32) + lax.dot_general(
            d_proj, weight_in, contract, preferred_element_type=jnp.float32
        )
        return total.astype(jnp.bfloat16)

    def tick(step, carry):
        incoming, grads = carry
        index = step - (section_count - 1 - section_place)
        active = (index >= 0) & (index < micro)
        slot = jnp.clip(index, 0, micro - 1)
        if micro == 1:
            d_input = stage(incoming, 0)
        else:
            d_input = lax.switch(slot, [functools.partial(stage, slot=m) for m in range(micro)], incoming)
        grads = jnp.where(active, lax.dynamic_update_index_in_dim(grads, d_input, slot, 0), grads)
        later = jnp.clip(index + 1, 0, micro - 1)
        top = lax.dynamic_index_in_dim(cotangent, later, 0, keepdims=False)
        incoming = jnp.where(section_place == section_count - 1, top, shifted(d_input, "section", -1))
        return (incoming, grads)

    start = (
        cotangent[0],
        jnp.zeros((micro, height, width), jnp.bfloat16),
    )
    incoming, grads = lax.fori_loop(0, micro + section_count - 1, tick, start)
    return grads[None]


def solution(mesh):
    return jax.shard_map(
        shards,
        mesh=mesh,
        in_specs=(
            P(None, "seq", None),
            P("section", None, "seq", None),
            P("section", None, None),
            P("section", None, None),
            P("section", None, None),
            P("section", "seq", None),
            P("section", None),
        ),
        out_specs=P("section", None, "seq", None),
        check_vma=False,
    )
```

```python
import functools
import math

import jax
import jax.numpy as jnp
from jax import lax
from jax.experimental import pallas as pl
from jax.experimental.pallas import tpu as pltpu
from jax.sharding import PartitionSpec as P

accuracy = lax.Precision.HIGH


def shifted(value, axis, by):
    count = lax.axis_size(axis)
    pairs = [(i, i + by) for i in range(count) if 0 <= i + by < count]
    return lax.ppermute(value, axis, pairs)


def phase_table(height, breadth, period):
    row_ids = lax.broadcasted_iota(jnp.int32, (height, breadth), 0)
    col_ids = lax.broadcasted_iota(jnp.int32, (height, breadth), 1)
    angle = (row_ids * col_ids % period).astype(jnp.float32) * (2.0 * math.pi / period)
    return (jnp.cos(angle), jnp.sin(angle))


def forward_spectrum(series, inner):
    length, chans = series.shape
    outer = 2 * length // inner
    blocks = series.reshape(length // inner, inner, chans)
    cos_outer, sin_outer = phase_table(outer, length // inner, outer)
    real_one = jnp.einsum("kn,nbc->cbk", cos_outer, blocks, precision=accuracy)
    imag_one = -jnp.einsum("kn,nbc->cbk", sin_outer, blocks, precision=accuracy)
    cos_twist, sin_twist = phase_table(inner, outer, 2 * length)
    real_two = real_one * cos_twist + imag_one * sin_twist
    imag_two = imag_one * cos_twist - real_one * sin_twist
    cos_inner, sin_inner = phase_table(inner, inner, inner)
    real = jnp.einsum("jb,cbk->cjk", cos_inner, real_two, precision=accuracy) + jnp.einsum(
        "jb,cbk->cjk", sin_inner, imag_two, precision=accuracy
    )
    imag = jnp.einsum("jb,cbk->cjk", cos_inner, imag_two, precision=accuracy) - jnp.einsum(
        "jb,cbk->cjk", sin_inner, real_two, precision=accuracy
    )
    return (real, imag)


def inverse_spectrum(real, imag, inner):
    chans, _, outer = real.shape
    length = outer * inner // 2
    cos_inner, sin_inner = phase_table(inner, inner, inner)
    real_one = jnp.einsum("jb,cjk->cbk", cos_inner, real, precision=accuracy) - jnp.einsum(
        "jb,cjk->cbk", sin_inner, imag, precision=accuracy
    )
    imag_one = jnp.einsum("jb,cjk->cbk", cos_inner, imag, precision=accuracy) + jnp.einsum(
        "jb,cjk->cbk", sin_inner, real, precision=accuracy
    )
    cos_twist, sin_twist = phase_table(inner, outer, 2 * length)
    real_two = real_one * cos_twist - imag_one * sin_twist
    imag_two = imag_one * cos_twist + real_one * sin_twist
    cos_outer, sin_outer = phase_table(outer, length // inner, outer)
    series = jnp.einsum("kn,cbk->nbc", cos_outer, real_two, precision=accuracy) - jnp.einsum(
        "kn,cbk->nbc", sin_outer, imag_two, precision=accuracy
    )
    return series.reshape(length, chans) / (2.0 * length)


def channel_conv(series, spectrum, bias_part, adjoint, inner):
    values = series.astype(jnp.float32)
    real, imag = forward_spectrum(values, inner)
    filter_real, filter_imag = spectrum
    if adjoint:
        prod_real = real * filter_real + imag * filter_imag
        prod_imag = imag * filter_real - real * filter_imag
    else:
        prod_real = real * filter_real - imag * filter_imag
        prod_imag = real * filter_imag + imag * filter_real
    return (inverse_spectrum(prod_real, prod_imag, inner) + bias_part * values).astype(jnp.bfloat16)


def exchange_kernel(x_ref, o_ref, landed, send_sems, recv_sems):
    count = x_ref.shape[0]
    me = lax.axis_index("seq")
    section = lax.axis_index("section")
    mesh_ids = pl.DeviceIdType.MESH
    barrier = pltpu.get_barrier_semaphore()

    def greet(k, _):
        peer = lax.rem(me + k, count)
        pl.semaphore_signal(barrier, inc=1, device_id=(peer, section), device_id_type=mesh_ids)
        return 0

    lax.fori_loop(1, count, greet, 0)
    pl.semaphore_wait(barrier, count - 1)

    def describe(k):
        peer = lax.rem(me + k, count)
        return pltpu.make_async_remote_copy(
            src_ref=x_ref.at[peer],
            dst_ref=landed.at[me],
            send_sem=send_sems.at[k],
            recv_sem=recv_sems.at[k],
            device_id=(peer, section),
            device_id_type=mesh_ids,
        )

    def send(k, _):
        describe(k).start()
        return 0

    def finish(k, _):
        describe(k).wait()
        return 0

    lax.fori_loop(1, count, send, 0)
    lax.fori_loop(1, count, finish, 0)
    o_ref[...] = landed[...]
    o_ref[pl.ds(me, 1)] = x_ref[pl.ds(me, 1)]


def seq_exchange(blocks):
    count = blocks.shape[0]
    return pl.pallas_call(
        exchange_kernel,
        out_shape=jax.ShapeDtypeStruct(blocks.shape, blocks.dtype),
        in_specs=[pl.BlockSpec(memory_space=pltpu.VMEM)],
        out_specs=pl.BlockSpec(memory_space=pltpu.VMEM),
        scratch_shapes=[
            pltpu.VMEM(blocks.shape, blocks.dtype),
            pltpu.SemaphoreType.DMA((count,)),
            pltpu.SemaphoreType.DMA((count,)),
        ],
        compiler_params=pltpu.CompilerParams(collective_id=0, has_side_effects=True),
    )(blocks)


def finish_kernel(
    sent_ref, d_out_ref, conv_ref, values_ref, keys_ref, grad_ref, taps_ref, weight_ref,
    o_ref, landed, extended, head, send_sems, recv_sems, rim_sems,
):
    count = lax.axis_size("seq")
    rows, width = d_out_ref.shape
    chans = sent_ref.shape[0] // count
    me = lax.axis_index("seq")
    section = lax.axis_index("section")
    mesh_ids = pl.DeviceIdType.MESH
    barrier = pltpu.get_barrier_semaphore()

    def greet(k, _):
        peer = lax.rem(me + k, count)
        pl.semaphore_signal(barrier, inc=1, device_id=(peer, section), device_id_type=mesh_ids)
        return 0

    lax.fori_loop(1, count, greet, 0)
    pl.semaphore_wait(barrier, count - 1)

    def describe(k):
        peer = lax.rem(me + k, count)
        return pltpu.make_async_remote_copy(
            src_ref=sent_ref.at[pl.ds(pl.multiple_of(peer * chans, 8), chans)],
            dst_ref=landed.at[pl.ds(pl.multiple_of(me * chans, 8), chans)],
            send_sem=send_sems.at[k],
            recv_sem=recv_sems.at[k],
            device_id=(peer, section),
            device_id_type=mesh_ids,
        )

    def send(k, _):
        describe(k).start()
        return 0

    def finish(k, _):
        describe(k).wait()
        return 0

    lax.fori_loop(1, count, send, 0)
    own = pl.ds(pl.multiple_of(me * chans, 8), chans)
    landed[own] = sent_ref[own]
    lax.fori_loop(1, count, finish, 0)

    d_prod = landed[...].T
    d_mixed = jnp.concatenate(
        [
            (d_out_ref[...] * conv_ref[...]).astype(jnp.bfloat16),
            (d_prod * values_ref[...]).astype(jnp.bfloat16),
            (d_prod * keys_ref[...]).astype(jnp.bfloat16),
        ],
        axis=1,
    ).astype(jnp.float32)
    head[...] = d_mixed[:8]
    rim = pltpu.make_async_remote_copy(
        src_ref=head,
        dst_ref=extended.at[pl.ds(rows, 8)],
        send_sem=rim_sems.at[0],
        recv_sem=rim_sems.at[1],
        device_id=(jnp.maximum(me - 1, 0), section),
        device_id_type=mesh_ids,
    )

    @pl.when(me > 0)
    def _():
        rim.start()

    extended[pl.ds(0, rows)] = d_mixed

    @pl.when(me == count - 1)
    def _():
        extended[pl.ds(rows, 8)] = jnp.zeros((8, extended.shape[1]), jnp.float32)

    @pl.when(me < count - 1)
    def _():
        rim.wait_recv()

    taps = taps_ref[...]
    d_proj = (
        taps[0:1] * extended[pl.ds(0, rows)]
        + taps[1:2] * extended[pl.ds(1, rows)]
        + taps[2:3] * extended[pl.ds(2, rows)]
    ).astype(jnp.bfloat16)
    total = grad_ref[...].astype(jnp.float32) + lax.dot_general(
        d_proj, weight_ref[...], (((1,), (1,)), ((), ())), preferred_element_type=jnp.float32
    )
    o_ref[...] = total.astype(o_ref.dtype)

    @pl.when(me > 0)
    def _():
        rim.wait_send()


def exchange_and_finish(sent, d_out, conv_wide, values, keys, grad_out, taps, weight_in):
    count = lax.axis_size("seq")
    rows, width = d_out.shape
    vmem = pl.BlockSpec(memory_space=pltpu.VMEM)
    return pl.pallas_call(
        finish_kernel,
        out_shape=jax.ShapeDtypeStruct(grad_out.shape, grad_out.dtype),
        in_specs=[vmem] * 8,
        out_specs=vmem,
        scratch_shapes=[
            pltpu.VMEM(sent.shape, jnp.float32),
            pltpu.VMEM((rows + 8, taps.shape[1]), jnp.float32),
            pltpu.VMEM((8, taps.shape[1]), jnp.float32),
            pltpu.SemaphoreType.DMA((count,)),
            pltpu.SemaphoreType.DMA((count,)),
            pltpu.SemaphoreType.DMA((2,)),
        ],
        compiler_params=pltpu.CompilerParams(collective_id=1, has_side_effects=True),
    )(sent, d_out, conv_wide, values, keys, grad_out, taps, weight_in)


def when(active, action, *operands):

    def skipped(*inputs):
        return jax.tree.map(jnp.zeros_like, action(*inputs))

    return lax.cond(active, action, skipped, *operands)


def shards(cotangent, projected, w_in, w_out, short_filter, long_filter, filter_bias):
    seq_count = lax.axis_size("seq")
    seq_place = lax.axis_index("seq")
    section_count = lax.axis_size("section")
    section_place = lax.axis_index("section")
    micro = projected.shape[1]
    height = projected.shape[2]
    width = w_out.shape[2]
    length = height * seq_count
    inner = math.gcd(length, 32)
    chans = width // seq_count
    bias_part = lax.dynamic_slice_in_dim(filter_bias[0], seq_place * chans, chans, 0)
    weight_in = w_in[0]
    weight_out = w_out[0]
    taps = short_filter[0]
    contract = (((1,), (1,)), ((), ()))

    held = {}

    def causal(series):
        return channel_conv(series, held["spectrum"], bias_part, False, inner)

    def adjoint(series):
        return channel_conv(series, held["spectrum"], bias_part, True, inner)

    forward = []
    for slot in range(micro):
        proj = projected[0, slot]
        rim = shifted(proj[height - 2 :], "seq", 1)
        padded = jnp.concatenate([rim, proj], axis=0).astype(jnp.float32)
        mixed = taps[0] * padded[2:] + taps[1] * padded[1:-1] + taps[2] * padded[:-2]
        query = mixed[:, :width]
        keys = mixed[:, width : 2 * width]
        values = mixed[:, 2 * width :]
        product = (keys * values).astype(jnp.bfloat16)
        if slot == 0:
            both = jnp.stack([long_filter[0].astype(jnp.bfloat16), product])
            both = lax.all_to_all(both, "seq", split_axis=2, concat_axis=1, tiled=True)
            held["spectrum"] = forward_spectrum(both[0].astype(jnp.float32), inner)
            product_local = both[1]
        else:
            product_local = lax.all_to_all(product, "seq", split_axis=1, concat_axis=0, tiled=True)
        conv = lax.all_to_all(causal(product_local), "seq", split_axis=0, concat_axis=1, tiled=True)
        forward.append((query, keys, values, conv.astype(jnp.float32)))

    def stage(grad_out, slot):
        query, keys, values, conv_wide = forward[slot]
        d_out = lax.dot_general(grad_out, weight_out, contract, preferred_element_type=jnp.float32)
        d_conv = (d_out * query).astype(jnp.bfloat16)
        sent = seq_exchange(d_conv.reshape(height, seq_count, chans).transpose(1, 2, 0))
        d_conv_local = sent.transpose(0, 2, 1).reshape(length, chans)
        d_prod_local = adjoint(d_conv_local)
        sent_back = d_prod_local.reshape(seq_count, height, chans).transpose(0, 2, 1)
        sent_back = sent_back.reshape(seq_count * chans, height).astype(jnp.float32)
        return exchange_and_finish(
            sent_back, d_out, conv_wide, values, keys, grad_out, taps, weight_in
        )

    def tick(step, carry):
        incoming, grads = carry
        index = step - (section_count - 1 - section_place)
        active = (index >= 0) & (index < micro)
        slot = jnp.clip(index, 0, micro - 1)
        if micro == 1:
            d_input = stage(incoming, 0)
        else:
            d_input = lax.switch(slot, [functools.partial(stage, slot=m) for m in range(micro)], incoming)
        grads = jnp.where(active, lax.dynamic_update_index_in_dim(grads, d_input, slot, 0), grads)
        later = jnp.clip(index + 1, 0, micro - 1)
        top = lax.dynamic_index_in_dim(cotangent, later, 0, keepdims=False)
        incoming = jnp.where(section_place == section_count - 1, top, shifted(d_input, "section", -1))
        return (incoming, grads)

    start = (
        cotangent[0],
        jnp.zeros((micro, height, width), jnp.bfloat16),
    )
    incoming, grads = lax.fori_loop(0, micro + section_count - 1, tick, start)
    return grads[None]


def solution(mesh):
    return jax.shard_map(
        shards,
        mesh=mesh,
        in_specs=(
            P(None, "seq", None),
            P("section", None, "seq", None),
            P("section", None, None),
            P("section", None, None),
            P("section", None, None),
            P("section", "seq", None),
            P("section", None),
        ),
        out_specs=P("section", None, "seq", None),
        check_vma=False,
    )
```

```python
import functools
import math

import jax
import jax.numpy as jnp
from jax import lax
from jax.experimental import pallas as pl
from jax.experimental.pallas import tpu as pltpu
from jax.sharding import PartitionSpec as P

accuracy = lax.Precision.HIGH


def shifted(value, axis, by):
    count = lax.axis_size(axis)
    pairs = [(i, i + by) for i in range(count) if 0 <= i + by < count]
    return lax.ppermute(value, axis, pairs)


def phase_table(height, breadth, period):
    row_ids = lax.broadcasted_iota(jnp.int32, (height, breadth), 0)
    col_ids = lax.broadcasted_iota(jnp.int32, (height, breadth), 1)
    angle = (row_ids * col_ids % period).astype(jnp.float32) * (2.0 * math.pi / period)
    return (jnp.cos(angle), jnp.sin(angle))


def forward_spectrum(series, inner):
    length, chans = series.shape
    outer = 2 * length // inner
    blocks = series.reshape(length // inner, inner, chans)
    cos_outer, sin_outer = phase_table(outer, length // inner, outer)
    real_one = jnp.einsum("kn,nbc->cbk", cos_outer, blocks, precision=accuracy)
    imag_one = -jnp.einsum("kn,nbc->cbk", sin_outer, blocks, precision=accuracy)
    cos_twist, sin_twist = phase_table(inner, outer, 2 * length)
    real_two = real_one * cos_twist + imag_one * sin_twist
    imag_two = imag_one * cos_twist - real_one * sin_twist
    cos_inner, sin_inner = phase_table(inner, inner, inner)
    real = jnp.einsum("jb,cbk->cjk", cos_inner, real_two, precision=accuracy) + jnp.einsum(
        "jb,cbk->cjk", sin_inner, imag_two, precision=accuracy
    )
    imag = jnp.einsum("jb,cbk->cjk", cos_inner, imag_two, precision=accuracy) - jnp.einsum(
        "jb,cbk->cjk", sin_inner, real_two, precision=accuracy
    )
    return (real, imag)


def inverse_spectrum(real, imag, inner):
    chans, _, outer = real.shape
    length = outer * inner // 2
    cos_inner, sin_inner = phase_table(inner, inner, inner)
    real_one = jnp.einsum("jb,cjk->cbk", cos_inner, real, precision=accuracy) - jnp.einsum(
        "jb,cjk->cbk", sin_inner, imag, precision=accuracy
    )
    imag_one = jnp.einsum("jb,cjk->cbk", cos_inner, imag, precision=accuracy) + jnp.einsum(
        "jb,cjk->cbk", sin_inner, real, precision=accuracy
    )
    cos_twist, sin_twist = phase_table(inner, outer, 2 * length)
    real_two = real_one * cos_twist - imag_one * sin_twist
    imag_two = imag_one * cos_twist + real_one * sin_twist
    cos_outer, sin_outer = phase_table(outer, length // inner, outer)
    series = jnp.einsum("kn,cbk->nbc", cos_outer, real_two, precision=accuracy) - jnp.einsum(
        "kn,cbk->nbc", sin_outer, imag_two, precision=accuracy
    )
    return series.reshape(length, chans) / (2.0 * length)


def channel_conv(series, spectrum, bias_part, adjoint, inner):
    values = series.astype(jnp.float32)
    real, imag = forward_spectrum(values, inner)
    filter_real, filter_imag = spectrum
    if adjoint:
        prod_real = real * filter_real + imag * filter_imag
        prod_imag = imag * filter_real - real * filter_imag
    else:
        prod_real = real * filter_real - imag * filter_imag
        prod_imag = real * filter_imag + imag * filter_real
    return (inverse_spectrum(prod_real, prod_imag, inner) + bias_part * values).astype(jnp.bfloat16)


def exchange_kernel(x_ref, o_ref, landed, send_sems, recv_sems):
    count = x_ref.shape[0]
    me = lax.axis_index("seq")
    section = lax.axis_index("section")
    mesh_ids = pl.DeviceIdType.MESH
    barrier = pltpu.get_barrier_semaphore()

    def greet(k, _):
        peer = lax.rem(me + k, count)
        pl.semaphore_signal(barrier, inc=1, device_id=(peer, section), device_id_type=mesh_ids)
        return 0

    lax.fori_loop(1, count, greet, 0)
    pl.semaphore_wait(barrier, count - 1)

    def describe(k):
        peer = lax.rem(me + k, count)
        return pltpu.make_async_remote_copy(
            src_ref=x_ref.at[peer],
            dst_ref=landed.at[me],
            send_sem=send_sems.at[k],
            recv_sem=recv_sems.at[k],
            device_id=(peer, section),
            device_id_type=mesh_ids,
        )

    def send(k, _):
        describe(k).start()
        return 0

    def finish(k, _):
        describe(k).wait()
        return 0

    lax.fori_loop(1, count, send, 0)
    lax.fori_loop(1, count, finish, 0)
    o_ref[...] = landed[...]
    o_ref[pl.ds(me, 1)] = x_ref[pl.ds(me, 1)]


def seq_exchange(blocks):
    count = blocks.shape[0]
    return pl.pallas_call(
        exchange_kernel,
        out_shape=jax.ShapeDtypeStruct(blocks.shape, blocks.dtype),
        in_specs=[pl.BlockSpec(memory_space=pltpu.VMEM)],
        out_specs=pl.BlockSpec(memory_space=pltpu.VMEM),
        scratch_shapes=[
            pltpu.VMEM(blocks.shape, blocks.dtype),
            pltpu.SemaphoreType.DMA((count,)),
            pltpu.SemaphoreType.DMA((count,)),
        ],
        compiler_params=pltpu.CompilerParams(collective_id=0, has_side_effects=True),
    )(blocks)


def finish_kernel(
    sent_ref, d_out_ref, conv_ref, values_ref, keys_ref, grad_ref, taps_ref, weight_ref,
    o_ref, next_ref, landed, extended, head, from_above, send_sems, recv_sems, rim_sems, hand_sems, acks,
):
    count = lax.axis_size("seq")
    rows, width = d_out_ref.shape
    chans = sent_ref.shape[0] // count
    me = lax.axis_index("seq")
    section = lax.axis_index("section")
    mesh_ids = pl.DeviceIdType.MESH
    barrier = pltpu.get_barrier_semaphore()

    def greet(k, _):
        peer = lax.rem(me + k, count)
        pl.semaphore_signal(barrier, inc=1, device_id=(peer, section), device_id_type=mesh_ids)
        return 0

    lax.fori_loop(1, count, greet, 0)
    sections = lax.axis_size("section")
    has_up = section < sections - 1
    has_down = section > 0
    up = (me, jnp.minimum(section + 1, sections - 1))
    down = (me, jnp.maximum(section - 1, 0))
    neighbours = has_up.astype(jnp.int32) + has_down.astype(jnp.int32)

    @pl.when(has_up)
    def _():
        pl.semaphore_signal(barrier, inc=1, device_id=up, device_id_type=mesh_ids)

    @pl.when(has_down)
    def _():
        pl.semaphore_signal(barrier, inc=1, device_id=down, device_id_type=mesh_ids)

    pl.semaphore_wait(barrier, count - 1 + neighbours)

    @pl.when(has_up)
    def _():
        pl.semaphore_signal(acks, inc=1, device_id=up, device_id_type=mesh_ids)

    @pl.when(has_down)
    def _():
        pl.semaphore_signal(acks, inc=1, device_id=down, device_id_type=mesh_ids)

    def describe(k):
        peer = lax.rem(me + k, count)
        return pltpu.make_async_remote_copy(
            src_ref=sent_ref.at[pl.ds(pl.multiple_of(peer * chans, 8), chans)],
            dst_ref=landed.at[pl.ds(pl.multiple_of(me * chans, 8), chans)],
            send_sem=send_sems.at[k],
            recv_sem=recv_sems.at[k],
            device_id=(peer, section),
            device_id_type=mesh_ids,
        )

    def send(k, _):
        describe(k).start()
        return 0

    def finish(k, _):
        describe(k).wait()
        return 0

    lax.fori_loop(1, count, send, 0)
    own = pl.ds(pl.multiple_of(me * chans, 8), chans)
    landed[own] = sent_ref[own]
    lax.fori_loop(1, count, finish, 0)

    d_prod = landed[...].T
    d_mixed = jnp.concatenate(
        [
            (d_out_ref[...] * conv_ref[...]).astype(jnp.bfloat16),
            (d_prod * values_ref[...]).astype(jnp.bfloat16),
            (d_prod * keys_ref[...]).astype(jnp.bfloat16),
        ],
        axis=1,
    ).astype(jnp.float32)
    head[...] = d_mixed[:8]
    rim = pltpu.make_async_remote_copy(
        src_ref=head,
        dst_ref=extended.at[pl.ds(rows, 8)],
        send_sem=rim_sems.at[0],
        recv_sem=rim_sems.at[1],
        device_id=(jnp.maximum(me - 1, 0), section),
        device_id_type=mesh_ids,
    )

    @pl.when(me > 0)
    def _():
        rim.start()

    extended[pl.ds(0, rows)] = d_mixed

    @pl.when(me == count - 1)
    def _():
        extended[pl.ds(rows, 8)] = jnp.zeros((8, extended.shape[1]), jnp.float32)

    @pl.when(me < count - 1)
    def _():
        rim.wait_recv()

    taps = taps_ref[...]
    d_proj = (
        taps[0:1] * extended[pl.ds(0, rows)]
        + taps[1:2] * extended[pl.ds(1, rows)]
        + taps[2:3] * extended[pl.ds(2, rows)]
    ).astype(jnp.bfloat16)
    total = grad_ref[...].astype(jnp.float32) + lax.dot_general(
        d_proj, weight_ref[...], (((1,), (1,)), ((), ())), preferred_element_type=jnp.float32
    )
    o_ref[...] = total.astype(o_ref.dtype)
    hand = pltpu.make_async_remote_copy(
        src_ref=o_ref,
        dst_ref=from_above,
        send_sem=hand_sems.at[0],
        recv_sem=hand_sems.at[1],
        device_id=down,
        device_id_type=mesh_ids,
    )

    @pl.when(has_down)
    def _():
        hand.start()

    @pl.when(me > 0)
    def _():
        rim.wait_send()

    @pl.when(has_up)
    def _():
        hand.wait_recv()
        next_ref[...] = from_above[...]

    @pl.when(jnp.logical_not(has_up))
    def _():
        next_ref[...] = jnp.zeros(next_ref.shape, next_ref.dtype)

    @pl.when(has_down)
    def _():
        hand.wait_send()

    pl.semaphore_wait(acks, neighbours)


def exchange_and_finish(sent, d_out, conv_wide, values, keys, grad_out, taps, weight_in):
    count = lax.axis_size("seq")
    rows, width = d_out.shape
    vmem = pl.BlockSpec(memory_space=pltpu.VMEM)
    return pl.pallas_call(
        finish_kernel,
        out_shape=(
            jax.ShapeDtypeStruct(grad_out.shape, grad_out.dtype),
            jax.ShapeDtypeStruct(grad_out.shape, grad_out.dtype),
        ),
        in_specs=[vmem] * 8,
        out_specs=(vmem, vmem),
        scratch_shapes=[
            pltpu.VMEM(sent.shape, jnp.float32),
            pltpu.VMEM((rows + 8, taps.shape[1]), jnp.float32),
            pltpu.VMEM((8, taps.shape[1]), jnp.float32),
            pltpu.VMEM(grad_out.shape, grad_out.dtype),
            pltpu.SemaphoreType.DMA((count,)),
            pltpu.SemaphoreType.DMA((count,)),
            pltpu.SemaphoreType.DMA((2,)),
            pltpu.SemaphoreType.DMA((2,)),
            pltpu.SemaphoreType.REGULAR,
        ],
        compiler_params=pltpu.CompilerParams(collective_id=1, has_side_effects=True),
    )(sent, d_out, conv_wide, values, keys, grad_out, taps, weight_in)


def when(active, action, *operands):

    def skipped(*inputs):
        return jax.tree.map(jnp.zeros_like, action(*inputs))

    return lax.cond(active, action, skipped, *operands)


def shards(cotangent, projected, w_in, w_out, short_filter, long_filter, filter_bias):
    seq_count = lax.axis_size("seq")
    seq_place = lax.axis_index("seq")
    section_count = lax.axis_size("section")
    section_place = lax.axis_index("section")
    micro = projected.shape[1]
    height = projected.shape[2]
    width = w_out.shape[2]
    length = height * seq_count
    inner = math.gcd(length, 32)
    chans = width // seq_count
    bias_part = lax.dynamic_slice_in_dim(filter_bias[0], seq_place * chans, chans, 0)
    weight_in = w_in[0]
    weight_out = w_out[0]
    taps = short_filter[0]
    contract = (((1,), (1,)), ((), ()))

    held = {}

    def causal(series):
        return channel_conv(series, held["spectrum"], bias_part, False, inner)

    def adjoint(series):
        return channel_conv(series, held["spectrum"], bias_part, True, inner)

    forward = []
    for slot in range(micro):
        proj = projected[0, slot]
        rim = shifted(proj[height - 2 :], "seq", 1)
        padded = jnp.concatenate([rim, proj], axis=0).astype(jnp.float32)
        mixed = taps[0] * padded[2:] + taps[1] * padded[1:-1] + taps[2] * padded[:-2]
        query = mixed[:, :width]
        keys = mixed[:, width : 2 * width]
        values = mixed[:, 2 * width :]
        product = (keys * values).astype(jnp.bfloat16)
        if slot == 0:
            both = jnp.stack([long_filter[0].astype(jnp.bfloat16), product])
            both = lax.all_to_all(both, "seq", split_axis=2, concat_axis=1, tiled=True)
            held["spectrum"] = forward_spectrum(both[0].astype(jnp.float32), inner)
            product_local = both[1]
        else:
            product_local = lax.all_to_all(product, "seq", split_axis=1, concat_axis=0, tiled=True)
        conv = lax.all_to_all(causal(product_local), "seq", split_axis=0, concat_axis=1, tiled=True)
        forward.append((query, keys, values, conv.astype(jnp.float32)))

    def stage(grad_out, slot):
        query, keys, values, conv_wide = forward[slot]
        d_out = lax.dot_general(grad_out, weight_out, contract, preferred_element_type=jnp.float32)
        d_conv = (d_out * query).astype(jnp.bfloat16)
        sent = seq_exchange(d_conv.reshape(height, seq_count, chans).transpose(1, 2, 0))
        d_conv_local = sent.transpose(0, 2, 1).reshape(length, chans)
        d_prod_local = adjoint(d_conv_local)
        sent_back = d_prod_local.reshape(seq_count, height, chans).transpose(0, 2, 1)
        sent_back = sent_back.reshape(seq_count * chans, height).astype(jnp.float32)
        return exchange_and_finish(
            sent_back, d_out, conv_wide, values, keys, grad_out, taps, weight_in
        )

    def tick(step, carry):
        incoming, grads = carry
        index = step - (section_count - 1 - section_place)
        active = (index >= 0) & (index < micro)
        slot = jnp.clip(index, 0, micro - 1)
        if micro == 1:
            d_input, arrived = stage(incoming, 0)
        else:
            d_input, arrived = lax.switch(
                slot, [functools.partial(stage, slot=m) for m in range(micro)], incoming
            )
        grads = jnp.where(active, lax.dynamic_update_index_in_dim(grads, d_input, slot, 0), grads)
        later = jnp.clip(index + 1, 0, micro - 1)
        top = lax.dynamic_index_in_dim(cotangent, later, 0, keepdims=False)
        incoming = jnp.where(section_place == section_count - 1, top, arrived)
        return (incoming, grads)

    start = (
        cotangent[0],
        jnp.zeros((micro, height, width), jnp.bfloat16),
    )
    incoming, grads = lax.fori_loop(0, micro + section_count - 1, tick, start)
    return grads[None]


def solution(mesh):
    return jax.shard_map(
        shards,
        mesh=mesh,
        in_specs=(
            P(None, "seq", None),
            P("section", None, "seq", None),
            P("section", None, None),
            P("section", None, None),
            P("section", None, None),
            P("section", "seq", None),
            P("section", None),
        ),
        out_specs=P("section", None, "seq", None),
        check_vma=False,
    )
```

```python
import functools
import math

import jax
import jax.numpy as jnp
from jax import lax
from jax.experimental import pallas as pl
from jax.experimental.pallas import tpu as pltpu
from jax.sharding import PartitionSpec as P

accuracy = lax.Precision.HIGH


def shifted(value, axis, by):
    count = lax.axis_size(axis)
    pairs = [(i, i + by) for i in range(count) if 0 <= i + by < count]
    return lax.ppermute(value, axis, pairs)


def phase_table(height, breadth, period):
    row_ids = lax.broadcasted_iota(jnp.int32, (height, breadth), 0)
    col_ids = lax.broadcasted_iota(jnp.int32, (height, breadth), 1)
    angle = (row_ids * col_ids % period).astype(jnp.float32) * (2.0 * math.pi / period)
    return (jnp.cos(angle), jnp.sin(angle))


def forward_spectrum(series, inner):
    length, chans = series.shape
    outer = 2 * length // inner
    blocks = series.reshape(length // inner, inner, chans)
    cos_outer, sin_outer = phase_table(outer, length // inner, outer)
    one = jnp.einsum(
        "kn,nbc->cbk", jnp.concatenate([cos_outer, -sin_outer], axis=0), blocks, precision=accuracy
    )
    real_one = one[:, :, :outer]
    imag_one = one[:, :, outer:]
    cos_twist, sin_twist = phase_table(inner, outer, 2 * length)
    real_two = real_one * cos_twist + imag_one * sin_twist
    imag_two = imag_one * cos_twist - real_one * sin_twist
    cos_inner, sin_inner = phase_table(inner, inner, inner)
    mixer = jnp.concatenate(
        [
            jnp.concatenate([cos_inner, sin_inner], axis=1),
            jnp.concatenate([-sin_inner, cos_inner], axis=1),
        ],
        axis=0,
    )
    both = jnp.einsum(
        "jb,cbk->cjk", mixer, jnp.concatenate([real_two, imag_two], axis=1), precision=accuracy
    )
    return (both[:, :inner], both[:, inner:])


def inverse_spectrum(real, imag, inner):
    chans, _, outer = real.shape
    length = outer * inner // 2
    cos_inner, sin_inner = phase_table(inner, inner, inner)
    mixer = jnp.concatenate(
        [
            jnp.concatenate([cos_inner, -sin_inner], axis=1),
            jnp.concatenate([sin_inner, cos_inner], axis=1),
        ],
        axis=0,
    )
    both = jnp.einsum(
        "jb,cjk->cbk", mixer.T, jnp.concatenate([real, imag], axis=1), precision=accuracy
    )
    real_one = both[:, :inner]
    imag_one = both[:, inner:]
    cos_twist, sin_twist = phase_table(inner, outer, 2 * length)
    real_two = real_one * cos_twist - imag_one * sin_twist
    imag_two = imag_one * cos_twist + real_one * sin_twist
    cos_outer, sin_outer = phase_table(outer, length // inner, outer)
    series = jnp.einsum(
        "kn,cbk->nbc",
        jnp.concatenate([cos_outer, -sin_outer], axis=0),
        jnp.concatenate([real_two, imag_two], axis=2),
        precision=accuracy,
    )
    return series.reshape(length, chans) / (2.0 * length)


def channel_conv(series, spectrum, bias_part, adjoint, inner):
    values = series.astype(jnp.float32)
    real, imag = forward_spectrum(values, inner)
    filter_real, filter_imag = spectrum
    if adjoint:
        prod_real = real * filter_real + imag * filter_imag
        prod_imag = imag * filter_real - real * filter_imag
    else:
        prod_real = real * filter_real - imag * filter_imag
        prod_imag = real * filter_imag + imag * filter_real
    return (inverse_spectrum(prod_real, prod_imag, inner) + bias_part * values).astype(jnp.bfloat16)


def exchange_kernel(x_ref, o_ref, landed, send_sems, recv_sems):
    count = x_ref.shape[0]
    me = lax.axis_index("seq")
    section = lax.axis_index("section")
    mesh_ids = pl.DeviceIdType.MESH
    barrier = pltpu.get_barrier_semaphore()

    def greet(k, _):
        peer = lax.rem(me + k, count)
        pl.semaphore_signal(barrier, inc=1, device_id=(peer, section), device_id_type=mesh_ids)
        return 0

    lax.fori_loop(1, count, greet, 0)
    pl.semaphore_wait(barrier, count - 1)

    def describe(k):
        peer = lax.rem(me + k, count)
        return pltpu.make_async_remote_copy(
            src_ref=x_ref.at[peer],
            dst_ref=landed.at[me],
            send_sem=send_sems.at[k],
            recv_sem=recv_sems.at[k],
            device_id=(peer, section),
            device_id_type=mesh_ids,
        )

    def send(k, _):
        describe(k).start()
        return 0

    def finish(k, _):
        describe(k).wait()
        return 0

    lax.fori_loop(1, count, send, 0)
    lax.fori_loop(1, count, finish, 0)
    o_ref[...] = landed[...]
    o_ref[pl.ds(me, 1)] = x_ref[pl.ds(me, 1)]


def seq_exchange(blocks):
    count = blocks.shape[0]
    return pl.pallas_call(
        exchange_kernel,
        out_shape=jax.ShapeDtypeStruct(blocks.shape, blocks.dtype),
        in_specs=[pl.BlockSpec(memory_space=pltpu.VMEM)],
        out_specs=pl.BlockSpec(memory_space=pltpu.VMEM),
        scratch_shapes=[
            pltpu.VMEM(blocks.shape, blocks.dtype),
            pltpu.SemaphoreType.DMA((count,)),
            pltpu.SemaphoreType.DMA((count,)),
        ],
        compiler_params=pltpu.CompilerParams(collective_id=0, has_side_effects=True),
    )(blocks)


def finish_kernel(
    sent_ref, d_out_ref, conv_ref, values_ref, keys_ref, grad_ref, taps_ref, weight_ref, top_ref,
    o_ref, next_ref, landed, extended, head, from_above, send_sems, recv_sems, rim_sems, hand_sems, acks,
):
    count = lax.axis_size("seq")
    rows, width = d_out_ref.shape
    chans = sent_ref.shape[0] // count
    me = lax.axis_index("seq")
    section = lax.axis_index("section")
    mesh_ids = pl.DeviceIdType.MESH
    barrier = pltpu.get_barrier_semaphore()

    def greet(k, _):
        peer = lax.rem(me + k, count)
        pl.semaphore_signal(barrier, inc=1, device_id=(peer, section), device_id_type=mesh_ids)
        return 0

    lax.fori_loop(1, count, greet, 0)
    sections = lax.axis_size("section")
    has_up = section < sections - 1
    has_down = section > 0
    up = (me, jnp.minimum(section + 1, sections - 1))
    down = (me, jnp.maximum(section - 1, 0))
    neighbours = has_up.astype(jnp.int32) + has_down.astype(jnp.int32)

    @pl.when(has_up)
    def _():
        pl.semaphore_signal(barrier, inc=1, device_id=up, device_id_type=mesh_ids)

    @pl.when(has_down)
    def _():
        pl.semaphore_signal(barrier, inc=1, device_id=down, device_id_type=mesh_ids)

    pl.semaphore_wait(barrier, count - 1 + neighbours)

    @pl.when(has_up)
    def _():
        pl.semaphore_signal(acks, inc=1, device_id=up, device_id_type=mesh_ids)

    @pl.when(has_down)
    def _():
        pl.semaphore_signal(acks, inc=1, device_id=down, device_id_type=mesh_ids)

    def describe(k):
        peer = lax.rem(me + k, count)
        return pltpu.make_async_remote_copy(
            src_ref=sent_ref.at[pl.ds(pl.multiple_of(peer * chans, 8), chans)],
            dst_ref=landed.at[pl.ds(pl.multiple_of(me * chans, 8), chans)],
            send_sem=send_sems.at[k],
            recv_sem=recv_sems.at[k],
            device_id=(peer, section),
            device_id_type=mesh_ids,
        )

    def send(k, _):
        describe(k).start()
        return 0

    def finish(k, _):
        describe(k).wait()
        return 0

    lax.fori_loop(1, count, send, 0)
    own = pl.ds(pl.multiple_of(me * chans, 8), chans)
    landed[own] = sent_ref[own]
    lax.fori_loop(1, count, finish, 0)

    d_prod = landed[...].T
    d_mixed = jnp.concatenate(
        [
            (d_out_ref[...] * conv_ref[...]).astype(jnp.bfloat16),
            (d_prod * values_ref[...]).astype(jnp.bfloat16),
            (d_prod * keys_ref[...]).astype(jnp.bfloat16),
        ],
        axis=1,
    ).astype(jnp.float32)
    head[...] = d_mixed[:8]
    rim = pltpu.make_async_remote_copy(
        src_ref=head,
        dst_ref=extended.at[pl.ds(rows, 8)],
        send_sem=rim_sems.at[0],
        recv_sem=rim_sems.at[1],
        device_id=(jnp.maximum(me - 1, 0), section),
        device_id_type=mesh_ids,
    )

    @pl.when(me > 0)
    def _():
        rim.start()

    extended[pl.ds(0, rows)] = d_mixed

    @pl.when(me == count - 1)
    def _():
        extended[pl.ds(rows, 8)] = jnp.zeros((8, extended.shape[1]), jnp.float32)

    @pl.when(me < count - 1)
    def _():
        rim.wait_recv()

    taps = taps_ref[...]
    d_proj = (
        taps[0:1] * extended[pl.ds(0, rows)]
        + taps[1:2] * extended[pl.ds(1, rows)]
        + taps[2:3] * extended[pl.ds(2, rows)]
    ).astype(jnp.bfloat16)
    total = grad_ref[...].astype(jnp.float32) + lax.dot_general(
        d_proj, weight_ref[...], (((1,), (1,)), ((), ())), preferred_element_type=jnp.float32
    )
    o_ref[...] = total.astype(o_ref.dtype)
    hand = pltpu.make_async_remote_copy(
        src_ref=o_ref,
        dst_ref=from_above,
        send_sem=hand_sems.at[0],
        recv_sem=hand_sems.at[1],
        device_id=down,
        device_id_type=mesh_ids,
    )

    @pl.when(has_down)
    def _():
        hand.start()

    @pl.when(me > 0)
    def _():
        rim.wait_send()

    @pl.when(has_up)
    def _():
        hand.wait_recv()
        next_ref[...] = from_above[...]

    @pl.when(jnp.logical_not(has_up))
    def _():
        next_ref[...] = top_ref[...]

    @pl.when(has_down)
    def _():
        hand.wait_send()

    pl.semaphore_wait(acks, neighbours)


def exchange_and_finish(sent, d_out, conv_wide, values, keys, grad_out, taps, weight_in, top):
    count = lax.axis_size("seq")
    rows, width = d_out.shape
    vmem = pl.BlockSpec(memory_space=pltpu.VMEM)
    return pl.pallas_call(
        finish_kernel,
        out_shape=(
            jax.ShapeDtypeStruct(grad_out.shape, grad_out.dtype),
            jax.ShapeDtypeStruct(grad_out.shape, grad_out.dtype),
        ),
        in_specs=[vmem] * 9,
        out_specs=(vmem, vmem),
        scratch_shapes=[
            pltpu.VMEM(sent.shape, jnp.float32),
            pltpu.VMEM((rows + 8, taps.shape[1]), jnp.float32),
            pltpu.VMEM((8, taps.shape[1]), jnp.float32),
            pltpu.VMEM(grad_out.shape, grad_out.dtype),
            pltpu.SemaphoreType.DMA((count,)),
            pltpu.SemaphoreType.DMA((count,)),
            pltpu.SemaphoreType.DMA((2,)),
            pltpu.SemaphoreType.DMA((2,)),
            pltpu.SemaphoreType.REGULAR,
        ],
        compiler_params=pltpu.CompilerParams(collective_id=1, has_side_effects=True),
    )(sent, d_out, conv_wide, values, keys, grad_out, taps, weight_in, top)


def when(active, action, *operands):

    def skipped(*inputs):
        return jax.tree.map(jnp.zeros_like, action(*inputs))

    return lax.cond(active, action, skipped, *operands)


def shards(cotangent, projected, w_in, w_out, short_filter, long_filter, filter_bias):
    seq_count = lax.axis_size("seq")
    seq_place = lax.axis_index("seq")
    section_count = lax.axis_size("section")
    section_place = lax.axis_index("section")
    micro = projected.shape[1]
    height = projected.shape[2]
    width = w_out.shape[2]
    length = height * seq_count
    inner = math.gcd(length, 32)
    chans = width // seq_count
    bias_part = lax.dynamic_slice_in_dim(filter_bias[0], seq_place * chans, chans, 0)
    weight_in = w_in[0]
    weight_out = w_out[0]
    taps = short_filter[0]
    contract = (((1,), (1,)), ((), ()))

    held = {}

    def causal(series):
        return channel_conv(series, held["spectrum"], bias_part, False, inner)

    def adjoint(series):
        return channel_conv(series, held["spectrum"], bias_part, True, inner)

    forward = []
    for slot in range(micro):
        proj = projected[0, slot]
        rim = shifted(proj[height - 2 :], "seq", 1)
        padded = jnp.concatenate([rim, proj], axis=0).astype(jnp.float32)
        mixed = taps[0] * padded[2:] + taps[1] * padded[1:-1] + taps[2] * padded[:-2]
        query = mixed[:, :width]
        keys = mixed[:, width : 2 * width]
        values = mixed[:, 2 * width :]
        product = (keys * values).astype(jnp.bfloat16)
        if slot == 0:
            both = jnp.stack([long_filter[0].astype(jnp.bfloat16), product])
            both = lax.all_to_all(both, "seq", split_axis=2, concat_axis=1, tiled=True)
            held["spectrum"] = forward_spectrum(both[0].astype(jnp.float32), inner)
            product_local = both[1]
        else:
            product_local = lax.all_to_all(product, "seq", split_axis=1, concat_axis=0, tiled=True)
        conv = lax.all_to_all(causal(product_local), "seq", split_axis=0, concat_axis=1, tiled=True)
        forward.append((query, keys, values, conv.astype(jnp.float32)))

    def stage(grad_out, top, slot):
        query, keys, values, conv_wide = forward[slot]
        d_out = lax.dot_general(grad_out, weight_out, contract, preferred_element_type=jnp.float32)
        d_conv = (d_out * query).astype(jnp.bfloat16)
        sent = seq_exchange(d_conv.reshape(height, seq_count, chans).transpose(1, 2, 0))
        d_conv_local = sent.transpose(0, 2, 1).reshape(length, chans)
        d_prod_local = adjoint(d_conv_local)
        sent_back = d_prod_local.reshape(seq_count, height, chans).transpose(0, 2, 1)
        sent_back = sent_back.reshape(seq_count * chans, height).astype(jnp.float32)
        return exchange_and_finish(
            sent_back, d_out, conv_wide, values, keys, grad_out, taps, weight_in, top
        )

    def tick(step, carry):
        incoming, grads = carry
        index = step - (section_count - 1 - section_place)
        active = (index >= 0) & (index < micro)
        slot = jnp.clip(index, 0, micro - 1)
        later = jnp.clip(index + 1, 0, micro - 1)
        top = lax.dynamic_index_in_dim(cotangent, later, 0, keepdims=False)
        if micro == 1:
            d_input, incoming = stage(incoming, top, 0)
        else:
            d_input, incoming = lax.switch(
                slot, [functools.partial(stage, slot=m) for m in range(micro)], incoming, top
            )
        grads = jnp.where(active, lax.dynamic_update_index_in_dim(grads, d_input, slot, 0), grads)
        return (incoming, grads)

    start = (
        cotangent[0],
        jnp.zeros((micro, height, width), jnp.bfloat16),
    )
    incoming, grads = lax.fori_loop(0, micro + section_count - 1, tick, start)
    return grads[None]


def solution(mesh):
    return jax.shard_map(
        shards,
        mesh=mesh,
        in_specs=(
            P(None, "seq", None),
            P("section", None, "seq", None),
            P("section", None, None),
            P("section", None, None),
            P("section", None, None),
            P("section", "seq", None),
            P("section", None),
        ),
        out_specs=P("section", None, "seq", None),
        check_vma=False,
    )
```

```python
import functools
import math

import jax
import jax.numpy as jnp
from jax import lax
from jax.experimental import pallas as pl
from jax.experimental.pallas import tpu as pltpu
from jax.sharding import PartitionSpec as P

accuracy = lax.Precision.HIGH


def shifted(value, axis, by):
    count = lax.axis_size(axis)
    pairs = [(i, i + by) for i in range(count) if 0 <= i + by < count]
    return lax.ppermute(value, axis, pairs)


def phase_table(height, breadth, period):
    row_ids = lax.broadcasted_iota(jnp.int32, (height, breadth), 0)
    col_ids = lax.broadcasted_iota(jnp.int32, (height, breadth), 1)
    angle = (row_ids * col_ids % period).astype(jnp.float32) * (2.0 * math.pi / period)
    return (jnp.cos(angle), jnp.sin(angle))


def spectrum_tables(length, inner):
    outer = 2 * length // inner
    cos_outer, sin_outer = phase_table(outer, length // inner, outer)
    cos_twist, sin_twist = phase_table(inner, outer, 2 * length)
    cos_inner, sin_inner = phase_table(inner, inner, inner)
    mixer = jnp.concatenate(
        [
            jnp.concatenate([cos_inner, sin_inner], axis=1),
            jnp.concatenate([-sin_inner, cos_inner], axis=1),
        ],
        axis=0,
    )
    return {
        "outer": jnp.concatenate([cos_outer, -sin_outer], axis=0),
        "twist": (cos_twist, sin_twist),
        "forward": mixer,
        "inverse": mixer,
    }


def forward_blocks(blocks, tables):
    count, chans, inner = blocks.shape
    outer = 2 * count
    one = jnp.einsum("kn,ncb->cbk", tables["outer"], blocks, precision=accuracy)
    real_one = one[:, :, :outer]
    imag_one = one[:, :, outer:]
    cos_twist, sin_twist = tables["twist"]
    real_two = real_one * cos_twist + imag_one * sin_twist
    imag_two = imag_one * cos_twist - real_one * sin_twist
    both = jnp.einsum(
        "jb,cbk->cjk",
        tables["forward"],
        jnp.concatenate([real_two, imag_two], axis=1),
        precision=accuracy,
    )
    return (both[:, :inner], both[:, inner:])


def inverse_blocks(real, imag, tables):
    chans, inner, outer = real.shape
    length = outer * inner // 2
    both = jnp.einsum(
        "jb,cjk->cbk", tables["inverse"], jnp.concatenate([real, imag], axis=1), precision=accuracy
    )
    real_one = both[:, :inner]
    imag_one = both[:, inner:]
    cos_twist, sin_twist = tables["twist"]
    real_two = real_one * cos_twist - imag_one * sin_twist
    imag_two = imag_one * cos_twist + real_one * sin_twist
    series = jnp.einsum(
        "kn,cbk->ncb",
        tables["outer"],
        jnp.concatenate([real_two, imag_two], axis=2),
        precision=accuracy,
    )
    return series / (2.0 * length)


def channel_conv(blocks, spectrum, bias_part, adjoint, tables):
    values = blocks.astype(jnp.float32)
    real, imag = forward_blocks(values, tables)
    filter_real, filter_imag = spectrum
    if adjoint:
        prod_real = real * filter_real + imag * filter_imag
        prod_imag = imag * filter_real - real * filter_imag
    else:
        prod_real = real * filter_real - imag * filter_imag
        prod_imag = real * filter_imag + imag * filter_real
    direct = bias_part[None, :, None] * values
    return (inverse_blocks(prod_real, prod_imag, tables) + direct).astype(jnp.bfloat16)


def exchange_kernel(x_ref, o_ref, landed, send_sems, recv_sems):
    count = x_ref.shape[0]
    me = lax.axis_index("seq")
    section = lax.axis_index("section")
    mesh_ids = pl.DeviceIdType.MESH
    barrier = pltpu.get_barrier_semaphore()

    def greet(k, _):
        peer = lax.rem(me + k, count)
        pl.semaphore_signal(barrier, inc=1, device_id=(peer, section), device_id_type=mesh_ids)
        return 0

    lax.fori_loop(1, count, greet, 0)
    pl.semaphore_wait(barrier, count - 1)

    def describe(k):
        peer = lax.rem(me + k, count)
        return pltpu.make_async_remote_copy(
            src_ref=x_ref.at[peer],
            dst_ref=landed.at[me],
            send_sem=send_sems.at[k],
            recv_sem=recv_sems.at[k],
            device_id=(peer, section),
            device_id_type=mesh_ids,
        )

    def send(k, _):
        describe(k).start()
        return 0

    def finish(k, _):
        describe(k).wait()
        return 0

    lax.fori_loop(1, count, send, 0)
    lax.fori_loop(1, count, finish, 0)
    o_ref[...] = landed[...]
    o_ref[pl.ds(me, 1)] = x_ref[pl.ds(me, 1)]


def seq_exchange(blocks):
    count = blocks.shape[0]
    return pl.pallas_call(
        exchange_kernel,
        out_shape=jax.ShapeDtypeStruct(blocks.shape, blocks.dtype),
        in_specs=[pl.BlockSpec(memory_space=pltpu.VMEM)],
        out_specs=pl.BlockSpec(memory_space=pltpu.VMEM),
        scratch_shapes=[
            pltpu.VMEM(blocks.shape, blocks.dtype),
            pltpu.SemaphoreType.DMA((count,)),
            pltpu.SemaphoreType.DMA((count,)),
        ],
        compiler_params=pltpu.CompilerParams(collective_id=0, has_side_effects=True),
    )(blocks)


def finish_kernel(
    sent_ref, d_out_ref, conv_ref, values_ref, keys_ref, grad_ref, taps_ref, weight_ref, top_ref,
    o_ref, next_ref, landed, extended, head, from_above, send_sems, recv_sems, rim_sems, hand_sems, acks,
):
    count = lax.axis_size("seq")
    rows, width = d_out_ref.shape
    chans = sent_ref.shape[0] // count
    me = lax.axis_index("seq")
    section = lax.axis_index("section")
    mesh_ids = pl.DeviceIdType.MESH
    barrier = pltpu.get_barrier_semaphore()

    def greet(k, _):
        peer = lax.rem(me + k, count)
        pl.semaphore_signal(barrier, inc=1, device_id=(peer, section), device_id_type=mesh_ids)
        return 0

    lax.fori_loop(1, count, greet, 0)
    sections = lax.axis_size("section")
    has_up = section < sections - 1
    has_down = section > 0
    up = (me, jnp.minimum(section + 1, sections - 1))
    down = (me, jnp.maximum(section - 1, 0))
    neighbours = has_up.astype(jnp.int32) + has_down.astype(jnp.int32)

    @pl.when(has_up)
    def _():
        pl.semaphore_signal(barrier, inc=1, device_id=up, device_id_type=mesh_ids)

    @pl.when(has_down)
    def _():
        pl.semaphore_signal(barrier, inc=1, device_id=down, device_id_type=mesh_ids)

    pl.semaphore_wait(barrier, count - 1 + neighbours)

    @pl.when(has_up)
    def _():
        pl.semaphore_signal(acks, inc=1, device_id=up, device_id_type=mesh_ids)

    @pl.when(has_down)
    def _():
        pl.semaphore_signal(acks, inc=1, device_id=down, device_id_type=mesh_ids)

    def describe(k):
        peer = lax.rem(me + k, count)
        return pltpu.make_async_remote_copy(
            src_ref=sent_ref.at[pl.ds(pl.multiple_of(peer * chans, 8), chans)],
            dst_ref=landed.at[pl.ds(pl.multiple_of(me * chans, 8), chans)],
            send_sem=send_sems.at[k],
            recv_sem=recv_sems.at[k],
            device_id=(peer, section),
            device_id_type=mesh_ids,
        )

    def send(k, _):
        describe(k).start()
        return 0

    def finish(k, _):
        describe(k).wait()
        return 0

    lax.fori_loop(1, count, send, 0)
    own = pl.ds(pl.multiple_of(me * chans, 8), chans)
    landed[own] = sent_ref[own]
    lax.fori_loop(1, count, finish, 0)

    d_prod = landed[...].T
    d_mixed = jnp.concatenate(
        [
            (d_out_ref[...] * conv_ref[...]).astype(jnp.bfloat16),
            (d_prod * values_ref[...]).astype(jnp.bfloat16),
            (d_prod * keys_ref[...]).astype(jnp.bfloat16),
        ],
        axis=1,
    ).astype(jnp.float32)
    head[...] = d_mixed[:8]
    rim = pltpu.make_async_remote_copy(
        src_ref=head,
        dst_ref=extended.at[pl.ds(rows, 8)],
        send_sem=rim_sems.at[0],
        recv_sem=rim_sems.at[1],
        device_id=(jnp.maximum(me - 1, 0), section),
        device_id_type=mesh_ids,
    )

    @pl.when(me > 0)
    def _():
        rim.start()

    extended[pl.ds(0, rows)] = d_mixed

    @pl.when(me == count - 1)
    def _():
        extended[pl.ds(rows, 8)] = jnp.zeros((8, extended.shape[1]), jnp.float32)

    @pl.when(me < count - 1)
    def _():
        rim.wait_recv()

    taps = taps_ref[...]
    d_proj = (
        taps[0:1] * extended[pl.ds(0, rows)]
        + taps[1:2] * extended[pl.ds(1, rows)]
        + taps[2:3] * extended[pl.ds(2, rows)]
    ).astype(jnp.bfloat16)
    total = grad_ref[...].astype(jnp.float32) + lax.dot_general(
        d_proj, weight_ref[...], (((1,), (1,)), ((), ())), preferred_element_type=jnp.float32
    )
    o_ref[...] = total.astype(o_ref.dtype)
    hand = pltpu.make_async_remote_copy(
        src_ref=o_ref,
        dst_ref=from_above,
        send_sem=hand_sems.at[0],
        recv_sem=hand_sems.at[1],
        device_id=down,
        device_id_type=mesh_ids,
    )

    @pl.when(has_down)
    def _():
        hand.start()

    @pl.when(me > 0)
    def _():
        rim.wait_send()

    @pl.when(has_up)
    def _():
        hand.wait_recv()
        next_ref[...] = from_above[...]

    @pl.when(jnp.logical_not(has_up))
    def _():
        next_ref[...] = top_ref[...]

    @pl.when(has_down)
    def _():
        hand.wait_send()

    pl.semaphore_wait(acks, neighbours)


def exchange_and_finish(sent, d_out, conv_wide, values, keys, grad_out, taps, weight_in, top):
    count = lax.axis_size("seq")
    rows, width = d_out.shape
    vmem = pl.BlockSpec(memory_space=pltpu.VMEM)
    return pl.pallas_call(
        finish_kernel,
        out_shape=(
            jax.ShapeDtypeStruct(grad_out.shape, grad_out.dtype),
            jax.ShapeDtypeStruct(grad_out.shape, grad_out.dtype),
        ),
        in_specs=[vmem] * 9,
        out_specs=(vmem, vmem),
        scratch_shapes=[
            pltpu.VMEM(sent.shape, jnp.float32),
            pltpu.VMEM((rows + 8, taps.shape[1]), jnp.float32),
            pltpu.VMEM((8, taps.shape[1]), jnp.float32),
            pltpu.VMEM(grad_out.shape, grad_out.dtype),
            pltpu.SemaphoreType.DMA((count,)),
            pltpu.SemaphoreType.DMA((count,)),
            pltpu.SemaphoreType.DMA((2,)),
            pltpu.SemaphoreType.DMA((2,)),
            pltpu.SemaphoreType.REGULAR,
        ],
        compiler_params=pltpu.CompilerParams(collective_id=1, has_side_effects=True),
    )(sent, d_out, conv_wide, values, keys, grad_out, taps, weight_in, top)


def when(active, action, *operands):

    def skipped(*inputs):
        return jax.tree.map(jnp.zeros_like, action(*inputs))

    return lax.cond(active, action, skipped, *operands)


def shards(cotangent, projected, w_in, w_out, short_filter, long_filter, filter_bias):
    seq_count = lax.axis_size("seq")
    seq_place = lax.axis_index("seq")
    section_count = lax.axis_size("section")
    section_place = lax.axis_index("section")
    micro = projected.shape[1]
    height = projected.shape[2]
    width = w_out.shape[2]
    length = height * seq_count
    tables = spectrum_tables(length, height)
    chans = width // seq_count
    bias_part = lax.dynamic_slice_in_dim(filter_bias[0], seq_place * chans, chans, 0)
    weight_in = w_in[0]
    weight_out = w_out[0]
    taps = short_filter[0]
    contract = (((1,), (1,)), ((), ()))

    held = {}

    def causal(blocks):
        return channel_conv(blocks, held["spectrum"], bias_part, False, tables)

    def adjoint(blocks):
        return channel_conv(blocks, held["spectrum"], bias_part, True, tables)

    def to_blocks(series):
        return series.reshape(seq_count, height, chans).transpose(0, 2, 1)

    forward = []
    for slot in range(micro):
        proj = projected[0, slot]
        rim = shifted(proj[height - 2 :], "seq", 1)
        padded = jnp.concatenate([rim, proj], axis=0).astype(jnp.float32)
        mixed = taps[0] * padded[2:] + taps[1] * padded[1:-1] + taps[2] * padded[:-2]
        query = mixed[:, :width]
        keys = mixed[:, width : 2 * width]
        values = mixed[:, 2 * width :]
        product = (keys * values).astype(jnp.bfloat16)
        if slot == 0:
            both = jnp.stack([long_filter[0].astype(jnp.bfloat16), product])
            both = lax.all_to_all(both, "seq", split_axis=2, concat_axis=1, tiled=True)
            held["spectrum"] = forward_blocks(to_blocks(both[0].astype(jnp.float32)), tables)
            product_local = both[1]
        else:
            product_local = lax.all_to_all(product, "seq", split_axis=1, concat_axis=0, tiled=True)
        conv_local = causal(to_blocks(product_local)).transpose(0, 2, 1).reshape(length, chans)
        conv = lax.all_to_all(conv_local, "seq", split_axis=0, concat_axis=1, tiled=True)
        forward.append((query, keys, values, conv.astype(jnp.float32)))

    def stage(grad_out, top, slot):
        query, keys, values, conv_wide = forward[slot]
        d_out = lax.dot_general(grad_out, weight_out, contract, preferred_element_type=jnp.float32)
        d_conv = (d_out * query).astype(jnp.bfloat16)
        sent = seq_exchange(d_conv.reshape(height, seq_count, chans).transpose(1, 2, 0))
        d_prod_blocks = adjoint(sent)
        sent_back = d_prod_blocks.reshape(seq_count * chans, height).astype(jnp.float32)
        return exchange_and_finish(
            sent_back, d_out, conv_wide, values, keys, grad_out, taps, weight_in, top
        )

    def tick(step, carry):
        incoming, grads = carry
        index = step - (section_count - 1 - section_place)
        active = (index >= 0) & (index < micro)
        slot = jnp.clip(index, 0, micro - 1)
        later = jnp.clip(index + 1, 0, micro - 1)
        top = lax.dynamic_index_in_dim(cotangent, later, 0, keepdims=False)
        if micro == 1:
            d_input, incoming = stage(incoming, top, 0)
        else:
            d_input, incoming = lax.switch(
                slot, [functools.partial(stage, slot=m) for m in range(micro)], incoming, top
            )
        grads = jnp.where(active, lax.dynamic_update_index_in_dim(grads, d_input, slot, 0), grads)
        return (incoming, grads)

    start = (
        cotangent[0],
        jnp.zeros((micro, height, width), jnp.bfloat16),
    )
    incoming, grads = lax.fori_loop(0, micro + section_count - 1, tick, start)
    return grads[None]


def solution(mesh):
    return jax.shard_map(
        shards,
        mesh=mesh,
        in_specs=(
            P(None, "seq", None),
            P("section", None, "seq", None),
            P("section", None, None),
            P("section", None, None),
            P("section", None, None),
            P("section", "seq", None),
            P("section", None),
        ),
        out_specs=P("section", None, "seq", None),
        check_vma=False,
    )
```

```python
import functools
import math

import jax
import jax.numpy as jnp
from jax import lax
from jax.experimental import pallas as pl
from jax.experimental.pallas import tpu as pltpu
from jax.sharding import PartitionSpec as P

accuracy = lax.Precision.HIGH


def shifted(value, axis, by):
    count = lax.axis_size(axis)
    pairs = [(i, i + by) for i in range(count) if 0 <= i + by < count]
    return lax.ppermute(value, axis, pairs)


def phase_table(height, breadth, period):
    row_ids = lax.broadcasted_iota(jnp.int32, (height, breadth), 0)
    col_ids = lax.broadcasted_iota(jnp.int32, (height, breadth), 1)
    angle = (row_ids * col_ids % period).astype(jnp.float32) * (2.0 * math.pi / period)
    return (jnp.cos(angle), jnp.sin(angle))


def spectrum_tables(length, inner):
    outer = 2 * length // inner
    cos_outer, sin_outer = phase_table(outer, length // inner, outer)
    cos_twist, sin_twist = phase_table(inner, outer, 2 * length)
    cos_inner, sin_inner = phase_table(inner, inner, inner)
    mixer = jnp.concatenate(
        [
            jnp.concatenate([cos_inner, sin_inner], axis=1),
            jnp.concatenate([-sin_inner, cos_inner], axis=1),
        ],
        axis=0,
    )
    return {
        "outer": jnp.concatenate([cos_outer, -sin_outer], axis=0),
        "twist": (cos_twist, sin_twist),
        "forward": mixer,
        "inverse": mixer,
    }


def forward_blocks(blocks, tables):
    count, chans, inner = blocks.shape
    outer = 2 * count
    one = jnp.einsum("kn,ncb->cbk", tables["outer"], blocks, precision=accuracy)
    real_one = one[:, :, :outer]
    imag_one = one[:, :, outer:]
    cos_twist, sin_twist = tables["twist"]
    real_two = real_one * cos_twist + imag_one * sin_twist
    imag_two = imag_one * cos_twist - real_one * sin_twist
    both = jnp.einsum(
        "jb,cbk->cjk",
        tables["forward"],
        jnp.concatenate([real_two, imag_two], axis=1),
        precision=accuracy,
    )
    return (both[:, :inner], both[:, inner:])


def inverse_blocks(real, imag, tables):
    chans, inner, outer = real.shape
    length = outer * inner // 2
    both = jnp.einsum(
        "jb,cjk->cbk", tables["inverse"], jnp.concatenate([real, imag], axis=1), precision=accuracy
    )
    real_one = both[:, :inner]
    imag_one = both[:, inner:]
    cos_twist, sin_twist = tables["twist"]
    real_two = real_one * cos_twist - imag_one * sin_twist
    imag_two = imag_one * cos_twist + real_one * sin_twist
    series = jnp.einsum(
        "kn,cbk->ncb",
        tables["outer"],
        jnp.concatenate([real_two, imag_two], axis=2),
        precision=accuracy,
    )
    return series / (2.0 * length)


def channel_conv(blocks, spectrum, bias_part, adjoint, tables):
    values = blocks.astype(jnp.float32)
    real, imag = forward_blocks(values, tables)
    filter_real, filter_imag = spectrum
    if adjoint:
        prod_real = real * filter_real + imag * filter_imag
        prod_imag = imag * filter_real - real * filter_imag
    else:
        prod_real = real * filter_real - imag * filter_imag
        prod_imag = real * filter_imag + imag * filter_real
    direct = bias_part[None, :, None] * values
    return (inverse_blocks(prod_real, prod_imag, tables) + direct).astype(jnp.bfloat16)


def begin_kernel(grad_ref, weight_ref, query_ref, d_out_ref, o_ref, outgoing, landed, send_sems, recv_sems):
    count = lax.axis_size("seq")
    chans = o_ref.shape[0] // count
    me = lax.axis_index("seq")
    section = lax.axis_index("section")
    mesh_ids = pl.DeviceIdType.MESH
    barrier = pltpu.get_barrier_semaphore()

    def greet(k, _):
        peer = lax.rem(me + k, count)
        pl.semaphore_signal(barrier, inc=1, device_id=(peer, section), device_id_type=mesh_ids)
        return 0

    lax.fori_loop(1, count, greet, 0)
    d_out = lax.dot_general(
        grad_ref[...], weight_ref[...], (((1,), (1,)), ((), ())), preferred_element_type=jnp.float32
    )
    d_out_ref[...] = d_out
    d_conv = (d_out * query_ref[...]).astype(jnp.bfloat16).astype(jnp.float32)
    outgoing[...] = d_conv.T
    pl.semaphore_wait(barrier, count - 1)

    def describe(k):
        peer = lax.rem(me + k, count)
        return pltpu.make_async_remote_copy(
            src_ref=outgoing.at[pl.ds(pl.multiple_of(peer * chans, 8), chans)],
            dst_ref=landed.at[pl.ds(pl.multiple_of(me * chans, 8), chans)],
            send_sem=send_sems.at[k],
            recv_sem=recv_sems.at[k],
            device_id=(peer, section),
            device_id_type=mesh_ids,
        )

    def send(k, _):
        describe(k).start()
        return 0

    def finish(k, _):
        describe(k).wait()
        return 0

    lax.fori_loop(1, count, send, 0)
    own = pl.ds(pl.multiple_of(me * chans, 8), chans)
    landed[own] = outgoing[own]
    lax.fori_loop(1, count, finish, 0)
    o_ref[...] = landed[...]


def project_and_exchange(grad_out, weight_out, query):
    count = lax.axis_size("seq")
    rows, width = query.shape
    vmem = pl.BlockSpec(memory_space=pltpu.VMEM)
    block = (width, rows)
    return pl.pallas_call(
        begin_kernel,
        out_shape=(
            jax.ShapeDtypeStruct((rows, width), jnp.float32),
            jax.ShapeDtypeStruct(block, jnp.float32),
        ),
        in_specs=[vmem] * 3,
        out_specs=(vmem, vmem),
        scratch_shapes=[
            pltpu.VMEM(block, jnp.float32),
            pltpu.VMEM(block, jnp.float32),
            pltpu.SemaphoreType.DMA((count,)),
            pltpu.SemaphoreType.DMA((count,)),
        ],
        compiler_params=pltpu.CompilerParams(collective_id=0, has_side_effects=True),
    )(grad_out, weight_out, query)


def finish_kernel(
    sent_ref, d_out_ref, conv_ref, values_ref, keys_ref, grad_ref, taps_ref, weight_ref, top_ref,
    o_ref, next_ref, landed, extended, head, from_above, send_sems, recv_sems, rim_sems, hand_sems, acks,
):
    count = lax.axis_size("seq")
    rows, width = d_out_ref.shape
    chans = sent_ref.shape[0] // count
    me = lax.axis_index("seq")
    section = lax.axis_index("section")
    mesh_ids = pl.DeviceIdType.MESH
    barrier = pltpu.get_barrier_semaphore()

    def greet(k, _):
        peer = lax.rem(me + k, count)
        pl.semaphore_signal(barrier, inc=1, device_id=(peer, section), device_id_type=mesh_ids)
        return 0

    lax.fori_loop(1, count, greet, 0)
    sections = lax.axis_size("section")
    has_up = section < sections - 1
    has_down = section > 0
    up = (me, jnp.minimum(section + 1, sections - 1))
    down = (me, jnp.maximum(section - 1, 0))
    neighbours = has_up.astype(jnp.int32) + has_down.astype(jnp.int32)

    @pl.when(has_up)
    def _():
        pl.semaphore_signal(barrier, inc=1, device_id=up, device_id_type=mesh_ids)

    @pl.when(has_down)
    def _():
        pl.semaphore_signal(barrier, inc=1, device_id=down, device_id_type=mesh_ids)

    pl.semaphore_wait(barrier, count - 1 + neighbours)

    @pl.when(has_up)
    def _():
        pl.semaphore_signal(acks, inc=1, device_id=up, device_id_type=mesh_ids)

    @pl.when(has_down)
    def _():
        pl.semaphore_signal(acks, inc=1, device_id=down, device_id_type=mesh_ids)

    def describe(k):
        peer = lax.rem(me + k, count)
        return pltpu.make_async_remote_copy(
            src_ref=sent_ref.at[pl.ds(pl.multiple_of(peer * chans, 8), chans)],
            dst_ref=landed.at[pl.ds(pl.multiple_of(me * chans, 8), chans)],
            send_sem=send_sems.at[k],
            recv_sem=recv_sems.at[k],
            device_id=(peer, section),
            device_id_type=mesh_ids,
        )

    def send(k, _):
        describe(k).start()
        return 0

    def finish(k, _):
        describe(k).wait()
        return 0

    lax.fori_loop(1, count, send, 0)
    own = pl.ds(pl.multiple_of(me * chans, 8), chans)
    landed[own] = sent_ref[own]
    lax.fori_loop(1, count, finish, 0)

    d_prod = landed[...].T
    d_mixed = jnp.concatenate(
        [
            (d_out_ref[...] * conv_ref[...]).astype(jnp.bfloat16),
            (d_prod * values_ref[...]).astype(jnp.bfloat16),
            (d_prod * keys_ref[...]).astype(jnp.bfloat16),
        ],
        axis=1,
    ).astype(jnp.float32)
    head[...] = d_mixed[:8]
    rim = pltpu.make_async_remote_copy(
        src_ref=head,
        dst_ref=extended.at[pl.ds(rows, 8)],
        send_sem=rim_sems.at[0],
        recv_sem=rim_sems.at[1],
        device_id=(jnp.maximum(me - 1, 0), section),
        device_id_type=mesh_ids,
    )

    @pl.when(me > 0)
    def _():
        rim.start()

    extended[pl.ds(0, rows)] = d_mixed

    @pl.when(me == count - 1)
    def _():
        extended[pl.ds(rows, 8)] = jnp.zeros((8, extended.shape[1]), jnp.float32)

    @pl.when(me < count - 1)
    def _():
        rim.wait_recv()

    taps = taps_ref[...]
    d_proj = (
        taps[0:1] * extended[pl.ds(0, rows)]
        + taps[1:2] * extended[pl.ds(1, rows)]
        + taps[2:3] * extended[pl.ds(2, rows)]
    ).astype(jnp.bfloat16)
    total = grad_ref[...].astype(jnp.float32) + lax.dot_general(
        d_proj, weight_ref[...], (((1,), (1,)), ((), ())), preferred_element_type=jnp.float32
    )
    o_ref[...] = total.astype(o_ref.dtype)
    hand = pltpu.make_async_remote_copy(
        src_ref=o_ref,
        dst_ref=from_above,
        send_sem=hand_sems.at[0],
        recv_sem=hand_sems.at[1],
        device_id=down,
        device_id_type=mesh_ids,
    )

    @pl.when(has_down)
    def _():
        hand.start()

    @pl.when(me > 0)
    def _():
        rim.wait_send()

    @pl.when(has_up)
    def _():
        hand.wait_recv()
        next_ref[...] = from_above[...]

    @pl.when(jnp.logical_not(has_up))
    def _():
        next_ref[...] = top_ref[...]

    @pl.when(has_down)
    def _():
        hand.wait_send()

    pl.semaphore_wait(acks, neighbours)


def exchange_and_finish(sent, d_out, conv_wide, values, keys, grad_out, taps, weight_in, top):
    count = lax.axis_size("seq")
    rows, width = d_out.shape
    vmem = pl.BlockSpec(memory_space=pltpu.VMEM)
    return pl.pallas_call(
        finish_kernel,
        out_shape=(
            jax.ShapeDtypeStruct(grad_out.shape, grad_out.dtype),
            jax.ShapeDtypeStruct(grad_out.shape, grad_out.dtype),
        ),
        in_specs=[vmem] * 9,
        out_specs=(vmem, vmem),
        scratch_shapes=[
            pltpu.VMEM(sent.shape, jnp.float32),
            pltpu.VMEM((rows + 8, taps.shape[1]), jnp.float32),
            pltpu.VMEM((8, taps.shape[1]), jnp.float32),
            pltpu.VMEM(grad_out.shape, grad_out.dtype),
            pltpu.SemaphoreType.DMA((count,)),
            pltpu.SemaphoreType.DMA((count,)),
            pltpu.SemaphoreType.DMA((2,)),
            pltpu.SemaphoreType.DMA((2,)),
            pltpu.SemaphoreType.REGULAR,
        ],
        compiler_params=pltpu.CompilerParams(collective_id=1, has_side_effects=True),
    )(sent, d_out, conv_wide, values, keys, grad_out, taps, weight_in, top)


def when(active, action, *operands):

    def skipped(*inputs):
        return jax.tree.map(jnp.zeros_like, action(*inputs))

    return lax.cond(active, action, skipped, *operands)


def shards(cotangent, projected, w_in, w_out, short_filter, long_filter, filter_bias):
    seq_count = lax.axis_size("seq")
    seq_place = lax.axis_index("seq")
    section_count = lax.axis_size("section")
    section_place = lax.axis_index("section")
    micro = projected.shape[1]
    height = projected.shape[2]
    width = w_out.shape[2]
    length = height * seq_count
    tables = spectrum_tables(length, height)
    chans = width // seq_count
    bias_part = lax.dynamic_slice_in_dim(filter_bias[0], seq_place * chans, chans, 0)
    weight_in = w_in[0]
    weight_out = w_out[0]
    taps = short_filter[0]
    contract = (((1,), (1,)), ((), ()))

    held = {}

    def causal(blocks):
        return channel_conv(blocks, held["spectrum"], bias_part, False, tables)

    def adjoint(blocks):
        return channel_conv(blocks, held["spectrum"], bias_part, True, tables)

    def to_blocks(series):
        return series.reshape(seq_count, height, chans).transpose(0, 2, 1)

    forward = []
    for slot in range(micro):
        proj = projected[0, slot]
        rim = shifted(proj[height - 2 :], "seq", 1)
        padded = jnp.concatenate([rim, proj], axis=0).astype(jnp.float32)
        mixed = taps[0] * padded[2:] + taps[1] * padded[1:-1] + taps[2] * padded[:-2]
        query = mixed[:, :width]
        keys = mixed[:, width : 2 * width]
        values = mixed[:, 2 * width :]
        product = (keys * values).astype(jnp.bfloat16)
        if slot == 0:
            both = jnp.stack([long_filter[0].astype(jnp.bfloat16), product])
            both = lax.all_to_all(both, "seq", split_axis=2, concat_axis=1, tiled=True)
            held["spectrum"] = forward_blocks(to_blocks(both[0].astype(jnp.float32)), tables)
            product_local = both[1]
        else:
            product_local = lax.all_to_all(product, "seq", split_axis=1, concat_axis=0, tiled=True)
        conv_local = causal(to_blocks(product_local)).transpose(0, 2, 1).reshape(length, chans)
        conv = lax.all_to_all(conv_local, "seq", split_axis=0, concat_axis=1, tiled=True)
        forward.append((query, keys, values, conv.astype(jnp.float32)))

    def stage(grad_out, top, slot):
        query, keys, values, conv_wide = forward[slot]
        d_out, sent = project_and_exchange(grad_out, weight_out, query)
        sent = sent.reshape(seq_count, chans, height)
        d_prod_blocks = adjoint(sent)
        sent_back = d_prod_blocks.reshape(seq_count * chans, height).astype(jnp.float32)
        return exchange_and_finish(
            sent_back, d_out, conv_wide, values, keys, grad_out, taps, weight_in, top
        )

    def tick(step, carry):
        incoming, grads = carry
        index = step - (section_count - 1 - section_place)
        active = (index >= 0) & (index < micro)
        slot = jnp.clip(index, 0, micro - 1)
        later = jnp.clip(index + 1, 0, micro - 1)
        top = lax.dynamic_index_in_dim(cotangent, later, 0, keepdims=False)
        if micro == 1:
            d_input, incoming = stage(incoming, top, 0)
        else:
            d_input, incoming = lax.switch(
                slot, [functools.partial(stage, slot=m) for m in range(micro)], incoming, top
            )
        grads = jnp.where(active, lax.dynamic_update_index_in_dim(grads, d_input, slot, 0), grads)
        return (incoming, grads)

    start = (
        cotangent[0],
        jnp.zeros((micro, height, width), jnp.bfloat16),
    )
    incoming, grads = lax.fori_loop(0, micro + section_count - 1, tick, start)
    return grads[None]


def solution(mesh):
    return jax.shard_map(
        shards,
        mesh=mesh,
        in_specs=(
            P(None, "seq", None),
            P("section", None, "seq", None),
            P("section", None, None),
            P("section", None, None),
            P("section", None, None),
            P("section", "seq", None),
            P("section", None),
        ),
        out_specs=P("section", None, "seq", None),
        check_vma=False,
    )
```

```python
import functools
import math

import jax
import jax.numpy as jnp
from jax import lax
from jax.experimental import pallas as pl
from jax.experimental.pallas import tpu as pltpu
from jax.sharding import PartitionSpec as P

accuracy = lax.Precision.HIGH


def shifted(value, axis, by):
    count = lax.axis_size(axis)
    pairs = [(i, i + by) for i in range(count) if 0 <= i + by < count]
    return lax.ppermute(value, axis, pairs)


def phase_table(height, breadth, period):
    row_ids = lax.broadcasted_iota(jnp.int32, (height, breadth), 0)
    col_ids = lax.broadcasted_iota(jnp.int32, (height, breadth), 1)
    angle = (row_ids * col_ids % period).astype(jnp.float32) * (2.0 * math.pi / period)
    return (jnp.cos(angle), jnp.sin(angle))


def spectrum_tables(length, inner):
    outer = 2 * length // inner
    cos_outer, sin_outer = phase_table(outer, length // inner, outer)
    cos_twist, sin_twist = phase_table(inner, outer, 2 * length)
    cos_inner, sin_inner = phase_table(inner, inner, inner)
    mixer = jnp.concatenate(
        [
            jnp.concatenate([cos_inner, sin_inner], axis=1),
            jnp.concatenate([-sin_inner, cos_inner], axis=1),
        ],
        axis=0,
    )
    return {
        "outer": jnp.concatenate([cos_outer, -sin_outer], axis=0),
        "twist": (cos_twist, sin_twist),
        "forward": mixer,
        "inverse": mixer,
    }


def forward_blocks(blocks, tables):
    count, chans, inner = blocks.shape
    outer = 2 * count
    one = jnp.einsum("kn,ncb->cbk", tables["outer"], blocks, precision=accuracy)
    real_one = one[:, :, :outer]
    imag_one = one[:, :, outer:]
    cos_twist, sin_twist = tables["twist"]
    real_two = real_one * cos_twist + imag_one * sin_twist
    imag_two = imag_one * cos_twist - real_one * sin_twist
    both = jnp.einsum(
        "jb,cbk->cjk",
        tables["forward"],
        jnp.concatenate([real_two, imag_two], axis=1),
        precision=accuracy,
    )
    return (both[:, :inner], both[:, inner:])


def inverse_blocks(real, imag, tables):
    chans, inner, outer = real.shape
    length = outer * inner // 2
    both = jnp.einsum(
        "jb,cjk->cbk", tables["inverse"], jnp.concatenate([real, imag], axis=1), precision=accuracy
    )
    real_one = both[:, :inner]
    imag_one = both[:, inner:]
    cos_twist, sin_twist = tables["twist"]
    real_two = real_one * cos_twist - imag_one * sin_twist
    imag_two = imag_one * cos_twist + real_one * sin_twist
    series = jnp.einsum(
        "kn,cbk->ncb",
        tables["outer"],
        jnp.concatenate([real_two, imag_two], axis=2),
        precision=accuracy,
    )
    return series / (2.0 * length)


def channel_conv(blocks, spectrum, bias_part, adjoint, tables):
    values = blocks.astype(jnp.float32)
    real, imag = forward_blocks(values, tables)
    filter_real, filter_imag = spectrum
    if adjoint:
        prod_real = real * filter_real + imag * filter_imag
        prod_imag = imag * filter_real - real * filter_imag
    else:
        prod_real = real * filter_real - imag * filter_imag
        prod_imag = real * filter_imag + imag * filter_real
    direct = bias_part[None, :, None] * values
    return (inverse_blocks(prod_real, prod_imag, tables) + direct).astype(jnp.bfloat16)


def begin_kernel(grad_ref, weight_ref, query_ref, d_out_ref, o_ref, outgoing, landed, send_sems, recv_sems):
    count = lax.axis_size("seq")
    chans = o_ref.shape[0] // count
    me = lax.axis_index("seq")
    section = lax.axis_index("section")
    mesh_ids = pl.DeviceIdType.MESH
    barrier = pltpu.get_barrier_semaphore()

    def greet(k, _):
        peer = lax.rem(me + k, count)
        pl.semaphore_signal(barrier, inc=1, device_id=(peer, section), device_id_type=mesh_ids)
        return 0

    lax.fori_loop(1, count, greet, 0)
    d_out = lax.dot_general(
        grad_ref[...], weight_ref[...], (((1,), (1,)), ((), ())), preferred_element_type=jnp.float32
    )
    d_out_ref[...] = d_out
    d_conv = (d_out * query_ref[...]).astype(jnp.bfloat16).astype(jnp.float32)
    outgoing[...] = d_conv.T
    pl.semaphore_wait(barrier, count - 1)

    def describe(k):
        peer = lax.rem(me + k, count)
        return pltpu.make_async_remote_copy(
            src_ref=outgoing.at[pl.ds(pl.multiple_of(peer * chans, 8), chans)],
            dst_ref=landed.at[pl.ds(pl.multiple_of(me * chans, 8), chans)],
            send_sem=send_sems.at[k],
            recv_sem=recv_sems.at[k],
            device_id=(peer, section),
            device_id_type=mesh_ids,
        )

    def send(k, _):
        describe(k).start()
        return 0

    def finish(k, _):
        describe(k).wait()
        return 0

    lax.fori_loop(1, count, send, 0)
    own = pl.ds(pl.multiple_of(me * chans, 8), chans)
    landed[own] = outgoing[own]
    lax.fori_loop(1, count, finish, 0)
    o_ref[...] = landed[...]


def project_and_exchange(grad_out, weight_out, query):
    count = lax.axis_size("seq")
    rows, width = query.shape
    vmem = pl.BlockSpec(memory_space=pltpu.VMEM)
    block = (width, rows)
    return pl.pallas_call(
        begin_kernel,
        out_shape=(
            jax.ShapeDtypeStruct((rows, width), jnp.float32),
            jax.ShapeDtypeStruct(block, jnp.float32),
        ),
        in_specs=[vmem] * 3,
        out_specs=(vmem, vmem),
        scratch_shapes=[
            pltpu.VMEM(block, jnp.float32),
            pltpu.VMEM(block, jnp.float32),
            pltpu.SemaphoreType.DMA((count,)),
            pltpu.SemaphoreType.DMA((count,)),
        ],
        compiler_params=pltpu.CompilerParams(collective_id=0, has_side_effects=True),
    )(grad_out, weight_out, query)


def finish_kernel(
    sent_ref, d_out_ref, conv_ref, values_ref, keys_ref, grad_ref, taps_ref, weight_ref, top_ref,
    o_ref, next_ref, landed, extended, head, from_above, send_sems, recv_sems, rim_sems, hand_sems, acks,
):
    count = lax.axis_size("seq")
    rows, width = d_out_ref.shape
    chans = sent_ref.shape[0] // count
    me = lax.axis_index("seq")
    section = lax.axis_index("section")
    mesh_ids = pl.DeviceIdType.MESH
    barrier = pltpu.get_barrier_semaphore()

    def greet(k, _):
        peer = lax.rem(me + k, count)
        pl.semaphore_signal(barrier, inc=1, device_id=(peer, section), device_id_type=mesh_ids)
        return 0

    lax.fori_loop(1, count, greet, 0)
    sections = lax.axis_size("section")
    has_up = section < sections - 1
    has_down = section > 0
    up = (me, jnp.minimum(section + 1, sections - 1))
    down = (me, jnp.maximum(section - 1, 0))
    neighbours = has_up.astype(jnp.int32) + has_down.astype(jnp.int32)

    @pl.when(has_up)
    def _():
        pl.semaphore_signal(barrier, inc=1, device_id=up, device_id_type=mesh_ids)

    @pl.when(has_down)
    def _():
        pl.semaphore_signal(barrier, inc=1, device_id=down, device_id_type=mesh_ids)

    pl.semaphore_wait(barrier, count - 1 + neighbours)

    @pl.when(has_up)
    def _():
        pl.semaphore_signal(acks, inc=1, device_id=up, device_id_type=mesh_ids)

    @pl.when(has_down)
    def _():
        pl.semaphore_signal(acks, inc=1, device_id=down, device_id_type=mesh_ids)

    def describe(k):
        peer = lax.rem(me + k, count)
        return pltpu.make_async_remote_copy(
            src_ref=sent_ref.at[pl.ds(pl.multiple_of(peer * chans, 8), chans)],
            dst_ref=landed.at[pl.ds(pl.multiple_of(me * chans, 8), chans)],
            send_sem=send_sems.at[k],
            recv_sem=recv_sems.at[k],
            device_id=(peer, section),
            device_id_type=mesh_ids,
        )

    def send(k, _):
        describe(k).start()
        return 0

    def finish(k, _):
        describe(k).wait()
        return 0

    lax.fori_loop(1, count, send, 0)
    own = pl.ds(pl.multiple_of(me * chans, 8), chans)
    landed[own] = sent_ref[own]
    lax.fori_loop(1, count, finish, 0)

    d_prod = landed[...].T
    d_mixed = jnp.concatenate(
        [
            (d_out_ref[...] * conv_ref[...]).astype(jnp.bfloat16),
            (d_prod * values_ref[...]).astype(jnp.bfloat16),
            (d_prod * keys_ref[...]).astype(jnp.bfloat16),
        ],
        axis=1,
    ).astype(jnp.float32)
    head[...] = d_mixed[:8]
    rim = pltpu.make_async_remote_copy(
        src_ref=head,
        dst_ref=extended.at[pl.ds(rows, 8)],
        send_sem=rim_sems.at[0],
        recv_sem=rim_sems.at[1],
        device_id=(jnp.maximum(me - 1, 0), section),
        device_id_type=mesh_ids,
    )

    @pl.when(me > 0)
    def _():
        rim.start()

    extended[pl.ds(0, rows)] = d_mixed

    @pl.when(me == count - 1)
    def _():
        extended[pl.ds(rows, 8)] = jnp.zeros((8, extended.shape[1]), jnp.float32)

    @pl.when(me < count - 1)
    def _():
        rim.wait_recv()

    taps = taps_ref[...]
    d_proj = (
        taps[0:1] * extended[pl.ds(0, rows)]
        + taps[1:2] * extended[pl.ds(1, rows)]
        + taps[2:3] * extended[pl.ds(2, rows)]
    ).astype(jnp.bfloat16)
    total = grad_ref[...].astype(jnp.float32) + lax.dot_general(
        d_proj, weight_ref[...], (((1,), (1,)), ((), ())), preferred_element_type=jnp.float32
    )
    o_ref[...] = total.astype(o_ref.dtype)
    hand = pltpu.make_async_remote_copy(
        src_ref=o_ref,
        dst_ref=from_above,
        send_sem=hand_sems.at[0],
        recv_sem=hand_sems.at[1],
        device_id=down,
        device_id_type=mesh_ids,
    )

    @pl.when(has_down)
    def _():
        hand.start()

    @pl.when(me > 0)
    def _():
        rim.wait_send()

    @pl.when(has_up)
    def _():
        hand.wait_recv()
        next_ref[...] = from_above[...]

    @pl.when(jnp.logical_not(has_up))
    def _():
        next_ref[...] = top_ref[...]

    @pl.when(has_down)
    def _():
        hand.wait_send()

    pl.semaphore_wait(acks, neighbours)


def exchange_and_finish(sent, d_out, conv_wide, values, keys, grad_out, taps, weight_in, top):
    count = lax.axis_size("seq")
    rows, width = d_out.shape
    vmem = pl.BlockSpec(memory_space=pltpu.VMEM)
    return pl.pallas_call(
        finish_kernel,
        out_shape=(
            jax.ShapeDtypeStruct(grad_out.shape, grad_out.dtype),
            jax.ShapeDtypeStruct(grad_out.shape, grad_out.dtype),
        ),
        in_specs=[vmem] * 9,
        out_specs=(vmem, vmem),
        scratch_shapes=[
            pltpu.VMEM(sent.shape, jnp.float32),
            pltpu.VMEM((rows + 8, taps.shape[1]), jnp.float32),
            pltpu.VMEM((8, taps.shape[1]), jnp.float32),
            pltpu.VMEM(grad_out.shape, grad_out.dtype),
            pltpu.SemaphoreType.DMA((count,)),
            pltpu.SemaphoreType.DMA((count,)),
            pltpu.SemaphoreType.DMA((2,)),
            pltpu.SemaphoreType.DMA((2,)),
            pltpu.SemaphoreType.REGULAR,
        ],
        compiler_params=pltpu.CompilerParams(collective_id=1, has_side_effects=True),
    )(sent, d_out, conv_wide, values, keys, grad_out, taps, weight_in, top)


def when(active, action, *operands):

    def skipped(*inputs):
        return jax.tree.map(jnp.zeros_like, action(*inputs))

    return lax.cond(active, action, skipped, *operands)


def shards(cotangent, projected, w_in, w_out, short_filter, long_filter, filter_bias):
    seq_count = lax.axis_size("seq")
    seq_place = lax.axis_index("seq")
    section_count = lax.axis_size("section")
    section_place = lax.axis_index("section")
    micro = projected.shape[1]
    height = projected.shape[2]
    width = w_out.shape[2]
    length = height * seq_count
    tables = spectrum_tables(length, height)
    chans = width // seq_count
    bias_part = lax.dynamic_slice_in_dim(filter_bias[0], seq_place * chans, chans, 0)
    weight_in = w_in[0]
    weight_out = w_out[0]
    taps = short_filter[0]
    contract = (((1,), (1,)), ((), ()))

    held = {}

    def causal(blocks):
        return channel_conv(blocks, held["spectrum"], bias_part, False, tables)

    def adjoint(blocks):
        return channel_conv(blocks, held["spectrum"], bias_part, True, tables)

    def to_blocks(series):
        return series.reshape(seq_count, height, chans).transpose(0, 2, 1)

    forward = []
    for slot in range(micro):
        proj = projected[0, slot]
        rim = shifted(proj[height - 2 :], "seq", 1)
        padded = jnp.concatenate([rim, proj], axis=0).astype(jnp.float32)
        mixed = taps[0] * padded[2:] + taps[1] * padded[1:-1] + taps[2] * padded[:-2]
        query = mixed[:, :width]
        keys = mixed[:, width : 2 * width]
        values = mixed[:, 2 * width :]
        product = (keys * values).astype(jnp.bfloat16)
        if slot == 0:
            both = jnp.stack([long_filter[0].astype(jnp.bfloat16), product])
            both = lax.all_to_all(both, "seq", split_axis=2, concat_axis=1, tiled=True)
            held["spectrum"] = forward_blocks(to_blocks(both[0].astype(jnp.float32)), tables)
            product_local = both[1]
        else:
            product_local = lax.all_to_all(product, "seq", split_axis=1, concat_axis=0, tiled=True)
        conv_local = causal(to_blocks(product_local)).transpose(0, 2, 1).reshape(length, chans)
        conv = lax.all_to_all(conv_local, "seq", split_axis=0, concat_axis=1, tiled=True)
        forward.append((query, keys, values, conv.astype(jnp.float32)))

    def stage(grad_out, top, slot):
        query, keys, values, conv_wide = forward[slot]
        d_out, sent = project_and_exchange(grad_out, weight_out, query)
        sent = sent.reshape(seq_count, chans, height)
        d_prod_blocks = adjoint(sent)
        sent_back = d_prod_blocks.reshape(seq_count * chans, height).astype(jnp.float32)
        return exchange_and_finish(
            sent_back, d_out, conv_wide, values, keys, grad_out, taps, weight_in, top
        )

    incoming = cotangent[0]
    every = []
    for step in range(micro + section_count - 1):
        index = step - (section_count - 1 - section_place)
        later = jnp.clip(index + 1, 0, micro - 1)
        top = lax.dynamic_index_in_dim(cotangent, later, 0, keepdims=False)
        if micro == 1:
            d_input, incoming = stage(incoming, top, 0)
        else:
            slot = jnp.clip(index, 0, micro - 1)
            d_input, incoming = lax.switch(
                slot, [functools.partial(stage, slot=m) for m in range(micro)], incoming, top
            )
        every.append(d_input)
    first = section_count - 1 - section_place
    grads = []
    for m in range(micro):
        picked = every[m]
        for step in range(m + 1, len(every)):
            picked = jnp.where(first + m == step, every[step], picked)
        grads.append(picked)
    return jnp.stack(grads)[None]


def solution(mesh):
    return jax.shard_map(
        shards,
        mesh=mesh,
        in_specs=(
            P(None, "seq", None),
            P("section", None, "seq", None),
            P("section", None, None),
            P("section", None, None),
            P("section", None, None),
            P("section", "seq", None),
            P("section", None),
        ),
        out_specs=P("section", None, "seq", None),
        check_vma=False,
    )
```

```python
import functools
import math

import jax
import jax.numpy as jnp
from jax import lax
from jax.experimental import pallas as pl
from jax.experimental.pallas import tpu as pltpu
from jax.sharding import PartitionSpec as P

accuracy = lax.Precision.HIGH


def shifted(value, axis, by):
    count = lax.axis_size(axis)
    pairs = [(i, i + by) for i in range(count) if 0 <= i + by < count]
    return lax.ppermute(value, axis, pairs)


def phase_table(height, breadth, period):
    row_ids = lax.broadcasted_iota(jnp.int32, (height, breadth), 0)
    col_ids = lax.broadcasted_iota(jnp.int32, (height, breadth), 1)
    angle = (row_ids * col_ids % period).astype(jnp.float32) * (2.0 * math.pi / period)
    return (jnp.cos(angle), jnp.sin(angle))


def spectrum_tables(length, inner):
    outer = 2 * length // inner
    cos_outer, sin_outer = phase_table(outer, length // inner, outer)
    cos_twist, sin_twist = phase_table(inner, outer, 2 * length)
    cos_inner, sin_inner = phase_table(inner, inner, inner)
    mixer = jnp.concatenate(
        [
            jnp.concatenate([cos_inner, sin_inner], axis=1),
            jnp.concatenate([-sin_inner, cos_inner], axis=1),
        ],
        axis=0,
    )
    return {
        "outer": jnp.concatenate([cos_outer, -sin_outer], axis=0),
        "twist": (cos_twist, sin_twist),
        "forward": mixer,
        "inverse": mixer,
    }


def forward_blocks(blocks, tables):
    count, chans, inner = blocks.shape
    outer = 2 * count
    one = jnp.einsum("kn,ncb->cbk", tables["outer"], blocks, precision=accuracy)
    real_one = one[:, :, :outer]
    imag_one = one[:, :, outer:]
    cos_twist, sin_twist = tables["twist"]
    real_two = real_one * cos_twist + imag_one * sin_twist
    imag_two = imag_one * cos_twist - real_one * sin_twist
    both = jnp.einsum(
        "jb,cbk->cjk",
        tables["forward"],
        jnp.concatenate([real_two, imag_two], axis=1),
        precision=accuracy,
    )
    return (both[:, :inner], both[:, inner:])


def inverse_blocks(real, imag, tables):
    chans, inner, outer = real.shape
    length = outer * inner // 2
    both = jnp.einsum(
        "jb,cjk->cbk", tables["inverse"], jnp.concatenate([real, imag], axis=1), precision=accuracy
    )
    real_one = both[:, :inner]
    imag_one = both[:, inner:]
    cos_twist, sin_twist = tables["twist"]
    real_two = real_one * cos_twist - imag_one * sin_twist
    imag_two = imag_one * cos_twist + real_one * sin_twist
    series = jnp.einsum(
        "kn,cbk->ncb",
        tables["outer"],
        jnp.concatenate([real_two, imag_two], axis=2),
        precision=accuracy,
    )
    return series / (2.0 * length)


def channel_conv(blocks, spectrum, bias_part, adjoint, tables):
    values = blocks.astype(jnp.float32)
    real, imag = forward_blocks(values, tables)
    filter_real, filter_imag = spectrum
    if adjoint:
        prod_real = real * filter_real + imag * filter_imag
        prod_imag = imag * filter_real - real * filter_imag
    else:
        prod_real = real * filter_real - imag * filter_imag
        prod_imag = real * filter_imag + imag * filter_real
    direct = bias_part[None, :, None] * values
    return (inverse_blocks(prod_real, prod_imag, tables) + direct).astype(jnp.bfloat16)


def begin_kernel(grad_ref, weight_ref, query_ref, d_out_ref, o_ref, outgoing, landed, send_sems, recv_sems):
    count = lax.axis_size("seq")
    me = lax.axis_index("seq")
    section = lax.axis_index("section")
    mesh_ids = pl.DeviceIdType.MESH
    barrier = pltpu.get_barrier_semaphore()

    def greet(k, _):
        peer = lax.rem(me + k, count)
        pl.semaphore_signal(barrier, inc=1, device_id=(peer, section), device_id_type=mesh_ids)
        return 0

    lax.fori_loop(1, count, greet, 0)
    d_out = lax.dot_general(
        grad_ref[...], weight_ref[...], (((1,), (1,)), ((), ())), preferred_element_type=jnp.float32
    )
    d_out_ref[...] = d_out
    d_conv = (d_out * query_ref[...]).astype(jnp.bfloat16).astype(jnp.float32)
    outgoing[...] = d_conv.T.reshape(outgoing.shape).astype(outgoing.dtype)
    pl.semaphore_wait(barrier, count - 1)

    def describe(k):
        peer = lax.rem(me + k, count)
        return pltpu.make_async_remote_copy(
            src_ref=outgoing.at[peer],
            dst_ref=landed.at[me],
            send_sem=send_sems.at[k],
            recv_sem=recv_sems.at[k],
            device_id=(peer, section),
            device_id_type=mesh_ids,
        )

    def send(k, _):
        describe(k).start()
        return 0

    def finish(k, _):
        describe(k).wait()
        return 0

    lax.fori_loop(1, count, send, 0)
    landed[pl.ds(me, 1)] = outgoing[pl.ds(me, 1)]
    lax.fori_loop(1, count, finish, 0)
    o_ref[...] = landed[...]


def project_and_exchange(grad_out, weight_out, query):
    count = lax.axis_size("seq")
    rows, width = query.shape
    vmem = pl.BlockSpec(memory_space=pltpu.VMEM)
    block = (count, width // count, rows)
    return pl.pallas_call(
        begin_kernel,
        out_shape=(
            jax.ShapeDtypeStruct((rows, width), jnp.float32),
            jax.ShapeDtypeStruct(block, jnp.bfloat16),
        ),
        in_specs=[vmem] * 3,
        out_specs=(vmem, vmem),
        scratch_shapes=[
            pltpu.VMEM(block, jnp.bfloat16),
            pltpu.VMEM(block, jnp.bfloat16),
            pltpu.SemaphoreType.DMA((count,)),
            pltpu.SemaphoreType.DMA((count,)),
        ],
        compiler_params=pltpu.CompilerParams(collective_id=0, has_side_effects=True),
    )(grad_out, weight_out, query)


def finish_kernel(
    sent_ref, d_out_ref, conv_ref, values_ref, keys_ref, grad_ref, taps_ref, weight_ref, top_ref,
    o_ref, next_ref, landed, extended, head, from_above, send_sems, recv_sems, rim_sems, hand_sems, acks,
):
    count = lax.axis_size("seq")
    rows, width = d_out_ref.shape
    me = lax.axis_index("seq")
    section = lax.axis_index("section")
    mesh_ids = pl.DeviceIdType.MESH
    barrier = pltpu.get_barrier_semaphore()

    def greet(k, _):
        peer = lax.rem(me + k, count)
        pl.semaphore_signal(barrier, inc=1, device_id=(peer, section), device_id_type=mesh_ids)
        return 0

    lax.fori_loop(1, count, greet, 0)
    sections = lax.axis_size("section")
    has_up = section < sections - 1
    has_down = section > 0
    up = (me, jnp.minimum(section + 1, sections - 1))
    down = (me, jnp.maximum(section - 1, 0))
    neighbours = has_up.astype(jnp.int32) + has_down.astype(jnp.int32)

    @pl.when(has_up)
    def _():
        pl.semaphore_signal(barrier, inc=1, device_id=up, device_id_type=mesh_ids)

    @pl.when(has_down)
    def _():
        pl.semaphore_signal(barrier, inc=1, device_id=down, device_id_type=mesh_ids)

    pl.semaphore_wait(barrier, count - 1 + neighbours)

    @pl.when(has_up)
    def _():
        pl.semaphore_signal(acks, inc=1, device_id=up, device_id_type=mesh_ids)

    @pl.when(has_down)
    def _():
        pl.semaphore_signal(acks, inc=1, device_id=down, device_id_type=mesh_ids)

    def describe(k):
        peer = lax.rem(me + k, count)
        return pltpu.make_async_remote_copy(
            src_ref=sent_ref.at[peer],
            dst_ref=landed.at[me],
            send_sem=send_sems.at[k],
            recv_sem=recv_sems.at[k],
            device_id=(peer, section),
            device_id_type=mesh_ids,
        )

    def send(k, _):
        describe(k).start()
        return 0

    def finish(k, _):
        describe(k).wait()
        return 0

    lax.fori_loop(1, count, send, 0)
    landed[pl.ds(me, 1)] = sent_ref[pl.ds(me, 1)]
    lax.fori_loop(1, count, finish, 0)

    d_prod = landed[...].astype(jnp.float32).reshape(width, rows).T
    d_mixed = jnp.concatenate(
        [
            (d_out_ref[...] * conv_ref[...]).astype(jnp.bfloat16),
            (d_prod * values_ref[...]).astype(jnp.bfloat16),
            (d_prod * keys_ref[...]).astype(jnp.bfloat16),
        ],
        axis=1,
    ).astype(jnp.float32)
    head[...] = d_mixed[:8]
    rim = pltpu.make_async_remote_copy(
        src_ref=head,
        dst_ref=extended.at[pl.ds(rows, 8)],
        send_sem=rim_sems.at[0],
        recv_sem=rim_sems.at[1],
        device_id=(jnp.maximum(me - 1, 0), section),
        device_id_type=mesh_ids,
    )

    @pl.when(me > 0)
    def _():
        rim.start()

    extended[pl.ds(0, rows)] = d_mixed

    @pl.when(me == count - 1)
    def _():
        extended[pl.ds(rows, 8)] = jnp.zeros((8, extended.shape[1]), jnp.float32)

    @pl.when(me < count - 1)
    def _():
        rim.wait_recv()

    taps = taps_ref[...]
    d_proj = (
        taps[0:1] * extended[pl.ds(0, rows)]
        + taps[1:2] * extended[pl.ds(1, rows)]
        + taps[2:3] * extended[pl.ds(2, rows)]
    ).astype(jnp.bfloat16)
    total = grad_ref[...].astype(jnp.float32) + lax.dot_general(
        d_proj, weight_ref[...], (((1,), (1,)), ((), ())), preferred_element_type=jnp.float32
    )
    o_ref[...] = total.astype(o_ref.dtype)
    hand = pltpu.make_async_remote_copy(
        src_ref=o_ref,
        dst_ref=from_above,
        send_sem=hand_sems.at[0],
        recv_sem=hand_sems.at[1],
        device_id=down,
        device_id_type=mesh_ids,
    )

    @pl.when(has_down)
    def _():
        hand.start()

    @pl.when(me > 0)
    def _():
        rim.wait_send()

    @pl.when(has_up)
    def _():
        hand.wait_recv()
        next_ref[...] = from_above[...]

    @pl.when(jnp.logical_not(has_up))
    def _():
        next_ref[...] = top_ref[...]

    @pl.when(has_down)
    def _():
        hand.wait_send()

    pl.semaphore_wait(acks, neighbours)


def exchange_and_finish(sent, d_out, conv_wide, values, keys, grad_out, taps, weight_in, top):
    count = lax.axis_size("seq")
    rows, width = d_out.shape
    vmem = pl.BlockSpec(memory_space=pltpu.VMEM)
    return pl.pallas_call(
        finish_kernel,
        out_shape=(
            jax.ShapeDtypeStruct(grad_out.shape, grad_out.dtype),
            jax.ShapeDtypeStruct(grad_out.shape, grad_out.dtype),
        ),
        in_specs=[vmem] * 9,
        out_specs=(vmem, vmem),
        scratch_shapes=[
            pltpu.VMEM(sent.shape, sent.dtype),
            pltpu.VMEM((rows + 8, taps.shape[1]), jnp.float32),
            pltpu.VMEM((8, taps.shape[1]), jnp.float32),
            pltpu.VMEM(grad_out.shape, grad_out.dtype),
            pltpu.SemaphoreType.DMA((count,)),
            pltpu.SemaphoreType.DMA((count,)),
            pltpu.SemaphoreType.DMA((2,)),
            pltpu.SemaphoreType.DMA((2,)),
            pltpu.SemaphoreType.REGULAR,
        ],
        compiler_params=pltpu.CompilerParams(collective_id=1, has_side_effects=True),
    )(sent, d_out, conv_wide, values, keys, grad_out, taps, weight_in, top)


def when(active, action, *operands):

    def skipped(*inputs):
        return jax.tree.map(jnp.zeros_like, action(*inputs))

    return lax.cond(active, action, skipped, *operands)


def shards(cotangent, projected, w_in, w_out, short_filter, long_filter, filter_bias):
    seq_count = lax.axis_size("seq")
    seq_place = lax.axis_index("seq")
    section_count = lax.axis_size("section")
    section_place = lax.axis_index("section")
    micro = projected.shape[1]
    height = projected.shape[2]
    width = w_out.shape[2]
    length = height * seq_count
    tables = spectrum_tables(length, height)
    chans = width // seq_count
    bias_part = lax.dynamic_slice_in_dim(filter_bias[0], seq_place * chans, chans, 0)
    weight_in = w_in[0]
    weight_out = w_out[0]
    taps = short_filter[0]
    contract = (((1,), (1,)), ((), ()))

    held = {}

    def causal(blocks):
        return channel_conv(blocks, held["spectrum"], bias_part, False, tables)

    def adjoint(blocks):
        return channel_conv(blocks, held["spectrum"], bias_part, True, tables)

    def to_blocks(series):
        return series.reshape(seq_count, height, chans).transpose(0, 2, 1)

    forward = []
    for slot in range(micro):
        proj = projected[0, slot]
        rim = shifted(proj[height - 2 :], "seq", 1)
        padded = jnp.concatenate([rim, proj], axis=0).astype(jnp.float32)
        mixed = taps[0] * padded[2:] + taps[1] * padded[1:-1] + taps[2] * padded[:-2]
        query = mixed[:, :width]
        keys = mixed[:, width : 2 * width]
        values = mixed[:, 2 * width :]
        product = (keys * values).astype(jnp.bfloat16)
        if slot == 0:
            both = jnp.stack([long_filter[0].astype(jnp.bfloat16), product])
            both = lax.all_to_all(both, "seq", split_axis=2, concat_axis=1, tiled=True)
            held["spectrum"] = forward_blocks(to_blocks(both[0].astype(jnp.float32)), tables)
            product_local = both[1]
        else:
            product_local = lax.all_to_all(product, "seq", split_axis=1, concat_axis=0, tiled=True)
        conv_local = causal(to_blocks(product_local)).transpose(0, 2, 1).reshape(length, chans)
        conv = lax.all_to_all(conv_local, "seq", split_axis=0, concat_axis=1, tiled=True)
        forward.append((query, keys, values, conv.astype(jnp.float32)))

    def stage(grad_out, top, slot):
        query, keys, values, conv_wide = forward[slot]
        d_out, sent = project_and_exchange(grad_out, weight_out, query)
        d_prod_blocks = adjoint(sent)
        return exchange_and_finish(
            d_prod_blocks, d_out, conv_wide, values, keys, grad_out, taps, weight_in, top
        )

    incoming = cotangent[0]
    every = []
    for step in range(micro + section_count - 1):
        index = step - (section_count - 1 - section_place)
        later = jnp.clip(index + 1, 0, micro - 1)
        top = lax.dynamic_index_in_dim(cotangent, later, 0, keepdims=False)
        if micro == 1:
            d_input, incoming = stage(incoming, top, 0)
        else:
            slot = jnp.clip(index, 0, micro - 1)
            d_input, incoming = lax.switch(
                slot, [functools.partial(stage, slot=m) for m in range(micro)], incoming, top
            )
        every.append(d_input)
    first = section_count - 1 - section_place
    grads = []
    for m in range(micro):
        picked = every[m]
        for step in range(m + 1, len(every)):
            picked = jnp.where(first + m == step, every[step], picked)
        grads.append(picked)
    return jnp.stack(grads)[None]


def solution(mesh):
    return jax.shard_map(
        shards,
        mesh=mesh,
        in_specs=(
            P(None, "seq", None),
            P("section", None, "seq", None),
            P("section", None, None),
            P("section", None, None),
            P("section", None, None),
            P("section", "seq", None),
            P("section", None),
        ),
        out_specs=P("section", None, "seq", None),
        check_vma=False,
    )
```

```python
import functools
import math

import jax
import jax.numpy as jnp
from jax import lax
from jax.experimental import pallas as pl
from jax.experimental.pallas import tpu as pltpu
from jax.sharding import PartitionSpec as P

accuracy = lax.Precision.HIGH


def shifted(value, axis, by):
    count = lax.axis_size(axis)
    pairs = [(i, i + by) for i in range(count) if 0 <= i + by < count]
    return lax.ppermute(value, axis, pairs)


def phase_table(height, breadth, period):
    row_ids = lax.broadcasted_iota(jnp.int32, (height, breadth), 0)
    col_ids = lax.broadcasted_iota(jnp.int32, (height, breadth), 1)
    angle = (row_ids * col_ids % period).astype(jnp.float32) * (2.0 * math.pi / period)
    return (jnp.cos(angle), jnp.sin(angle))


def spectrum_tables(length, inner):
    outer = 2 * length // inner
    cos_outer, sin_outer = phase_table(outer, length // inner, outer)
    cos_twist, sin_twist = phase_table(inner, outer, 2 * length)
    cos_inner, sin_inner = phase_table(inner, inner, inner)
    mixer = jnp.concatenate(
        [
            jnp.concatenate([cos_inner, sin_inner], axis=1),
            jnp.concatenate([-sin_inner, cos_inner], axis=1),
        ],
        axis=0,
    )
    return {
        "outer": jnp.concatenate([cos_outer, -sin_outer], axis=0),
        "twist": (cos_twist, sin_twist),
        "forward": mixer,
        "inverse": mixer,
    }


def forward_blocks(blocks, tables):
    count, chans, inner = blocks.shape
    outer = 2 * count
    one = jnp.einsum("kn,ncb->cbk", tables["outer"], blocks, precision=accuracy)
    real_one = one[:, :, :outer]
    imag_one = one[:, :, outer:]
    cos_twist, sin_twist = tables["twist"]
    real_two = real_one * cos_twist + imag_one * sin_twist
    imag_two = imag_one * cos_twist - real_one * sin_twist
    both = jnp.einsum(
        "jb,cbk->cjk",
        tables["forward"],
        jnp.concatenate([real_two, imag_two], axis=1),
        precision=accuracy,
    )
    return (both[:, :inner], both[:, inner:])


def inverse_blocks(real, imag, tables):
    chans, inner, outer = real.shape
    length = outer * inner // 2
    both = jnp.einsum(
        "jb,cjk->cbk", tables["inverse"], jnp.concatenate([real, imag], axis=1), precision=accuracy
    )
    real_one = both[:, :inner]
    imag_one = both[:, inner:]
    cos_twist, sin_twist = tables["twist"]
    real_two = real_one * cos_twist - imag_one * sin_twist
    imag_two = imag_one * cos_twist + real_one * sin_twist
    series = jnp.einsum(
        "kn,cbk->ncb",
        tables["outer"],
        jnp.concatenate([real_two, imag_two], axis=2),
        precision=accuracy,
    )
    return series / (2.0 * length)


def channel_conv(blocks, spectrum, bias_part, adjoint, tables):
    values = blocks.astype(jnp.float32)
    real, imag = forward_blocks(values, tables)
    filter_real, filter_imag = spectrum
    if adjoint:
        prod_real = real * filter_real + imag * filter_imag
        prod_imag = imag * filter_real - real * filter_imag
    else:
        prod_real = real * filter_real - imag * filter_imag
        prod_imag = real * filter_imag + imag * filter_real
    direct = bias_part[None, :, None] * values
    return (inverse_blocks(prod_real, prod_imag, tables) + direct).astype(jnp.bfloat16)


def begin_kernel(grad_ref, weight_ref, query_ref, d_out_ref, o_ref, outgoing, landed, send_sems, recv_sems):
    count = lax.axis_size("seq")
    me = lax.axis_index("seq")
    section = lax.axis_index("section")
    mesh_ids = pl.DeviceIdType.MESH
    barrier = pltpu.get_barrier_semaphore()

    def greet(k, _):
        peer = lax.rem(me + k, count)
        pl.semaphore_signal(barrier, inc=1, device_id=(peer, section), device_id_type=mesh_ids)
        return 0

    lax.fori_loop(1, count, greet, 0)
    d_out = lax.dot_general(
        grad_ref[...], weight_ref[...], (((1,), (1,)), ((), ())), preferred_element_type=jnp.float32
    )
    d_out_ref[...] = d_out
    d_conv = (d_out * query_ref[...]).astype(jnp.bfloat16).astype(jnp.float32)
    outgoing[...] = d_conv.T.reshape(outgoing.shape).astype(outgoing.dtype)
    pl.semaphore_wait(barrier, count - 1)

    def describe(k):
        peer = lax.rem(me + k, count)
        return pltpu.make_async_remote_copy(
            src_ref=outgoing.at[peer],
            dst_ref=landed.at[me],
            send_sem=send_sems.at[k],
            recv_sem=recv_sems.at[k],
            device_id=(peer, section),
            device_id_type=mesh_ids,
        )

    def send(k, _):
        describe(k).start()
        return 0

    def finish(k, _):
        describe(k).wait()
        return 0

    lax.fori_loop(1, count, send, 0)
    landed[pl.ds(me, 1)] = outgoing[pl.ds(me, 1)]
    lax.fori_loop(1, count, finish, 0)
    o_ref[...] = landed[...]


def project_and_exchange(grad_out, weight_out, query):
    count = lax.axis_size("seq")
    rows, width = query.shape
    vmem = pl.BlockSpec(memory_space=pltpu.VMEM)
    block = (count, width // count, rows)
    return pl.pallas_call(
        begin_kernel,
        out_shape=(
            jax.ShapeDtypeStruct((rows, width), jnp.float32),
            jax.ShapeDtypeStruct(block, jnp.bfloat16),
        ),
        in_specs=[vmem] * 3,
        out_specs=(vmem, vmem),
        scratch_shapes=[
            pltpu.VMEM(block, jnp.bfloat16),
            pltpu.VMEM(block, jnp.bfloat16),
            pltpu.SemaphoreType.DMA((count,)),
            pltpu.SemaphoreType.DMA((count,)),
        ],
        compiler_params=pltpu.CompilerParams(collective_id=0, has_side_effects=True),
    )(grad_out, weight_out, query)


def finish_kernel(
    sent_ref, d_out_ref, conv_ref, values_ref, keys_ref, grad_ref, taps_ref, weight_ref, top_ref,
    o_ref, next_ref, landed, extended, head, from_above, send_sems, recv_sems, rim_sems, hand_sems, acks,
):
    count = lax.axis_size("seq")
    rows, width = d_out_ref.shape
    me = lax.axis_index("seq")
    section = lax.axis_index("section")
    mesh_ids = pl.DeviceIdType.MESH
    barrier = pltpu.get_barrier_semaphore()

    def greet(k, _):
        peer = lax.rem(me + k, count)
        pl.semaphore_signal(barrier, inc=1, device_id=(peer, section), device_id_type=mesh_ids)
        return 0

    lax.fori_loop(1, count, greet, 0)
    sections = lax.axis_size("section")
    has_up = section < sections - 1
    has_down = section > 0
    up = (me, jnp.minimum(section + 1, sections - 1))
    down = (me, jnp.maximum(section - 1, 0))
    neighbours = has_up.astype(jnp.int32) + has_down.astype(jnp.int32)

    @pl.when(has_up)
    def _():
        pl.semaphore_signal(barrier, inc=1, device_id=up, device_id_type=mesh_ids)

    @pl.when(has_down)
    def _():
        pl.semaphore_signal(barrier, inc=1, device_id=down, device_id_type=mesh_ids)

    pl.semaphore_wait(barrier, count - 1 + neighbours)

    @pl.when(has_up)
    def _():
        pl.semaphore_signal(acks, inc=1, device_id=up, device_id_type=mesh_ids)

    @pl.when(has_down)
    def _():
        pl.semaphore_signal(acks, inc=1, device_id=down, device_id_type=mesh_ids)

    def describe(k):
        peer = lax.rem(me + k, count)
        return pltpu.make_async_remote_copy(
            src_ref=sent_ref.at[peer],
            dst_ref=landed.at[me],
            send_sem=send_sems.at[k],
            recv_sem=recv_sems.at[k],
            device_id=(peer, section),
            device_id_type=mesh_ids,
        )

    def send(k, _):
        describe(k).start()
        return 0

    def finish(k, _):
        describe(k).wait()
        return 0

    lax.fori_loop(1, count, send, 0)
    landed[pl.ds(me, 1)] = sent_ref[pl.ds(me, 1)]
    lax.fori_loop(1, count, finish, 0)

    d_prod = landed[...].astype(jnp.float32).reshape(width, rows).T
    d_mixed = jnp.concatenate(
        [
            (d_out_ref[...] * conv_ref[...]).astype(jnp.bfloat16),
            (d_prod * values_ref[...]).astype(jnp.bfloat16),
            (d_prod * keys_ref[...]).astype(jnp.bfloat16),
        ],
        axis=1,
    ).astype(jnp.float32)
    head[...] = d_mixed[:8]
    rim = pltpu.make_async_remote_copy(
        src_ref=head,
        dst_ref=extended.at[pl.ds(rows, 8)],
        send_sem=rim_sems.at[0],
        recv_sem=rim_sems.at[1],
        device_id=(jnp.maximum(me - 1, 0), section),
        device_id_type=mesh_ids,
    )

    @pl.when(me > 0)
    def _():
        rim.start()

    extended[pl.ds(0, rows)] = d_mixed

    @pl.when(me == count - 1)
    def _():
        extended[pl.ds(rows, 8)] = jnp.zeros((8, extended.shape[1]), jnp.float32)

    taps = taps_ref[...]
    weight = weight_ref[...]
    split = rows - 16

    def project(start, size):
        d_proj = (
            taps[0:1] * extended[pl.ds(start, size)]
            + taps[1:2] * extended[pl.ds(start + 1, size)]
            + taps[2:3] * extended[pl.ds(start + 2, size)]
        ).astype(jnp.bfloat16)
        total = grad_ref[pl.ds(start, size)].astype(jnp.float32) + lax.dot_general(
            d_proj, weight, (((1,), (1,)), ((), ())), preferred_element_type=jnp.float32
        )
        o_ref[pl.ds(start, size)] = total.astype(o_ref.dtype)

    def hand(start, size, slot):
        return pltpu.make_async_remote_copy(
            src_ref=o_ref.at[pl.ds(start, size)],
            dst_ref=from_above.at[pl.ds(start, size)],
            send_sem=hand_sems.at[2 * slot],
            recv_sem=hand_sems.at[2 * slot + 1],
            device_id=down,
            device_id_type=mesh_ids,
        )

    first, last = hand(0, split, 0), hand(split, rows - split, 1)
    project(0, split)

    @pl.when(has_down)
    def _():
        first.start()

    @pl.when(me < count - 1)
    def _():
        rim.wait_recv()

    project(split, rows - split)

    @pl.when(has_down)
    def _():
        last.start()

    @pl.when(me > 0)
    def _():
        rim.wait_send()

    @pl.when(has_up)
    def _():
        first.wait_recv()
        last.wait_recv()
        next_ref[...] = from_above[...]

    @pl.when(jnp.logical_not(has_up))
    def _():
        next_ref[...] = top_ref[...]

    @pl.when(has_down)
    def _():
        first.wait_send()
        last.wait_send()

    pl.semaphore_wait(acks, neighbours)


def exchange_and_finish(sent, d_out, conv_wide, values, keys, grad_out, taps, weight_in, top):
    count = lax.axis_size("seq")
    rows, width = d_out.shape
    vmem = pl.BlockSpec(memory_space=pltpu.VMEM)
    return pl.pallas_call(
        finish_kernel,
        out_shape=(
            jax.ShapeDtypeStruct(grad_out.shape, grad_out.dtype),
            jax.ShapeDtypeStruct(grad_out.shape, grad_out.dtype),
        ),
        in_specs=[vmem] * 9,
        out_specs=(vmem, vmem),
        scratch_shapes=[
            pltpu.VMEM(sent.shape, sent.dtype),
            pltpu.VMEM((rows + 8, taps.shape[1]), jnp.float32),
            pltpu.VMEM((8, taps.shape[1]), jnp.float32),
            pltpu.VMEM(grad_out.shape, grad_out.dtype),
            pltpu.SemaphoreType.DMA((count,)),
            pltpu.SemaphoreType.DMA((count,)),
            pltpu.SemaphoreType.DMA((2,)),
            pltpu.SemaphoreType.DMA((4,)),
            pltpu.SemaphoreType.REGULAR,
        ],
        compiler_params=pltpu.CompilerParams(collective_id=1, has_side_effects=True),
    )(sent, d_out, conv_wide, values, keys, grad_out, taps, weight_in, top)


def when(active, action, *operands):

    def skipped(*inputs):
        return jax.tree.map(jnp.zeros_like, action(*inputs))

    return lax.cond(active, action, skipped, *operands)


def shards(cotangent, projected, w_in, w_out, short_filter, long_filter, filter_bias):
    seq_count = lax.axis_size("seq")
    seq_place = lax.axis_index("seq")
    section_count = lax.axis_size("section")
    section_place = lax.axis_index("section")
    micro = projected.shape[1]
    height = projected.shape[2]
    width = w_out.shape[2]
    length = height * seq_count
    tables = spectrum_tables(length, height)
    chans = width // seq_count
    bias_part = lax.dynamic_slice_in_dim(filter_bias[0], seq_place * chans, chans, 0)
    weight_in = w_in[0]
    weight_out = w_out[0]
    taps = short_filter[0]
    contract = (((1,), (1,)), ((), ()))

    held = {}

    def causal(blocks):
        return channel_conv(blocks, held["spectrum"], bias_part, False, tables)

    def adjoint(blocks):
        return channel_conv(blocks, held["spectrum"], bias_part, True, tables)

    def to_blocks(series):
        return series.reshape(seq_count, height, chans).transpose(0, 2, 1)

    forward = []
    for slot in range(micro):
        proj = projected[0, slot]
        rim = shifted(proj[height - 2 :], "seq", 1)
        padded = jnp.concatenate([rim, proj], axis=0).astype(jnp.float32)
        mixed = taps[0] * padded[2:] + taps[1] * padded[1:-1] + taps[2] * padded[:-2]
        query = mixed[:, :width]
        keys = mixed[:, width : 2 * width]
        values = mixed[:, 2 * width :]
        product = (keys * values).astype(jnp.bfloat16)
        if slot == 0:
            both = jnp.stack([long_filter[0].astype(jnp.bfloat16), product])
            both = lax.all_to_all(both, "seq", split_axis=2, concat_axis=1, tiled=True)
            held["spectrum"] = forward_blocks(to_blocks(both[0].astype(jnp.float32)), tables)
            product_local = both[1]
        else:
            product_local = lax.all_to_all(product, "seq", split_axis=1, concat_axis=0, tiled=True)
        conv_local = causal(to_blocks(product_local)).transpose(0, 2, 1).reshape(length, chans)
        conv = lax.all_to_all(conv_local, "seq", split_axis=0, concat_axis=1, tiled=True)
        forward.append((query, keys, values, conv.astype(jnp.float32)))

    def stage(grad_out, top, slot):
        query, keys, values, conv_wide = forward[slot]
        d_out, sent = project_and_exchange(grad_out, weight_out, query)
        d_prod_blocks = adjoint(sent)
        return exchange_and_finish(
            d_prod_blocks, d_out, conv_wide, values, keys, grad_out, taps, weight_in, top
        )

    incoming = cotangent[0]
    every = []
    for step in range(micro + section_count - 1):
        index = step - (section_count - 1 - section_place)
        later = jnp.clip(index + 1, 0, micro - 1)
        top = lax.dynamic_index_in_dim(cotangent, later, 0, keepdims=False)
        if micro == 1:
            d_input, incoming = stage(incoming, top, 0)
        else:
            slot = jnp.clip(index, 0, micro - 1)
            d_input, incoming = lax.switch(
                slot, [functools.partial(stage, slot=m) for m in range(micro)], incoming, top
            )
        every.append(d_input)
    first = section_count - 1 - section_place
    grads = []
    for m in range(micro):
        picked = every[m]
        for step in range(m + 1, len(every)):
            picked = jnp.where(first + m == step, every[step], picked)
        grads.append(picked)
    return jnp.stack(grads)[None]


def solution(mesh):
    return jax.shard_map(
        shards,
        mesh=mesh,
        in_specs=(
            P(None, "seq", None),
            P("section", None, "seq", None),
            P("section", None, None),
            P("section", None, None),
            P("section", None, None),
            P("section", "seq", None),
            P("section", None),
        ),
        out_specs=P("section", None, "seq", None),
        check_vma=False,
    )
```

```python
import functools
import math

import jax
import jax.numpy as jnp
from jax import lax
from jax.experimental import pallas as pl
from jax.experimental.pallas import tpu as pltpu
from jax.sharding import PartitionSpec as P

accuracy = lax.Precision.HIGH


def shifted(value, axis, by):
    count = lax.axis_size(axis)
    pairs = [(i, i + by) for i in range(count) if 0 <= i + by < count]
    return lax.ppermute(value, axis, pairs)


def phase_table(height, breadth, period):
    row_ids = lax.broadcasted_iota(jnp.int32, (height, breadth), 0)
    col_ids = lax.broadcasted_iota(jnp.int32, (height, breadth), 1)
    angle = (row_ids * col_ids % period).astype(jnp.float32) * (2.0 * math.pi / period)
    return (jnp.cos(angle), jnp.sin(angle))


def spectrum_tables(length, inner):
    outer = 2 * length // inner
    cos_outer, sin_outer = phase_table(outer, length // inner, outer)
    cos_twist, sin_twist = phase_table(inner, outer, 2 * length)
    cos_inner, sin_inner = phase_table(inner, inner, inner)
    mixer = jnp.concatenate(
        [
            jnp.concatenate([cos_inner, sin_inner], axis=1),
            jnp.concatenate([-sin_inner, cos_inner], axis=1),
        ],
        axis=0,
    )
    return {
        "outer": jnp.concatenate([cos_outer, -sin_outer], axis=0),
        "twist": (cos_twist, sin_twist),
        "forward": mixer,
        "inverse": mixer,
    }


def forward_blocks(blocks, tables):
    count, chans, inner = blocks.shape
    outer = 2 * count
    one = jnp.einsum("kn,ncb->cbk", tables["outer"], blocks, precision=accuracy)
    real_one = one[:, :, :outer]
    imag_one = one[:, :, outer:]
    cos_twist, sin_twist = tables["twist"]
    real_two = real_one * cos_twist + imag_one * sin_twist
    imag_two = imag_one * cos_twist - real_one * sin_twist
    both = jnp.einsum(
        "jb,cbk->cjk",
        tables["forward"],
        jnp.concatenate([real_two, imag_two], axis=1),
        precision=accuracy,
    )
    return (both[:, :inner], both[:, inner:])


def inverse_blocks(real, imag, tables):
    chans, inner, outer = real.shape
    length = outer * inner // 2
    both = jnp.einsum(
        "jb,cjk->cbk", tables["inverse"], jnp.concatenate([real, imag], axis=1), precision=accuracy
    )
    real_one = both[:, :inner]
    imag_one = both[:, inner:]
    cos_twist, sin_twist = tables["twist"]
    real_two = real_one * cos_twist - imag_one * sin_twist
    imag_two = imag_one * cos_twist + real_one * sin_twist
    series = jnp.einsum(
        "kn,cbk->ncb",
        tables["outer"],
        jnp.concatenate([real_two, imag_two], axis=2),
        precision=accuracy,
    )
    return series / (2.0 * length)


def channel_conv(blocks, spectrum, bias_part, adjoint, tables):
    values = blocks.astype(jnp.float32)
    real, imag = forward_blocks(values, tables)
    filter_real, filter_imag = spectrum
    if adjoint:
        prod_real = real * filter_real + imag * filter_imag
        prod_imag = imag * filter_real - real * filter_imag
    else:
        prod_real = real * filter_real - imag * filter_imag
        prod_imag = real * filter_imag + imag * filter_real
    direct = bias_part[None, :, None] * values
    return (inverse_blocks(prod_real, prod_imag, tables) + direct).astype(jnp.bfloat16)


def begin_kernel(grad_ref, weight_ref, query_ref, d_out_ref, o_ref, outgoing, landed, send_sems, recv_sems):
    count = lax.axis_size("seq")
    me = lax.axis_index("seq")
    section = lax.axis_index("section")
    mesh_ids = pl.DeviceIdType.MESH
    barrier = pltpu.get_barrier_semaphore()

    def greet(k, _):
        peer = lax.rem(me + k, count)
        pl.semaphore_signal(barrier, inc=1, device_id=(peer, section), device_id_type=mesh_ids)
        return 0

    lax.fori_loop(1, count, greet, 0)
    prepare(grad_ref[...], weight_ref, query_ref, d_out_ref, outgoing)
    pl.semaphore_wait(barrier, count - 1)
    scatter(o_ref, outgoing, landed, send_sems, recv_sems)


def prepare(grad, weight_ref, query_ref, d_out_ref, outgoing):
    d_out = lax.dot_general(
        grad, weight_ref[...], (((1,), (1,)), ((), ())), preferred_element_type=jnp.float32
    )
    d_out_ref[...] = d_out
    d_conv = (d_out * query_ref[...]).astype(jnp.bfloat16).astype(jnp.float32)
    outgoing[...] = d_conv.T.reshape(outgoing.shape).astype(outgoing.dtype)


def scatter(o_ref, outgoing, landed, send_sems, recv_sems):
    count = lax.axis_size("seq")
    me = lax.axis_index("seq")
    section = lax.axis_index("section")
    mesh_ids = pl.DeviceIdType.MESH

    def describe(k):
        peer = lax.rem(me + k, count)
        return pltpu.make_async_remote_copy(
            src_ref=outgoing.at[peer],
            dst_ref=landed.at[me],
            send_sem=send_sems.at[k],
            recv_sem=recv_sems.at[k],
            device_id=(peer, section),
            device_id_type=mesh_ids,
        )

    def send(k, _):
        describe(k).start()
        return 0

    def finish(k, _):
        describe(k).wait()
        return 0

    lax.fori_loop(1, count, send, 0)
    landed[pl.ds(me, 1)] = outgoing[pl.ds(me, 1)]
    lax.fori_loop(1, count, finish, 0)
    o_ref[...] = landed[...]


def project_and_exchange(grad_out, weight_out, query):
    count = lax.axis_size("seq")
    rows, width = query.shape
    vmem = pl.BlockSpec(memory_space=pltpu.VMEM)
    block = (count, width // count, rows)
    return pl.pallas_call(
        begin_kernel,
        out_shape=(
            jax.ShapeDtypeStruct((rows, width), jnp.float32),
            jax.ShapeDtypeStruct(block, jnp.bfloat16),
        ),
        in_specs=[vmem] * 3,
        out_specs=(vmem, vmem),
        scratch_shapes=[
            pltpu.VMEM(block, jnp.bfloat16),
            pltpu.VMEM(block, jnp.bfloat16),
            pltpu.SemaphoreType.DMA((count,)),
            pltpu.SemaphoreType.DMA((count,)),
        ],
        compiler_params=pltpu.CompilerParams(collective_id=0, has_side_effects=True),
    )(grad_out, weight_out, query)


def finish_kernel(then_begin, *refs):
    if then_begin:
        (sent_ref, d_out_ref, conv_ref, values_ref, keys_ref, grad_ref, taps_ref, weight_ref, top_ref,
         weight_out_ref, query_ref,
         o_ref, next_ref, next_d_out_ref, next_sent_ref,
         landed, extended, head, from_above, send_sems, recv_sems, rim_sems, hand_sems, acks,
         outgoing, landed_next, next_send_sems, next_recv_sems) = refs
    else:
        (sent_ref, d_out_ref, conv_ref, values_ref, keys_ref, grad_ref, taps_ref, weight_ref, top_ref,
         o_ref, next_ref,
         landed, extended, head, from_above, send_sems, recv_sems, rim_sems, hand_sems, acks) = refs
    count = lax.axis_size("seq")
    rows, width = d_out_ref.shape
    me = lax.axis_index("seq")
    section = lax.axis_index("section")
    mesh_ids = pl.DeviceIdType.MESH
    barrier = pltpu.get_barrier_semaphore()

    def greet(k, _):
        peer = lax.rem(me + k, count)
        pl.semaphore_signal(barrier, inc=1, device_id=(peer, section), device_id_type=mesh_ids)
        return 0

    lax.fori_loop(1, count, greet, 0)
    sections = lax.axis_size("section")
    has_up = section < sections - 1
    has_down = section > 0
    up = (me, jnp.minimum(section + 1, sections - 1))
    down = (me, jnp.maximum(section - 1, 0))
    neighbours = has_up.astype(jnp.int32) + has_down.astype(jnp.int32)

    @pl.when(has_up)
    def _():
        pl.semaphore_signal(barrier, inc=1, device_id=up, device_id_type=mesh_ids)

    @pl.when(has_down)
    def _():
        pl.semaphore_signal(barrier, inc=1, device_id=down, device_id_type=mesh_ids)

    pl.semaphore_wait(barrier, count - 1 + neighbours)

    @pl.when(has_up)
    def _():
        pl.semaphore_signal(acks, inc=1, device_id=up, device_id_type=mesh_ids)

    @pl.when(has_down)
    def _():
        pl.semaphore_signal(acks, inc=1, device_id=down, device_id_type=mesh_ids)

    def describe(k):
        peer = lax.rem(me + k, count)
        return pltpu.make_async_remote_copy(
            src_ref=sent_ref.at[peer],
            dst_ref=landed.at[me],
            send_sem=send_sems.at[k],
            recv_sem=recv_sems.at[k],
            device_id=(peer, section),
            device_id_type=mesh_ids,
        )

    def send(k, _):
        describe(k).start()
        return 0

    def finish(k, _):
        describe(k).wait()
        return 0

    lax.fori_loop(1, count, send, 0)
    landed[pl.ds(me, 1)] = sent_ref[pl.ds(me, 1)]
    lax.fori_loop(1, count, finish, 0)

    d_prod = landed[...].astype(jnp.float32).reshape(width, rows).T
    d_mixed = jnp.concatenate(
        [
            (d_out_ref[...] * conv_ref[...]).astype(jnp.bfloat16),
            (d_prod * values_ref[...]).astype(jnp.bfloat16),
            (d_prod * keys_ref[...]).astype(jnp.bfloat16),
        ],
        axis=1,
    ).astype(jnp.float32)
    head[...] = d_mixed[:8]
    rim = pltpu.make_async_remote_copy(
        src_ref=head,
        dst_ref=extended.at[pl.ds(rows, 8)],
        send_sem=rim_sems.at[0],
        recv_sem=rim_sems.at[1],
        device_id=(jnp.maximum(me - 1, 0), section),
        device_id_type=mesh_ids,
    )

    @pl.when(me > 0)
    def _():
        rim.start()

    extended[pl.ds(0, rows)] = d_mixed

    @pl.when(me == count - 1)
    def _():
        extended[pl.ds(rows, 8)] = jnp.zeros((8, extended.shape[1]), jnp.float32)

    taps = taps_ref[...]
    weight = weight_ref[...]
    split = rows - 16

    def project(start, size):
        d_proj = (
            taps[0:1] * extended[pl.ds(start, size)]
            + taps[1:2] * extended[pl.ds(start + 1, size)]
            + taps[2:3] * extended[pl.ds(start + 2, size)]
        ).astype(jnp.bfloat16)
        total = grad_ref[pl.ds(start, size)].astype(jnp.float32) + lax.dot_general(
            d_proj, weight, (((1,), (1,)), ((), ())), preferred_element_type=jnp.float32
        )
        o_ref[pl.ds(start, size)] = total.astype(o_ref.dtype)

    def hand(start, size, slot):
        return pltpu.make_async_remote_copy(
            src_ref=o_ref.at[pl.ds(start, size)],
            dst_ref=from_above.at[pl.ds(start, size)],
            send_sem=hand_sems.at[2 * slot],
            recv_sem=hand_sems.at[2 * slot + 1],
            device_id=down,
            device_id_type=mesh_ids,
        )

    first, last = hand(0, split, 0), hand(split, rows - split, 1)
    project(0, split)

    @pl.when(has_down)
    def _():
        first.start()

    @pl.when(me < count - 1)
    def _():
        rim.wait_recv()

    project(split, rows - split)

    @pl.when(has_down)
    def _():
        last.start()

    @pl.when(me > 0)
    def _():
        rim.wait_send()

    @pl.when(has_up)
    def _():
        first.wait_recv()
        last.wait_recv()
        next_ref[...] = from_above[...]

    @pl.when(jnp.logical_not(has_up))
    def _():
        next_ref[...] = top_ref[...]

    if then_begin:
        prepare(next_ref[...], weight_out_ref, query_ref, next_d_out_ref, outgoing)
        scatter(next_sent_ref, outgoing, landed_next, next_send_sems, next_recv_sems)

    @pl.when(has_down)
    def _():
        first.wait_send()
        last.wait_send()

    pl.semaphore_wait(acks, neighbours)


def exchange_and_finish(sent, d_out, conv_wide, values, keys, grad_out, taps, weight_in, top, then=None):
    count = lax.axis_size("seq")
    rows, width = d_out.shape
    vmem = pl.BlockSpec(memory_space=pltpu.VMEM)
    grads = jax.ShapeDtypeStruct(grad_out.shape, grad_out.dtype)
    scratch = [
        pltpu.VMEM(sent.shape, sent.dtype),
        pltpu.VMEM((rows + 8, taps.shape[1]), jnp.float32),
        pltpu.VMEM((8, taps.shape[1]), jnp.float32),
        pltpu.VMEM(grad_out.shape, grad_out.dtype),
        pltpu.SemaphoreType.DMA((count,)),
        pltpu.SemaphoreType.DMA((count,)),
        pltpu.SemaphoreType.DMA((2,)),
        pltpu.SemaphoreType.DMA((4,)),
        pltpu.SemaphoreType.REGULAR,
    ]
    operands = [sent, d_out, conv_wide, values, keys, grad_out, taps, weight_in, top]
    outs = [grads, grads]
    if then is not None:
        operands += list(then)
        outs += [
            jax.ShapeDtypeStruct((rows, width), jnp.float32),
            jax.ShapeDtypeStruct(sent.shape, sent.dtype),
        ]
        scratch += [
            pltpu.VMEM(sent.shape, sent.dtype),
            pltpu.VMEM(sent.shape, sent.dtype),
            pltpu.SemaphoreType.DMA((count,)),
            pltpu.SemaphoreType.DMA((count,)),
        ]
    return pl.pallas_call(
        functools.partial(finish_kernel, then is not None),
        out_shape=tuple(outs),
        in_specs=[vmem] * len(operands),
        out_specs=tuple([vmem] * len(outs)),
        scratch_shapes=scratch,
        compiler_params=pltpu.CompilerParams(
            collective_id=1 if then is None else 2, has_side_effects=True
        ),
    )(*operands)


def when(active, action, *operands):

    def skipped(*inputs):
        return jax.tree.map(jnp.zeros_like, action(*inputs))

    return lax.cond(active, action, skipped, *operands)


def shards(cotangent, projected, w_in, w_out, short_filter, long_filter, filter_bias):
    seq_count = lax.axis_size("seq")
    seq_place = lax.axis_index("seq")
    section_count = lax.axis_size("section")
    section_place = lax.axis_index("section")
    micro = projected.shape[1]
    height = projected.shape[2]
    width = w_out.shape[2]
    length = height * seq_count
    tables = spectrum_tables(length, height)
    chans = width // seq_count
    bias_part = lax.dynamic_slice_in_dim(filter_bias[0], seq_place * chans, chans, 0)
    weight_in = w_in[0]
    weight_out = w_out[0]
    taps = short_filter[0]
    contract = (((1,), (1,)), ((), ()))

    held = {}

    def causal(blocks):
        return channel_conv(blocks, held["spectrum"], bias_part, False, tables)

    def adjoint(blocks):
        return channel_conv(blocks, held["spectrum"], bias_part, True, tables)

    def to_blocks(series):
        return series.reshape(seq_count, height, chans).transpose(0, 2, 1)

    forward = []
    for slot in range(micro):
        proj = projected[0, slot]
        rim = shifted(proj[height - 2 :], "seq", 1)
        padded = jnp.concatenate([rim, proj], axis=0).astype(jnp.float32)
        mixed = taps[0] * padded[2:] + taps[1] * padded[1:-1] + taps[2] * padded[:-2]
        query = mixed[:, :width]
        keys = mixed[:, width : 2 * width]
        values = mixed[:, 2 * width :]
        product = (keys * values).astype(jnp.bfloat16)
        if slot == 0:
            both = jnp.stack([long_filter[0].astype(jnp.bfloat16), product])
            both = lax.all_to_all(both, "seq", split_axis=2, concat_axis=1, tiled=True)
            held["spectrum"] = forward_blocks(to_blocks(both[0].astype(jnp.float32)), tables)
            product_local = both[1]
        else:
            product_local = lax.all_to_all(product, "seq", split_axis=1, concat_axis=0, tiled=True)
        conv_local = causal(to_blocks(product_local)).transpose(0, 2, 1).reshape(length, chans)
        conv = lax.all_to_all(conv_local, "seq", split_axis=0, concat_axis=1, tiled=True)
        forward.append((query, keys, values, conv.astype(jnp.float32)))

    def stage(grad_out, top, slot):
        query, keys, values, conv_wide = forward[slot]
        d_out, sent = project_and_exchange(grad_out, weight_out, query)
        d_prod_blocks = adjoint(sent)
        return exchange_and_finish(
            d_prod_blocks, d_out, conv_wide, values, keys, grad_out, taps, weight_in, top
        )

    incoming = cotangent[0]
    every = []
    if micro == 1:
        query, keys, values, conv_wide = forward[0]
        top = cotangent[0]
        d_out, sent = project_and_exchange(incoming, weight_out, query)
        for step in range(section_count):
            d_prod_blocks = adjoint(sent)
            common = (d_prod_blocks, d_out, conv_wide, values, keys, incoming, taps, weight_in, top)
            if step == section_count - 1:
                d_input, incoming = exchange_and_finish(*common)
            else:
                d_input, incoming, d_out, sent = exchange_and_finish(
                    *common, then=(weight_out, query)
                )
            every.append(d_input)
    for step in range(micro + section_count - 1 if micro > 1 else 0):
        index = step - (section_count - 1 - section_place)
        later = jnp.clip(index + 1, 0, micro - 1)
        top = lax.dynamic_index_in_dim(cotangent, later, 0, keepdims=False)
        if micro == 1:
            d_input, incoming = stage(incoming, top, 0)
        else:
            slot = jnp.clip(index, 0, micro - 1)
            d_input, incoming = lax.switch(
                slot, [functools.partial(stage, slot=m) for m in range(micro)], incoming, top
            )
        every.append(d_input)
    first = section_count - 1 - section_place
    grads = []
    for m in range(micro):
        picked = every[m]
        for step in range(m + 1, len(every)):
            picked = jnp.where(first + m == step, every[step], picked)
        grads.append(picked)
    return jnp.stack(grads)[None]


def solution(mesh):
    return jax.shard_map(
        shards,
        mesh=mesh,
        in_specs=(
            P(None, "seq", None),
            P("section", None, "seq", None),
            P("section", None, None),
            P("section", None, None),
            P("section", None, None),
            P("section", "seq", None),
            P("section", None),
        ),
        out_specs=P("section", None, "seq", None),
        check_vma=False,
    )
```

```python
import functools
import math

import jax
import jax.numpy as jnp
from jax import lax
from jax.experimental import pallas as pl
from jax.experimental.pallas import tpu as pltpu
from jax.sharding import PartitionSpec as P

accuracy = lax.Precision.HIGH


def shifted(value, axis, by):
    count = lax.axis_size(axis)
    pairs = [(i, i + by) for i in range(count) if 0 <= i + by < count]
    return lax.ppermute(value, axis, pairs)


def phase_table(height, breadth, period):
    row_ids = lax.broadcasted_iota(jnp.int32, (height, breadth), 0)
    col_ids = lax.broadcasted_iota(jnp.int32, (height, breadth), 1)
    angle = (row_ids * col_ids % period).astype(jnp.float32) * (2.0 * math.pi / period)
    return (jnp.cos(angle), jnp.sin(angle))


def spectrum_tables(length, inner):
    outer = 2 * length // inner
    cos_outer, sin_outer = phase_table(outer, length // inner, outer)
    cos_twist, sin_twist = phase_table(inner, outer, 2 * length)
    cos_inner, sin_inner = phase_table(inner, inner, inner)
    mixer = jnp.concatenate(
        [
            jnp.concatenate([cos_inner, sin_inner], axis=1),
            jnp.concatenate([-sin_inner, cos_inner], axis=1),
        ],
        axis=0,
    )
    return {
        "outer": jnp.concatenate([cos_outer, -sin_outer], axis=0),
        "twist": (cos_twist, sin_twist),
        "forward": mixer,
        "inverse": mixer,
    }


def forward_blocks(blocks, tables):
    count, chans, inner = blocks.shape
    outer = 2 * count
    one = jnp.einsum("kn,ncb->cbk", tables["outer"], blocks, precision=accuracy)
    real_one = one[:, :, :outer]
    imag_one = one[:, :, outer:]
    cos_twist, sin_twist = tables["twist"]
    real_two = real_one * cos_twist + imag_one * sin_twist
    imag_two = imag_one * cos_twist - real_one * sin_twist
    both = jnp.einsum(
        "jb,cbk->cjk",
        tables["forward"],
        jnp.concatenate([real_two, imag_two], axis=1),
        precision=accuracy,
    )
    return (both[:, :inner], both[:, inner:])


def inverse_blocks(real, imag, tables):
    chans, inner, outer = real.shape
    length = outer * inner // 2
    both = jnp.einsum(
        "jb,cjk->cbk", tables["inverse"], jnp.concatenate([real, imag], axis=1), precision=accuracy
    )
    real_one = both[:, :inner]
    imag_one = both[:, inner:]
    cos_twist, sin_twist = tables["twist"]
    real_two = real_one * cos_twist - imag_one * sin_twist
    imag_two = imag_one * cos_twist + real_one * sin_twist
    series = jnp.einsum(
        "kn,cbk->ncb",
        tables["outer"],
        jnp.concatenate([real_two, imag_two], axis=2),
        precision=accuracy,
    )
    return series / (2.0 * length)


def channel_conv(blocks, spectrum, bias_part, adjoint, tables):
    values = blocks.astype(jnp.float32)
    real, imag = forward_blocks(values, tables)
    filter_real, filter_imag = spectrum
    if adjoint:
        prod_real = real * filter_real + imag * filter_imag
        prod_imag = imag * filter_real - real * filter_imag
    else:
        prod_real = real * filter_real - imag * filter_imag
        prod_imag = real * filter_imag + imag * filter_real
    direct = bias_part[None, :, None] * values
    return (inverse_blocks(prod_real, prod_imag, tables) + direct).astype(jnp.bfloat16)


def begin_kernel(grad_ref, weight_ref, query_ref, d_out_ref, o_ref, outgoing, landed, send_sems, recv_sems):
    count = lax.axis_size("seq")
    me = lax.axis_index("seq")
    section = lax.axis_index("section")
    mesh_ids = pl.DeviceIdType.MESH
    barrier = pltpu.get_barrier_semaphore()

    def greet(k, _):
        peer = lax.rem(me + k, count)
        pl.semaphore_signal(barrier, inc=1, device_id=(peer, section), device_id_type=mesh_ids)
        return 0

    lax.fori_loop(1, count, greet, 0)
    prepare(grad_ref[...], weight_ref, query_ref, d_out_ref, outgoing)
    pl.semaphore_wait(barrier, count - 1)
    scatter(o_ref, outgoing, landed, send_sems, recv_sems)


def prepare(grad, weight_ref, query_ref, d_out_ref, outgoing):
    d_out = lax.dot_general(
        grad, weight_ref[...], (((1,), (1,)), ((), ())), preferred_element_type=jnp.float32
    )
    d_out_ref[...] = d_out
    d_conv = (d_out * query_ref[...]).astype(jnp.bfloat16).astype(jnp.float32)
    outgoing[...] = d_conv.T.reshape(outgoing.shape).astype(outgoing.dtype)


def scatter(o_ref, outgoing, landed, send_sems, recv_sems):
    count = lax.axis_size("seq")
    me = lax.axis_index("seq")
    section = lax.axis_index("section")
    mesh_ids = pl.DeviceIdType.MESH

    def describe(k):
        peer = lax.rem(me + k, count)
        return pltpu.make_async_remote_copy(
            src_ref=outgoing.at[peer],
            dst_ref=landed.at[me],
            send_sem=send_sems.at[k],
            recv_sem=recv_sems.at[k],
            device_id=(peer, section),
            device_id_type=mesh_ids,
        )

    def send(k, _):
        describe(k).start()
        return 0

    def finish(k, _):
        describe(k).wait()
        return 0

    lax.fori_loop(1, count, send, 0)
    landed[pl.ds(me, 1)] = outgoing[pl.ds(me, 1)]
    lax.fori_loop(1, count, finish, 0)
    o_ref[...] = landed[...]


def project_and_exchange(grad_out, weight_out, query):
    count = lax.axis_size("seq")
    rows, width = query.shape
    vmem = pl.BlockSpec(memory_space=pltpu.VMEM)
    block = (count, width // count, rows)
    return pl.pallas_call(
        begin_kernel,
        out_shape=(
            jax.ShapeDtypeStruct((rows, width), jnp.float32),
            jax.ShapeDtypeStruct(block, jnp.bfloat16),
        ),
        in_specs=[vmem] * 3,
        out_specs=(vmem, vmem),
        scratch_shapes=[
            pltpu.VMEM(block, jnp.bfloat16),
            pltpu.VMEM(block, jnp.bfloat16),
            pltpu.SemaphoreType.DMA((count,)),
            pltpu.SemaphoreType.DMA((count,)),
        ],
        compiler_params=pltpu.CompilerParams(collective_id=0, has_side_effects=True),
    )(grad_out, weight_out, query)


def finish_kernel(then_begin, hand_on, *refs):
    if then_begin:
        (sent_ref, d_out_ref, conv_ref, values_ref, keys_ref, grad_ref, taps_ref, weight_ref, top_ref,
         weight_out_ref, query_ref,
         o_ref, next_ref, next_d_out_ref, next_sent_ref,
         landed, extended, head, from_above, send_sems, recv_sems, rim_sems, hand_sems, acks,
         outgoing, landed_next, next_send_sems, next_recv_sems) = refs
    else:
        (sent_ref, d_out_ref, conv_ref, values_ref, keys_ref, grad_ref, taps_ref, weight_ref, top_ref,
         o_ref, next_ref,
         landed, extended, head, from_above, send_sems, recv_sems, rim_sems, hand_sems, acks) = refs
    count = lax.axis_size("seq")
    rows, width = d_out_ref.shape
    me = lax.axis_index("seq")
    section = lax.axis_index("section")
    mesh_ids = pl.DeviceIdType.MESH
    barrier = pltpu.get_barrier_semaphore()

    def greet(k, _):
        peer = lax.rem(me + k, count)
        pl.semaphore_signal(barrier, inc=1, device_id=(peer, section), device_id_type=mesh_ids)
        return 0

    lax.fori_loop(1, count, greet, 0)
    sections = lax.axis_size("section")
    has_up = (section < sections - 1) & hand_on
    has_down = (section > 0) & hand_on
    up = (me, jnp.minimum(section + 1, sections - 1))
    down = (me, jnp.maximum(section - 1, 0))
    neighbours = has_up.astype(jnp.int32) + has_down.astype(jnp.int32)

    @pl.when(has_up)
    def _():
        pl.semaphore_signal(barrier, inc=1, device_id=up, device_id_type=mesh_ids)

    @pl.when(has_down)
    def _():
        pl.semaphore_signal(barrier, inc=1, device_id=down, device_id_type=mesh_ids)

    pl.semaphore_wait(barrier, count - 1 + neighbours)

    @pl.when(has_up)
    def _():
        pl.semaphore_signal(acks, inc=1, device_id=up, device_id_type=mesh_ids)

    @pl.when(has_down)
    def _():
        pl.semaphore_signal(acks, inc=1, device_id=down, device_id_type=mesh_ids)

    def describe(k):
        peer = lax.rem(me + k, count)
        return pltpu.make_async_remote_copy(
            src_ref=sent_ref.at[peer],
            dst_ref=landed.at[me],
            send_sem=send_sems.at[k],
            recv_sem=recv_sems.at[k],
            device_id=(peer, section),
            device_id_type=mesh_ids,
        )

    def send(k, _):
        describe(k).start()
        return 0

    def finish(k, _):
        describe(k).wait()
        return 0

    lax.fori_loop(1, count, send, 0)
    landed[pl.ds(me, 1)] = sent_ref[pl.ds(me, 1)]
    lax.fori_loop(1, count, finish, 0)

    d_prod = landed[...].astype(jnp.float32).reshape(width, rows).T
    d_mixed = jnp.concatenate(
        [
            (d_out_ref[...] * conv_ref[...]).astype(jnp.bfloat16),
            (d_prod * values_ref[...]).astype(jnp.bfloat16),
            (d_prod * keys_ref[...]).astype(jnp.bfloat16),
        ],
        axis=1,
    ).astype(jnp.float32)
    head[...] = d_mixed[:8]
    rim = pltpu.make_async_remote_copy(
        src_ref=head,
        dst_ref=extended.at[pl.ds(rows, 8)],
        send_sem=rim_sems.at[0],
        recv_sem=rim_sems.at[1],
        device_id=(jnp.maximum(me - 1, 0), section),
        device_id_type=mesh_ids,
    )

    @pl.when(me > 0)
    def _():
        rim.start()

    extended[pl.ds(0, rows)] = d_mixed

    @pl.when(me == count - 1)
    def _():
        extended[pl.ds(rows, 8)] = jnp.zeros((8, extended.shape[1]), jnp.float32)

    taps = taps_ref[...]
    weight = weight_ref[...]
    split = rows - 16

    def project(start, size):
        d_proj = (
            taps[0:1] * extended[pl.ds(start, size)]
            + taps[1:2] * extended[pl.ds(start + 1, size)]
            + taps[2:3] * extended[pl.ds(start + 2, size)]
        ).astype(jnp.bfloat16)
        total = grad_ref[pl.ds(start, size)].astype(jnp.float32) + lax.dot_general(
            d_proj, weight, (((1,), (1,)), ((), ())), preferred_element_type=jnp.float32
        )
        o_ref[pl.ds(start, size)] = total.astype(o_ref.dtype)

    def hand(start, size, slot):
        return pltpu.make_async_remote_copy(
            src_ref=o_ref.at[pl.ds(start, size)],
            dst_ref=from_above.at[pl.ds(start, size)],
            send_sem=hand_sems.at[2 * slot],
            recv_sem=hand_sems.at[2 * slot + 1],
            device_id=down,
            device_id_type=mesh_ids,
        )

    first, last = hand(0, split, 0), hand(split, rows - split, 1)
    project(0, split)

    @pl.when(has_down)
    def _():
        first.start()

    @pl.when(me < count - 1)
    def _():
        rim.wait_recv()

    project(split, rows - split)

    @pl.when(has_down)
    def _():
        last.start()

    @pl.when(me > 0)
    def _():
        rim.wait_send()

    @pl.when(has_up)
    def _():
        first.wait_recv()
        last.wait_recv()
        next_ref[...] = from_above[...]

    @pl.when(jnp.logical_not(has_up))
    def _():
        next_ref[...] = top_ref[...]

    if then_begin:
        prepare(next_ref[...], weight_out_ref, query_ref, next_d_out_ref, outgoing)
        scatter(next_sent_ref, outgoing, landed_next, next_send_sems, next_recv_sems)

    @pl.when(has_down)
    def _():
        first.wait_send()
        last.wait_send()

    if hand_on:
        pl.semaphore_wait(acks, neighbours)


def exchange_and_finish(
    sent, d_out, conv_wide, values, keys, grad_out, taps, weight_in, top, then=None, hand_on=True
):
    count = lax.axis_size("seq")
    rows, width = d_out.shape
    vmem = pl.BlockSpec(memory_space=pltpu.VMEM)
    grads = jax.ShapeDtypeStruct(grad_out.shape, grad_out.dtype)
    scratch = [
        pltpu.VMEM(sent.shape, sent.dtype),
        pltpu.VMEM((rows + 8, taps.shape[1]), jnp.float32),
        pltpu.VMEM((8, taps.shape[1]), jnp.float32),
        pltpu.VMEM(grad_out.shape, grad_out.dtype),
        pltpu.SemaphoreType.DMA((count,)),
        pltpu.SemaphoreType.DMA((count,)),
        pltpu.SemaphoreType.DMA((2,)),
        pltpu.SemaphoreType.DMA((4,)),
        pltpu.SemaphoreType.REGULAR,
    ]
    operands = [sent, d_out, conv_wide, values, keys, grad_out, taps, weight_in, top]
    outs = [grads, grads]
    if then is not None:
        operands += list(then)
        outs += [
            jax.ShapeDtypeStruct((rows, width), jnp.float32),
            jax.ShapeDtypeStruct(sent.shape, sent.dtype),
        ]
        scratch += [
            pltpu.VMEM(sent.shape, sent.dtype),
            pltpu.VMEM(sent.shape, sent.dtype),
            pltpu.SemaphoreType.DMA((count,)),
            pltpu.SemaphoreType.DMA((count,)),
        ]
    return pl.pallas_call(
        functools.partial(finish_kernel, then is not None, hand_on),
        out_shape=tuple(outs),
        in_specs=[vmem] * len(operands),
        out_specs=tuple([vmem] * len(outs)),
        scratch_shapes=scratch,
        compiler_params=pltpu.CompilerParams(
            collective_id=(1 if then is None else 2) + (0 if hand_on else 2), has_side_effects=True
        ),
    )(*operands)


def when(active, action, *operands):

    def skipped(*inputs):
        return jax.tree.map(jnp.zeros_like, action(*inputs))

    return lax.cond(active, action, skipped, *operands)


def shards(cotangent, projected, w_in, w_out, short_filter, long_filter, filter_bias):
    seq_count = lax.axis_size("seq")
    seq_place = lax.axis_index("seq")
    section_count = lax.axis_size("section")
    section_place = lax.axis_index("section")
    micro = projected.shape[1]
    height = projected.shape[2]
    width = w_out.shape[2]
    length = height * seq_count
    tables = spectrum_tables(length, height)
    chans = width // seq_count
    bias_part = lax.dynamic_slice_in_dim(filter_bias[0], seq_place * chans, chans, 0)
    weight_in = w_in[0]
    weight_out = w_out[0]
    taps = short_filter[0]
    contract = (((1,), (1,)), ((), ()))

    held = {}

    def causal(blocks):
        return channel_conv(blocks, held["spectrum"], bias_part, False, tables)

    def adjoint(blocks):
        return channel_conv(blocks, held["spectrum"], bias_part, True, tables)

    def to_blocks(series):
        return series.reshape(seq_count, height, chans).transpose(0, 2, 1)

    forward = []
    for slot in range(micro):
        proj = projected[0, slot]
        rim = shifted(proj[height - 2 :], "seq", 1)
        padded = jnp.concatenate([rim, proj], axis=0).astype(jnp.float32)
        mixed = taps[0] * padded[2:] + taps[1] * padded[1:-1] + taps[2] * padded[:-2]
        query = mixed[:, :width]
        keys = mixed[:, width : 2 * width]
        values = mixed[:, 2 * width :]
        product = (keys * values).astype(jnp.bfloat16)
        if slot == 0:
            both = jnp.stack([long_filter[0].astype(jnp.bfloat16), product])
            both = lax.all_to_all(both, "seq", split_axis=2, concat_axis=1, tiled=True)
            held["spectrum"] = forward_blocks(to_blocks(both[0].astype(jnp.float32)), tables)
            product_local = both[1]
        else:
            product_local = lax.all_to_all(product, "seq", split_axis=1, concat_axis=0, tiled=True)
        conv_local = causal(to_blocks(product_local)).transpose(0, 2, 1).reshape(length, chans)
        conv = lax.all_to_all(conv_local, "seq", split_axis=0, concat_axis=1, tiled=True)
        forward.append((query, keys, values, conv.astype(jnp.float32)))

    def stage(grad_out, top, slot):
        query, keys, values, conv_wide = forward[slot]
        d_out, sent = project_and_exchange(grad_out, weight_out, query)
        d_prod_blocks = adjoint(sent)
        return exchange_and_finish(
            d_prod_blocks, d_out, conv_wide, values, keys, grad_out, taps, weight_in, top
        )

    incoming = cotangent[0]
    every = []
    if micro == 1:
        query, keys, values, conv_wide = forward[0]
        top = cotangent[0]
        d_out, sent = project_and_exchange(incoming, weight_out, query)
        for step in range(section_count):
            d_prod_blocks = adjoint(sent)
            common = (d_prod_blocks, d_out, conv_wide, values, keys, incoming, taps, weight_in, top)
            if step == section_count - 1:
                d_input, incoming = exchange_and_finish(*common, hand_on=False)
            else:
                d_input, incoming, d_out, sent = exchange_and_finish(
                    *common, then=(weight_out, query)
                )
            every.append(d_input)
    for step in range(micro + section_count - 1 if micro > 1 else 0):
        index = step - (section_count - 1 - section_place)
        later = jnp.clip(index + 1, 0, micro - 1)
        top = lax.dynamic_index_in_dim(cotangent, later, 0, keepdims=False)
        if micro == 1:
            d_input, incoming = stage(incoming, top, 0)
        else:
            slot = jnp.clip(index, 0, micro - 1)
            d_input, incoming = lax.switch(
                slot, [functools.partial(stage, slot=m) for m in range(micro)], incoming, top
            )
        every.append(d_input)
    first = section_count - 1 - section_place
    grads = []
    for m in range(micro):
        picked = every[m]
        for step in range(m + 1, len(every)):
            picked = jnp.where(first + m == step, every[step], picked)
        grads.append(picked)
    return jnp.stack(grads)[None]


def solution(mesh):
    return jax.shard_map(
        shards,
        mesh=mesh,
        in_specs=(
            P(None, "seq", None),
            P("section", None, "seq", None),
            P("section", None, None),
            P("section", None, None),
            P("section", None, None),
            P("section", "seq", None),
            P("section", None),
        ),
        out_specs=P("section", None, "seq", None),
        check_vma=False,
    )
```

```python
import functools
import math

import jax
import jax.numpy as jnp
from jax import lax
from jax.experimental import pallas as pl
from jax.experimental.pallas import tpu as pltpu
from jax.sharding import PartitionSpec as P

accuracy = lax.Precision.HIGH


def shifted(value, axis, by):
    count = lax.axis_size(axis)
    pairs = [(i, i + by) for i in range(count) if 0 <= i + by < count]
    return lax.ppermute(value, axis, pairs)


def phase_table(height, breadth, period):
    row_ids = lax.broadcasted_iota(jnp.int32, (height, breadth), 0)
    col_ids = lax.broadcasted_iota(jnp.int32, (height, breadth), 1)
    angle = (row_ids * col_ids % period).astype(jnp.float32) * (2.0 * math.pi / period)
    return (jnp.cos(angle), jnp.sin(angle))


def spectrum_tables(length, inner):
    outer = 2 * length // inner
    cos_outer, sin_outer = phase_table(outer, length // inner, outer)
    cos_twist, sin_twist = phase_table(inner, outer, 2 * length)
    cos_inner, sin_inner = phase_table(inner, inner, inner)
    mixer = jnp.concatenate(
        [
            jnp.concatenate([cos_inner, sin_inner], axis=1),
            jnp.concatenate([-sin_inner, cos_inner], axis=1),
        ],
        axis=0,
    )
    return {
        "outer": jnp.concatenate([cos_outer, -sin_outer], axis=0),
        "twist": (cos_twist, sin_twist),
        "forward": mixer,
        "inverse": mixer,
    }


def forward_blocks(blocks, tables):
    count, chans, inner = blocks.shape
    outer = 2 * count
    one = jnp.einsum("kn,ncb->cbk", tables["outer"], blocks, precision=accuracy)
    real_one = one[:, :, :outer]
    imag_one = one[:, :, outer:]
    cos_twist, sin_twist = tables["twist"]
    real_two = real_one * cos_twist + imag_one * sin_twist
    imag_two = imag_one * cos_twist - real_one * sin_twist
    both = jnp.einsum(
        "jb,cbk->cjk",
        tables["forward"],
        jnp.concatenate([real_two, imag_two], axis=1),
        precision=accuracy,
    )
    return (both[:, :inner], both[:, inner:])


def inverse_blocks(real, imag, tables):
    chans, inner, outer = real.shape
    length = outer * inner // 2
    both = jnp.einsum(
        "jb,cjk->cbk", tables["inverse"], jnp.concatenate([real, imag], axis=1), precision=accuracy
    )
    real_one = both[:, :inner]
    imag_one = both[:, inner:]
    cos_twist, sin_twist = tables["twist"]
    real_two = real_one * cos_twist - imag_one * sin_twist
    imag_two = imag_one * cos_twist + real_one * sin_twist
    series = jnp.einsum(
        "kn,cbk->ncb",
        tables["outer"],
        jnp.concatenate([real_two, imag_two], axis=2),
        precision=accuracy,
    )
    return series / (2.0 * length)


def channel_conv(blocks, spectrum, bias_part, adjoint, tables):
    values = blocks.astype(jnp.float32)
    real, imag = forward_blocks(values, tables)
    filter_real, filter_imag = spectrum
    if adjoint:
        prod_real = real * filter_real + imag * filter_imag
        prod_imag = imag * filter_real - real * filter_imag
    else:
        prod_real = real * filter_real - imag * filter_imag
        prod_imag = real * filter_imag + imag * filter_real
    direct = bias_part[None, :, None] * values
    return (inverse_blocks(prod_real, prod_imag, tables) + direct).astype(jnp.bfloat16)


def begin_kernel(grad_ref, weight_ref, query_ref, d_out_ref, o_ref, outgoing, landed, send_sems, recv_sems):
    count = lax.axis_size("seq")
    me = lax.axis_index("seq")
    section = lax.axis_index("section")
    mesh_ids = pl.DeviceIdType.MESH
    barrier = pltpu.get_barrier_semaphore()

    def greet(k, _):
        peer = lax.rem(me + k, count)
        pl.semaphore_signal(barrier, inc=1, device_id=(peer, section), device_id_type=mesh_ids)
        return 0

    lax.fori_loop(1, count, greet, 0)
    prepare(grad_ref[...], weight_ref, query_ref, d_out_ref, outgoing)
    pl.semaphore_wait(barrier, count - 1)
    scatter(o_ref, outgoing, landed, send_sems, recv_sems)


def prepare(grad, weight_ref, query_ref, d_out_ref, outgoing):
    d_out = lax.dot_general(
        grad, weight_ref[...], (((1,), (1,)), ((), ())), preferred_element_type=jnp.float32
    )
    d_out_ref[...] = d_out
    d_conv = (d_out * query_ref[...]).astype(jnp.bfloat16).astype(jnp.float32)
    outgoing[...] = d_conv.T.reshape(outgoing.shape).astype(outgoing.dtype)


def scatter(o_ref, outgoing, landed, send_sems, recv_sems):
    count = lax.axis_size("seq")
    me = lax.axis_index("seq")
    section = lax.axis_index("section")
    mesh_ids = pl.DeviceIdType.MESH

    def describe(k):
        peer = lax.rem(me + k, count)
        return pltpu.make_async_remote_copy(
            src_ref=outgoing.at[peer],
            dst_ref=landed.at[me],
            send_sem=send_sems.at[k],
            recv_sem=recv_sems.at[k],
            device_id=(peer, section),
            device_id_type=mesh_ids,
        )

    def send(k, _):
        describe(k).start()
        return 0

    def finish(k, _):
        describe(k).wait()
        return 0

    lax.fori_loop(1, count, send, 0)
    landed[pl.ds(me, 1)] = outgoing[pl.ds(me, 1)]
    lax.fori_loop(1, count, finish, 0)
    o_ref[...] = landed[...]


def project_and_exchange(grad_out, weight_out, query):
    count = lax.axis_size("seq")
    rows, width = query.shape
    vmem = pl.BlockSpec(memory_space=pltpu.VMEM)
    block = (count, width // count, rows)
    return pl.pallas_call(
        begin_kernel,
        out_shape=(
            jax.ShapeDtypeStruct((rows, width), jnp.float32),
            jax.ShapeDtypeStruct(block, jnp.bfloat16),
        ),
        in_specs=[vmem] * 3,
        out_specs=(vmem, vmem),
        scratch_shapes=[
            pltpu.VMEM(block, jnp.bfloat16),
            pltpu.VMEM(block, jnp.bfloat16),
            pltpu.SemaphoreType.DMA((count,)),
            pltpu.SemaphoreType.DMA((count,)),
        ],
        compiler_params=pltpu.CompilerParams(collective_id=0, has_side_effects=True),
    )(grad_out, weight_out, query)


def finish_kernel(then_begin, hand_on, conv_in, *refs):
    if conv_in:
        refs = list(refs)
        conv_recv_sems, conv_send_sems = refs.pop(), refs.pop()
        conv_landed = refs.pop()
        conv_out_ref = refs.pop(15 if then_begin else 11)
    if then_begin:
        (sent_ref, d_out_ref, conv_ref, values_ref, keys_ref, grad_ref, taps_ref, weight_ref, top_ref,
         weight_out_ref, query_ref,
         o_ref, next_ref, next_d_out_ref, next_sent_ref,
         landed, extended, head, from_above, send_sems, recv_sems, rim_sems, hand_sems, acks,
         outgoing, landed_next, next_send_sems, next_recv_sems) = refs
    else:
        (sent_ref, d_out_ref, conv_ref, values_ref, keys_ref, grad_ref, taps_ref, weight_ref, top_ref,
         o_ref, next_ref,
         landed, extended, head, from_above, send_sems, recv_sems, rim_sems, hand_sems, acks) = refs
    count = lax.axis_size("seq")
    rows, width = d_out_ref.shape
    me = lax.axis_index("seq")
    section = lax.axis_index("section")
    mesh_ids = pl.DeviceIdType.MESH
    barrier = pltpu.get_barrier_semaphore()

    def greet(k, _):
        peer = lax.rem(me + k, count)
        pl.semaphore_signal(barrier, inc=1, device_id=(peer, section), device_id_type=mesh_ids)
        return 0

    lax.fori_loop(1, count, greet, 0)
    sections = lax.axis_size("section")
    has_up = (section < sections - 1) & hand_on
    has_down = (section > 0) & hand_on
    up = (me, jnp.minimum(section + 1, sections - 1))
    down = (me, jnp.maximum(section - 1, 0))
    neighbours = has_up.astype(jnp.int32) + has_down.astype(jnp.int32)

    @pl.when(has_up)
    def _():
        pl.semaphore_signal(barrier, inc=1, device_id=up, device_id_type=mesh_ids)

    @pl.when(has_down)
    def _():
        pl.semaphore_signal(barrier, inc=1, device_id=down, device_id_type=mesh_ids)

    pl.semaphore_wait(barrier, count - 1 + neighbours)

    @pl.when(has_up)
    def _():
        pl.semaphore_signal(acks, inc=1, device_id=up, device_id_type=mesh_ids)

    @pl.when(has_down)
    def _():
        pl.semaphore_signal(acks, inc=1, device_id=down, device_id_type=mesh_ids)

    def describe(k):
        peer = lax.rem(me + k, count)
        return pltpu.make_async_remote_copy(
            src_ref=sent_ref.at[peer],
            dst_ref=landed.at[me],
            send_sem=send_sems.at[k],
            recv_sem=recv_sems.at[k],
            device_id=(peer, section),
            device_id_type=mesh_ids,
        )

    def send(k, _):
        describe(k).start()
        return 0

    def finish(k, _):
        describe(k).wait()
        return 0

    def carry_conv(k):
        peer = lax.rem(me + k, count)
        return pltpu.make_async_remote_copy(
            src_ref=conv_ref.at[peer],
            dst_ref=conv_landed.at[me],
            send_sem=conv_send_sems.at[k],
            recv_sem=conv_recv_sems.at[k],
            device_id=(peer, section),
            device_id_type=mesh_ids,
        )

    def send_conv(k, _):
        carry_conv(k).start()
        return 0

    def finish_conv(k, _):
        carry_conv(k).wait()
        return 0

    if conv_in:
        lax.fori_loop(1, count, send_conv, 0)
    lax.fori_loop(1, count, send, 0)
    landed[pl.ds(me, 1)] = sent_ref[pl.ds(me, 1)]
    if conv_in:
        conv_landed[pl.ds(me, 1)] = conv_ref[pl.ds(me, 1)]
        lax.fori_loop(1, count, finish_conv, 0)
        conv_wide = conv_landed[...].astype(jnp.float32).reshape(width, rows).T
        conv_out_ref[...] = conv_wide
    else:
        conv_wide = conv_ref[...]
    lax.fori_loop(1, count, finish, 0)

    d_prod = landed[...].astype(jnp.float32).reshape(width, rows).T
    d_mixed = jnp.concatenate(
        [
            (d_out_ref[...] * conv_wide).astype(jnp.bfloat16),
            (d_prod * values_ref[...]).astype(jnp.bfloat16),
            (d_prod * keys_ref[...]).astype(jnp.bfloat16),
        ],
        axis=1,
    ).astype(jnp.float32)
    head[...] = d_mixed[:8]
    rim = pltpu.make_async_remote_copy(
        src_ref=head,
        dst_ref=extended.at[pl.ds(rows, 8)],
        send_sem=rim_sems.at[0],
        recv_sem=rim_sems.at[1],
        device_id=(jnp.maximum(me - 1, 0), section),
        device_id_type=mesh_ids,
    )

    @pl.when(me > 0)
    def _():
        rim.start()

    extended[pl.ds(0, rows)] = d_mixed

    @pl.when(me == count - 1)
    def _():
        extended[pl.ds(rows, 8)] = jnp.zeros((8, extended.shape[1]), jnp.float32)

    taps = taps_ref[...]
    weight = weight_ref[...]
    split = rows - 16

    def project(start, size):
        d_proj = (
            taps[0:1] * extended[pl.ds(start, size)]
            + taps[1:2] * extended[pl.ds(start + 1, size)]
            + taps[2:3] * extended[pl.ds(start + 2, size)]
        ).astype(jnp.bfloat16)
        total = grad_ref[pl.ds(start, size)].astype(jnp.float32) + lax.dot_general(
            d_proj, weight, (((1,), (1,)), ((), ())), preferred_element_type=jnp.float32
        )
        o_ref[pl.ds(start, size)] = total.astype(o_ref.dtype)

    def hand(start, size, slot):
        return pltpu.make_async_remote_copy(
            src_ref=o_ref.at[pl.ds(start, size)],
            dst_ref=from_above.at[pl.ds(start, size)],
            send_sem=hand_sems.at[2 * slot],
            recv_sem=hand_sems.at[2 * slot + 1],
            device_id=down,
            device_id_type=mesh_ids,
        )

    first, last = hand(0, split, 0), hand(split, rows - split, 1)
    project(0, split)

    @pl.when(has_down)
    def _():
        first.start()

    @pl.when(me < count - 1)
    def _():
        rim.wait_recv()

    project(split, rows - split)

    @pl.when(has_down)
    def _():
        last.start()

    @pl.when(me > 0)
    def _():
        rim.wait_send()

    @pl.when(has_up)
    def _():
        first.wait_recv()
        last.wait_recv()
        next_ref[...] = from_above[...]

    @pl.when(jnp.logical_not(has_up))
    def _():
        next_ref[...] = top_ref[...]

    if then_begin:
        prepare(next_ref[...], weight_out_ref, query_ref, next_d_out_ref, outgoing)
        scatter(next_sent_ref, outgoing, landed_next, next_send_sems, next_recv_sems)

    @pl.when(has_down)
    def _():
        first.wait_send()
        last.wait_send()

    if hand_on:
        pl.semaphore_wait(acks, neighbours)


def exchange_and_finish(
    sent, d_out, conv_wide, values, keys, grad_out, taps, weight_in, top, then=None, hand_on=True,
    conv_in=False,
):
    count = lax.axis_size("seq")
    rows, width = d_out.shape
    vmem = pl.BlockSpec(memory_space=pltpu.VMEM)
    grads = jax.ShapeDtypeStruct(grad_out.shape, grad_out.dtype)
    scratch = [
        pltpu.VMEM(sent.shape, sent.dtype),
        pltpu.VMEM((rows + 8, taps.shape[1]), jnp.float32),
        pltpu.VMEM((8, taps.shape[1]), jnp.float32),
        pltpu.VMEM(grad_out.shape, grad_out.dtype),
        pltpu.SemaphoreType.DMA((count,)),
        pltpu.SemaphoreType.DMA((count,)),
        pltpu.SemaphoreType.DMA((2,)),
        pltpu.SemaphoreType.DMA((4,)),
        pltpu.SemaphoreType.REGULAR,
    ]
    operands = [sent, d_out, conv_wide, values, keys, grad_out, taps, weight_in, top]
    outs = [grads, grads]
    if then is not None:
        operands += list(then)
        outs += [
            jax.ShapeDtypeStruct((rows, width), jnp.float32),
            jax.ShapeDtypeStruct(sent.shape, sent.dtype),
        ]
        scratch += [
            pltpu.VMEM(sent.shape, sent.dtype),
            pltpu.VMEM(sent.shape, sent.dtype),
            pltpu.SemaphoreType.DMA((count,)),
            pltpu.SemaphoreType.DMA((count,)),
        ]
    if conv_in:
        outs += [jax.ShapeDtypeStruct((rows, width), jnp.float32)]
        scratch += [
            pltpu.VMEM(sent.shape, sent.dtype),
            pltpu.SemaphoreType.DMA((count,)),
            pltpu.SemaphoreType.DMA((count,)),
        ]
    return pl.pallas_call(
        functools.partial(finish_kernel, then is not None, hand_on, conv_in),
        out_shape=tuple(outs),
        in_specs=[vmem] * len(operands),
        out_specs=tuple([vmem] * len(outs)),
        scratch_shapes=scratch,
        compiler_params=pltpu.CompilerParams(
            collective_id=(1 if then is None else 2) + (0 if hand_on else 2) + (4 if conv_in else 0),
            has_side_effects=True,
        ),
    )(*operands)


def when(active, action, *operands):

    def skipped(*inputs):
        return jax.tree.map(jnp.zeros_like, action(*inputs))

    return lax.cond(active, action, skipped, *operands)


def shards(cotangent, projected, w_in, w_out, short_filter, long_filter, filter_bias):
    seq_count = lax.axis_size("seq")
    seq_place = lax.axis_index("seq")
    section_count = lax.axis_size("section")
    section_place = lax.axis_index("section")
    micro = projected.shape[1]
    height = projected.shape[2]
    width = w_out.shape[2]
    length = height * seq_count
    tables = spectrum_tables(length, height)
    chans = width // seq_count
    bias_part = lax.dynamic_slice_in_dim(filter_bias[0], seq_place * chans, chans, 0)
    weight_in = w_in[0]
    weight_out = w_out[0]
    taps = short_filter[0]
    contract = (((1,), (1,)), ((), ()))

    held = {}

    def causal(blocks):
        return channel_conv(blocks, held["spectrum"], bias_part, False, tables)

    def adjoint(blocks):
        return channel_conv(blocks, held["spectrum"], bias_part, True, tables)

    def to_blocks(series):
        return series.reshape(seq_count, height, chans).transpose(0, 2, 1)

    forward = []
    for slot in range(micro):
        proj = projected[0, slot]
        rim = shifted(proj[height - 2 :], "seq", 1)
        padded = jnp.concatenate([rim, proj], axis=0).astype(jnp.float32)
        mixed = taps[0] * padded[2:] + taps[1] * padded[1:-1] + taps[2] * padded[:-2]
        query = mixed[:, :width]
        keys = mixed[:, width : 2 * width]
        values = mixed[:, 2 * width :]
        product = (keys * values).astype(jnp.bfloat16)
        if slot == 0:
            both = jnp.stack([long_filter[0].astype(jnp.bfloat16), product])
            both = lax.all_to_all(both, "seq", split_axis=2, concat_axis=1, tiled=True)
            held["spectrum"] = forward_blocks(to_blocks(both[0].astype(jnp.float32)), tables)
            product_local = both[1]
        else:
            product_local = lax.all_to_all(product, "seq", split_axis=1, concat_axis=0, tiled=True)
        conv_blocks = causal(to_blocks(product_local))
        conv_local = conv_blocks.transpose(0, 2, 1).reshape(length, chans)
        if micro == 1:
            forward.append((query, keys, values, conv_blocks))
        else:
            conv = lax.all_to_all(conv_local, "seq", split_axis=0, concat_axis=1, tiled=True)
            forward.append((query, keys, values, conv.astype(jnp.float32)))

    def stage(grad_out, top, slot):
        query, keys, values, conv_wide = forward[slot]
        d_out, sent = project_and_exchange(grad_out, weight_out, query)
        d_prod_blocks = adjoint(sent)
        return exchange_and_finish(
            d_prod_blocks, d_out, conv_wide, values, keys, grad_out, taps, weight_in, top
        )

    incoming = cotangent[0]
    every = []
    if micro == 1:
        query, keys, values, conv_blocks = forward[0]
        top = cotangent[0]
        d_out, sent = project_and_exchange(incoming, weight_out, query)
        conv_wide = None
        for step in range(section_count):
            d_prod_blocks = adjoint(sent)
            first = conv_wide is None
            common = (
                d_prod_blocks, d_out, conv_blocks if first else conv_wide, values, keys, incoming,
                taps, weight_in, top,
            )
            if step == section_count - 1:
                results = exchange_and_finish(*common, hand_on=False, conv_in=first)
                d_input, incoming = results[:2]
            else:
                results = exchange_and_finish(*common, then=(weight_out, query), conv_in=first)
                d_input, incoming, d_out, sent = results[:4]
            if first:
                conv_wide = results[-1]
            every.append(d_input)
    for step in range(micro + section_count - 1 if micro > 1 else 0):
        index = step - (section_count - 1 - section_place)
        later = jnp.clip(index + 1, 0, micro - 1)
        top = lax.dynamic_index_in_dim(cotangent, later, 0, keepdims=False)
        if micro == 1:
            d_input, incoming = stage(incoming, top, 0)
        else:
            slot = jnp.clip(index, 0, micro - 1)
            d_input, incoming = lax.switch(
                slot, [functools.partial(stage, slot=m) for m in range(micro)], incoming, top
            )
        every.append(d_input)
    first = section_count - 1 - section_place
    grads = []
    for m in range(micro):
        picked = every[m]
        for step in range(m + 1, len(every)):
            picked = jnp.where(first + m == step, every[step], picked)
        grads.append(picked)
    return jnp.stack(grads)[None]


def solution(mesh):
    return jax.shard_map(
        shards,
        mesh=mesh,
        in_specs=(
            P(None, "seq", None),
            P("section", None, "seq", None),
            P("section", None, None),
            P("section", None, None),
            P("section", None, None),
            P("section", "seq", None),
            P("section", None),
        ),
        out_specs=P("section", None, "seq", None),
        check_vma=False,
    )
```
